32 devices in a mesh: dp: 2 (over x), fsdp: 16 (over z, y, core).
Axes of the slice: x: 2, y: 2, z: 4, core: 2. Of those that a mesh axis runs over, the one named last changes fastest.
Arguments:
- tokens: bfloat16 [2, 32, 1024, 768], P(None, ('dp', 'fsdp')), may hold values from -6 to 6
- skip_values: bfloat16 [2, 32, 1024, 384], P(None, ('dp', 'fsdp')), may hold values from -6 to 6
- w_qkv: bfloat16 [768, 1920], P(('dp', 'fsdp')), may hold values from -0.21875 to 0.21875
- w_out: bfloat16 [768, 768], P(('dp', 'fsdp')), may hold values from -1.75 to 1.75
- w_fc: bfloat16 [768, 3072], P(('dp', 'fsdp')), may hold values from -0.21875 to 0.21875
- w_proj: bfloat16 [3072, 768], P(('dp', 'fsdp')), may hold values from -0.109375 to 0.109375
- norm_gains: bfloat16 [2, 768], P(None, ('dp', 'fsdp')), may hold values from 0.5 to 1.5
- norm_shifts: bfloat16 [2, 768], P(None, ('dp', 'fsdp')), may hold values from -1 to 1
- segment_ids: int32 [2, 32, 1024], P(None, ('dp', 'fsdp')), may hold values from 0 to 7, never falling along the last dimension, each value on 1 to 512 neighbouring positions
- pad_mask: int32 [2, 32, 1024], P(None, ('dp', 'fsdp')), may hold values 0 or 1
- cotangent: bfloat16 [2, 32, 1024, 768], P(None, ('dp', 'fsdp')), may hold values from -6 to 6
Outputs:
- layer_out: bfloat16 [2, 32, 1024, 768], P(None, ('dp', 'fsdp'))
- grad_tokens: float32 [2, 32, 1024, 768], P(None, ('dp', 'fsdp'))
- grad_skip: float32 [2, 32, 1024, 384], P(None, ('dp', 'fsdp'))
- grad_qkv: float32 [768, 1920], P(('dp', 'fsdp'))
- grad_out: float32 [768, 768], P(('dp', 'fsdp'))
- grad_fc: float32 [768, 3072], P(('dp', 'fsdp'))
- grad_proj: float32 [3072, 768], P(('dp', 'fsdp'))
- grad_gains: float32 [2, 768], P(None, ('dp', 'fsdp'))
- grad_shifts: float32 [2, 768], P(None, ('dp', 'fsdp'))
The draws below stay inside these ranges and needn't reach their ends.
Inputs may be any that keep to these rules, and one draw needn't show every extreme that they name: `segment_ids`: segment numbers never fall along a packed row; a document holds 1 to 512 tokens, and some document holds exactly 512.
All inputs are finite; a program needn't handle non-finite values. No bound on the sum of `pad_mask` on one device may be relied on, other than what follows from the above.
Results may differ from the reference program's by a relative error of at most 0.0097.
Values may be sent and summed in bfloat16 or wider, within the bound.
A program may use at most 320 MiB of HBM per device.

```python
import math
import jax
import jax.numpy as jnp
import numpy as np
from jax import lax

D = 768
HEADS = 12
HEAD = 64
FF = 3072
SEQ = 1024
MB = 2
BATCH = 32
QKV = 1920


def touch_ends(entries, stream_key, smallest, top_value):
    shape = entries.shape
    index_at = [jax.random.randint(jax.random.fold_in(stream_key, axis), (), 0, shape[axis]) for axis in range(len(shape))]
    entries = entries.at[tuple(index_at)].set(smallest)
    longest = shape.index(max(shape))
    index_at[longest] = (index_at[longest] + 1) % shape[longest]
    return entries.at[tuple(index_at)].set(top_value)


def levels(key, extent, cuts, least, largest):
    factor_of = 1.0
    for axis_at, blocks in cuts:
        steps = jax.random.uniform(jax.random.fold_in(jax.random.fold_in(key, 6), axis_at), (blocks,), jnp.float32, least / len(cuts), largest / len(cuts))
        factor_of = factor_of * jnp.repeat(jnp.exp(steps), extent[axis_at] // blocks).reshape((-1,) + (1,) * (len(extent) - 1 - axis_at))
    return factor_of


def profile(amount, total, limit, skew):
    loads = [(1 << 20) // math.isqrt(grade ** skew) + 1 for grade in range(2, amount + 1)]
    rest, counts = total - limit - (amount - 1), [1] * (amount - 1)
    while rest > 0:
        candidates = [i for i in range(amount - 1) if counts[i] < limit]
        pool, remaining = sum([loads[i] for i in candidates]), rest
        for i in candidates:
            addition = min(limit - counts[i], max(1, remaining * loads[i] // pool), rest)
            counts[i] = counts[i] + addition
            rest = rest - addition
    return np.array([limit] + counts)


def uneven(key, count, total, limit, lean):
    if count == 2:
        one = jax.random.randint(key, (), max(1, total - limit), min(limit, total - 1) + 1)
        return jnp.stack([one, total - one])
    lengths = jnp.asarray(profile(count, total, limit, lean), jnp.int32)
    couples = (count - 1) // 2
    donor, receiver = lengths[1:1 + 2 * couples:2], lengths[2:2 + 2 * couples:2]
    room = jnp.minimum(donor - 1, limit - receiver)
    moved = jax.random.randint(jax.random.fold_in(key, 1), (couples,), 0, 1 << 20) % (room + 1)
    lengths = lengths.at[1:1 + 2 * couples:2].set(donor - moved).at[2:2 + 2 * couples:2].set(receiver + moved)
    return lengths[jax.random.permutation(jax.random.fold_in(key, 2), count)]


def bell_draw(rng, extent, scale, most, cuts=(), held_as=jnp.bfloat16):
    entries = scale * jax.random.normal(rng, extent, jnp.float32)
    if cuts:
        entries = entries * levels(rng, extent, cuts, -0.22, 0.18)
    return jnp.clip(entries, -most, most).astype(held_as)


def setup_inputs(seed: int = 0) -> dict:
    splits = jax.random.split(jax.random.key(seed), 12)
    return {
        "tokens": bell_draw(splits[0], (MB, BATCH, SEQ, D), 1.0, 6.0, ((1, 32),)),
        "skip_values": bell_draw(splits[1], (MB, BATCH, SEQ, D // 2), 1.0, 6.0, ((1, 32),)),
        "w_qkv": bell_draw(splits[2], (D, QKV), D ** -0.5, 0.21875, ((0, 32),)),
        "w_out": bell_draw(splits[3], (D, D), (D // 64) ** -0.5, 1.75, ((0, 32),)),
        "w_fc": bell_draw(splits[4], (D, FF), D ** -0.5, 0.21875, ((0, 32),)),
        "w_proj": bell_draw(splits[5], (FF, D), FF ** -0.5, 0.109375, ((0, 32),)),
        "norm_gains": jnp.clip(1.0 + 0.1 * jax.random.normal(splits[6], (2, D), jnp.float32), 0.5, 1.5).astype(jnp.bfloat16),
        "norm_shifts": bell_draw(splits[7], (2, D), 0.2, 1.0, ((1, 32),)),
        "segment_ids": jax.vmap(lambda own: jnp.searchsorted(jnp.cumsum(uneven(own, 8, SEQ, SEQ // 2, 2)), jnp.arange(SEQ), side="right"))(jax.random.split(splits[8], MB * BATCH)).reshape((MB, BATCH, SEQ)).astype(jnp.int32),
        "pad_mask": touch_ends((jax.random.randint(splits[9], (MB, BATCH, SEQ), 0, 8) < 7).astype(jnp.int32), jax.random.fold_in(splits[9], 1), 0, 1),
        "cotangent": bell_draw(splits[10], (MB, BATCH, SEQ, D), 1.0, 6.0, ((1, 32),)),
    }


@jax.custom_vjp
def low(v):
    return lax.optimization_barrier(v.astype(jnp.bfloat16)).astype(jnp.float32)

@jax.custom_vjp
def low_back(v):
    return v

def low_keep(v):
    return (low(v), None)

def low_pass(kept, grad):
    return (grad,)

def back_keep(v):
    return (v, None)

def back_low(kept, grad):
    return (low(grad),)
low.defvjp(low_keep, low_pass)
low_back.defvjp(back_keep, back_low)
epsilon = 1e-05
masked_score = -1000000000.0
highest = lax.Precision.HIGHEST

def layer_norm(rows_in, gain_row, shift_row):
    row_mean = lax.optimization_barrier(jnp.mean(rows_in, axis=-1, keepdims=True))
    centred = rows_in - row_mean
    spread = lax.optimization_barrier(jnp.mean(centred * centred, axis=-1, keepdims=True))
    return centred * lax.rsqrt(spread + epsilon) * gain_row + shift_row

def attend_one(parts):
    queries, key_rows, values, seg_rows, pad_rows = parts
    positions = jnp.arange(SEQ, dtype=jnp.int32)
    same_doc = seg_rows[:, None] == seg_rows[None, :]
    causal = positions[:, None] >= positions[None, :]
    visible = (pad_rows[None, :] == 1) | (positions[:, None] == positions[None, :])
    allowed = same_doc & causal & visible
    scores = jnp.einsum('qhd,khd->hqk', queries, key_rows, precision=highest) * HEAD ** (-0.5)
    scores = low_back(jnp.where(allowed[None], scores, masked_score))
    row_max = lax.optimization_barrier(jnp.max(scores, axis=-1, keepdims=True))
    exponent = jnp.exp(scores - row_max)
    attn_probs = low(exponent / lax.optimization_barrier(jnp.sum(exponent, axis=-1, keepdims=True)))
    return jnp.einsum('hqk,khd->qhd', attn_probs, values, precision=highest)

def forward(rows_in, skip_in, w_qkv, w_out, w_fc, w_proj, norm_gains, norm_shifts, seg_rows, pad_rows):
    group_size = rows_in.shape[0]
    head_shape = (group_size, SEQ, HEADS, HEAD)
    normed = low(layer_norm(rows_in, norm_gains[0], norm_shifts[0]))
    mixed_rows = jnp.einsum('gsd,de->gse', normed, w_qkv, precision=highest)
    queries = low_back(low(mixed_rows[..., :D])).reshape(head_shape)
    key_rows = low_back(low(mixed_rows[..., D:2 * D])).reshape(head_shape)
    joined = jnp.concatenate([mixed_rows[..., 2 * D:], skip_in], axis=-1)
    values = low_back(low(joined)).reshape(head_shape)
    attended = lax.map(jax.checkpoint(attend_one), (queries, key_rows, values, seg_rows, pad_rows))
    attended = low_back(low(attended.reshape(group_size, SEQ, D)))
    hidden = rows_in + low_back(jnp.einsum('gsd,de->gse', attended, w_out, precision=highest))
    normed_two = low(layer_norm(hidden, norm_gains[1], norm_shifts[1]))
    fc_inner = low_back(jnp.einsum('gsd,df->gsf', normed_two, w_fc, precision=highest))
    fc_act = low(jax.nn.gelu(fc_inner, approximate=True))
    return hidden + low_back(jnp.einsum('gsf,fd->gsd', fc_act, w_proj, precision=highest))

def reference(tokens, skip_values, w_qkv, w_out, w_fc, w_proj, norm_gains, norm_shifts, segment_ids, pad_mask, cotangent):
    group_size = 4
    sequence_total = MB * BATCH

    def regroup(array):
        return array.reshape((sequence_total // group_size, group_size) + array.shape[2:])
    weights = tuple((w.astype(jnp.float32) for w in (w_qkv, w_out, w_fc, w_proj, norm_gains, norm_shifts)))

    def one_group(grad_sums, inputs):
        rows_in, skip_in, seg_rows, pad_rows, cot_in = inputs

        def apply_layer(rows_arg, skip_arg, *weight_args):
            return forward(rows_arg, skip_arg, *weight_args, seg_rows, pad_rows)
        result, pull_back = jax.vjp(apply_layer, rows_in.astype(jnp.float32), skip_in.astype(jnp.float32), *weights)
        gradients = pull_back(cot_in.astype(jnp.float32))
        grad_sums = tuple((a + b for a, b in zip(grad_sums, gradients[2:])))
        return (grad_sums, (result.astype(jnp.bfloat16), gradients[0], gradients[1]))
    initial = tuple((jnp.zeros(w.shape, jnp.float32) for w in weights))
    grad_sums, stacked = lax.scan(one_group, initial, (regroup(tokens), regroup(skip_values), regroup(segment_ids), regroup(pad_mask), regroup(cotangent)))
    layer_out = stacked[0].reshape(MB, BATCH, SEQ, D)
    grad_tokens = stacked[1].reshape(MB, BATCH, SEQ, D)
    grad_skip = stacked[2].reshape(MB, BATCH, SEQ, D // 2)
    return (layer_out, grad_tokens, grad_skip, grad_sums[0], grad_sums[1], grad_sums[2], grad_sums[3], grad_sums[4], grad_sums[5])
```

```python
import functools
import jax
import jax.numpy as jnp
from jax import lax
from jax.experimental import pallas as pl
from jax.experimental.pallas import tpu as pltpu
from jax.sharding import PartitionSpec as P

F32, BF16 = jnp.float32, jnp.bfloat16

HEAD = 64
BLK = 128
WIN = 5
MASKED = -1e9


def build_bias(seg_row, pad_row, bias_ref, n_blk):
    code = jnp.where(pad_row == 1, seg_row, -1)
    for qb in range(n_blk):
        seg_q = seg_row[:, qb * BLK:(qb + 1) * BLK]
        for kb in range(max(0, qb - WIN + 1), qb + 1):
            code_k = jnp.broadcast_to(code[:, kb * BLK:(kb + 1) * BLK], (BLK, BLK)).T
            vis = code_k == seg_q
            if kb == qb:
                key = lax.broadcasted_iota(jnp.int32, (BLK, BLK), 0)
                row = lax.broadcasted_iota(jnp.int32, (BLK, BLK), 1)
                vis = (vis & (key < row)) | (key == row)
            t = kb - qb + WIN - 1
            bias_ref[qb, t * BLK:(t + 1) * BLK, :] = jnp.where(vis, 0.0, MASKED)


def split_heads(x_t):
    low = lax.broadcasted_iota(jnp.int32, x_t.shape, 0) < HEAD
    zero = jnp.zeros_like(x_t)
    return jnp.concatenate([jnp.where(low, x_t, zero), jnp.where(low, zero, x_t)], axis=1)


def join_heads(x2):
    return jnp.concatenate([x2[:HEAD, :BLK], x2[HEAD:, BLK:]], axis=0)


def visible_blocks(seg_s, row, qb):
    first = seg_s[row, qb * BLK]
    n = jnp.int32(1)
    for back in range(1, WIN):
        kb = jnp.maximum(qb - back, 0)
        seen = (qb >= back) & (seg_s[row, kb * BLK + BLK - 1] == first)
        n = n + seen.astype(jnp.int32)
    return n


def fwd_kernel(n_blk, seg_s, seg_ref, pad_ref, q_ref, k_ref, v_ref, o_ref, lse_ref, bias_ref, qt_ref, vt_ref):
    row, pair = pl.program_id(0), pl.program_id(1)

    @pl.when(pair == 0)
    def _():
        build_bias(seg_ref[...], pad_ref[...], bias_ref, n_blk)

    for qb in range(n_blk):
        rows = pl.ds(qb * BLK, BLK)
        qt_ref[qb] = split_heads(q_ref[rows, :].T)
        vt_ref[:, rows] = v_ref[rows, :].T

    def one(n, qb):
        start = pl.multiple_of((qb - n + 1) * BLK, BLK)
        keys = pl.ds(start, n * BLK)
        s = jnp.dot(k_ref[keys, :], qt_ref[qb], preferred_element_type=F32)
        b = bias_ref[qb, (WIN - n) * BLK:, :]
        s = s + jnp.concatenate([b, b], axis=1)
        m = jnp.max(s, axis=0, keepdims=True)
        p = jnp.exp(s - m)
        total = jnp.sum(p, axis=0, keepdims=True)
        o2 = jnp.dot(vt_ref[:, keys], p.astype(BF16), preferred_element_type=F32)
        o2 = o2 * (1.0 / total)
        o_ref[pl.ds(pl.multiple_of(qb * BLK, BLK), BLK), :] = join_heads(o2).T.astype(BF16)
        lse = m + jnp.log(total)
        lse_ref[qb] = lse

    def step(qb, carry):
        n_vis = visible_blocks(seg_s, row, qb)
        for n in range(1, WIN + 1):
            @pl.when(n_vis == n)
            def _():
                one(n, qb)
        return carry
    lax.fori_loop(0, n_blk, step, 0)


def attend(q, k, v, seg, pad):
    rows, length, width = q.shape
    n_blk, pairs = length // BLK, width // 128
    tok = pl.BlockSpec((None, length, 128), lambda r, h, s: (r, 0, h))
    ids = pl.BlockSpec((None, 1, length), lambda r, h, s: (r, 0, 0))
    return pl.pallas_call(
        functools.partial(fwd_kernel, n_blk),
        grid_spec=pltpu.PrefetchScalarGridSpec(
            num_scalar_prefetch=1, grid=(rows, pairs),
            in_specs=[ids, ids, tok, tok, tok],
            out_specs=[tok, pl.BlockSpec((None, None, n_blk, 1, 2 * BLK), lambda r, h, s: (r, h, 0, 0, 0))],
            scratch_shapes=[pltpu.VMEM((n_blk, WIN * BLK, BLK), F32), pltpu.VMEM((n_blk, BLK, 2 * BLK), BF16), pltpu.VMEM((BLK, length), BF16)]),
        out_shape=[jax.ShapeDtypeStruct((rows, length, width), BF16), jax.ShapeDtypeStruct((rows, pairs, n_blk, 1, 2 * BLK), F32)],
        compiler_params=pltpu.CompilerParams(dimension_semantics=("arbitrary", "arbitrary")),
        name="attend",
    )(seg, seg[:, None, :], pad[:, None, :], q, k, v)


def stack_heads(x):
    low = lax.broadcasted_iota(jnp.int32, x.shape, 1) < HEAD
    zero = jnp.zeros_like(x)
    return jnp.concatenate([jnp.where(low, x, zero), jnp.where(low, zero, x)], axis=0)


def bwd_kernel(n_blk, seg_s, seg_ref, pad_ref, q_ref, k_ref, v_ref, g_ref, lse_ref, dq_ref, dk_ref, dv_ref,
               bias_ref, qt_ref, gt_ref, kt_ref, dk_acc, dv_acc):
    row, pair = pl.program_id(0), pl.program_id(1)

    @pl.when(pair == 0)
    def _():
        build_bias(seg_ref[...], pad_ref[...], bias_ref, n_blk)

    for qb in range(n_blk):
        rows = pl.ds(qb * BLK, BLK)
        qt_ref[qb] = split_heads(q_ref[rows, :].T)
        gt_ref[qb] = split_heads(g_ref[rows, :].T)
        kt_ref[:, rows] = k_ref[rows, :].T
    dk_acc[...] = jnp.zeros_like(dk_acc)
    dv_acc[...] = jnp.zeros_like(dv_acc)

    def one(n, qb):
        start = pl.multiple_of((qb - n + 1) * BLK, BLK)
        keys = pl.ds(start, n * BLK)
        here = pl.ds(pl.multiple_of(qb * BLK, BLK), BLK)
        s = jnp.dot(k_ref[keys, :], qt_ref[qb], preferred_element_type=F32)
        b = bias_ref[qb, (WIN - n) * BLK:, :]
        p = jnp.exp(s + jnp.concatenate([b, b], axis=1) - lse_ref[qb])
        dp = jnp.dot(v_ref[keys, :], gt_ref[qb], preferred_element_type=F32)
        inner = jnp.sum(p * dp, axis=0, keepdims=True)
        ds = (p * (dp - inner)).astype(BF16)
        dv_acc[keys, :] += jnp.dot(p.astype(BF16), stack_heads(g_ref[here, :]), preferred_element_type=F32)
        dk_acc[keys, :] += jnp.dot(ds, stack_heads(q_ref[here, :]), preferred_element_type=F32)
        dq2 = jnp.dot(kt_ref[:, keys], ds, preferred_element_type=F32)
        dq_ref[here, :] = (join_heads(dq2) * 0.125).T.astype(BF16)

    def step(qb, carry):
        n_vis = visible_blocks(seg_s, row, qb)
        for n in range(1, WIN + 1):
            @pl.when(n_vis == n)
            def _():
                one(n, qb)
        return carry
    lax.fori_loop(0, n_blk, step, 0)
    dk_ref[...] = dk_acc[...].astype(BF16)
    dv_ref[...] = dv_acc[...].astype(BF16)


def attend_back(q, k, v, g, lse, seg, pad):
    rows, length, width = q.shape
    n_blk, pairs = length // BLK, width // 128
    tok = pl.BlockSpec((None, length, 128), lambda r, h, s: (r, 0, h))
    ids = pl.BlockSpec((None, 1, length), lambda r, h, s: (r, 0, 0))
    out = jax.ShapeDtypeStruct((rows, length, width), BF16)
    return pl.pallas_call(
        functools.partial(bwd_kernel, n_blk),
        grid_spec=pltpu.PrefetchScalarGridSpec(
            num_scalar_prefetch=1, grid=(rows, pairs),
            in_specs=[ids, ids, tok, tok, tok, tok, pl.BlockSpec((None, None, n_blk, 1, 2 * BLK), lambda r, h, s: (r, h, 0, 0, 0))],
            out_specs=[tok, tok, tok],
            scratch_shapes=[pltpu.VMEM((n_blk, WIN * BLK, BLK), F32), pltpu.VMEM((n_blk, BLK, 2 * BLK), BF16),
                            pltpu.VMEM((n_blk, BLK, 2 * BLK), BF16), pltpu.VMEM((BLK, length), BF16),
                            pltpu.VMEM((length, BLK), F32), pltpu.VMEM((length, BLK), F32)]),
        out_shape=[out, out, out],
        compiler_params=pltpu.CompilerParams(dimension_semantics=("arbitrary", "arbitrary")),
        name="attend_back",
    )(seg, seg[:, None, :], pad[:, None, :], q, k, v, g, lse)


MESH = pl.DeviceIdType.MESH
NZ = 4


class Place:
    def __init__(self):
        dp, fs = lax.axis_index("dp"), lax.axis_index("fsdp")
        self.x, self.z, self.y, self.c = dp, fs // 4, (fs // 2) % 2, fs % 2
        self.slot = self.x * 16 + fs
        self.first = self.id(x=jnp.where(self.c == 0, 1 - self.x, self.x), y=jnp.where(self.c == 0, self.y, 1 - self.y))
        self.second = self.id(x=jnp.where(self.c == 0, self.x, 1 - self.x), y=jnp.where(self.c == 0, 1 - self.y, self.y))
        self.partner = self.id(c=1 - self.c)

    def id(self, x=None, y=None, z=None, c=None):
        x = self.x if x is None else x
        y = self.y if y is None else y
        z = self.z if z is None else z
        c = self.c if c is None else c
        return (x, z * 4 + y * 2 + c)

    def z_at(self, k):
        return (self.z + k) % NZ

    def peers(self):
        return [self.partner, self.first, self.second] + [self.id(z=self.z_at(k)) for k in (1, 2, 3)]

    def slot_of(self, df, ds, z):
        dx = jnp.where(self.c == 0, df, ds)
        dy = jnp.where(self.c == 0, ds, df)
        x = jnp.where(dx == 1, 1 - self.x, self.x)
        y = jnp.where(dy == 1, 1 - self.y, self.y)
        return x * 16 + z * 4 + y * 2 + self.c


def enter(place):
    bar = pltpu.get_barrier_semaphore()
    for peer in place.peers():
        pl.semaphore_signal(bar, inc=1, device_id=peer, device_id_type=MESH)
    pl.semaphore_wait(bar, 6)


N_SENDS = 31


class Gather:
    def __init__(self, place, shard, out, send, recv, own):
        self.p, self.shard, self.out, self.send, self.recv, self.own = place, shard, out, send, recv, own

    def push(self, src, slot, to):
        pltpu.make_async_remote_copy(src_ref=src, dst_ref=self.out.at[slot], send_sem=self.send, recv_sem=self.recv.at[slot],
                                     device_id=to, device_id_type=MESH).start()

    def arrived(self, slot):
        pltpu.make_async_copy(self.out.at[slot], self.out.at[slot], self.recv.at[slot]).wait()

    def s1(self):
        p = self.p
        pltpu.make_async_copy(self.shard, self.out.at[p.slot], self.own).start()
        for k in (1, 3, 2):
            self.push(self.shard, p.slot, p.id(z=p.z_at(k)))
        self.push(self.shard, p.slot, p.first)
        self.push(self.shard, p.slot, p.partner)
        self.push(self.shard, p.slot, p.second)

    def s2(self):
        p = self.p
        for k in (1, 3, 2):
            slot = p.slot_of(0, 0, p.z_at(k))
            self.arrived(slot)
            for to in (p.first, p.second, p.partner):
                self.push(self.out.at[slot], slot, to)

    def s3(self):
        p = self.p
        for k in (0, 1, 3, 2):
            slot = p.slot_of(1, 0, p.z_at(k))
            self.arrived(slot)
            for to in (p.second, p.partner):
                self.push(self.out.at[slot], slot, to)

    def s4(self):
        p = self.p
        for df in (0, 1):
            for k in (0, 1, 3, 2):
                slot = p.slot_of(df, 1, p.z_at(k))
                self.arrived(slot)
                self.push(self.out.at[slot], slot, p.partner)

    def s5(self):
        for k in range(16):
            self.arrived(2 * k + 1 - self.p.c)
        pltpu.make_async_copy(self.shard, self.out.at[self.p.slot], self.own).wait()

    def drain(self):
        done = self.out.at[pl.ds(0, N_SENDS)]
        pltpu.make_async_copy(done, done, self.send).wait()


def gather_kernel(n, *refs):
    shards, outs, sems = refs[:n], refs[n:2 * n], refs[2 * n:]
    place = Place()
    enter(place)
    jobs = [Gather(place, shards[i], outs[i], sems[0].at[i], sems[1].at[i], sems[2].at[i]) for i in range(n)]
    for job in jobs:
        job.s1()
    for t in range(n + 3):
        for lag, name in enumerate(("s2", "s3", "s4", "s5")):
            if 0 <= t - lag < n:
                getattr(jobs[t - lag], name)()
    for job in jobs:
        job.drain()


def gather_all(shards, collective_id=0):
    n = len(shards)
    return pl.pallas_call(
        functools.partial(gather_kernel, n),
        out_shape=[jax.ShapeDtypeStruct((32,) + s.shape, s.dtype) for s in shards],
        in_specs=[pl.BlockSpec(memory_space=pltpu.VMEM)] * n,
        out_specs=[pl.BlockSpec(memory_space=pl.ANY)] * n,
        scratch_shapes=[pltpu.SemaphoreType.DMA((n,)), pltpu.SemaphoreType.DMA((n, 32)), pltpu.SemaphoreType.DMA((n,))],
        compiler_params=pltpu.CompilerParams(collective_id=collective_id, has_side_effects=True),
        name="gather_weights",
    )(*shards)


class Reduce:
    def __init__(self, place, parts, total, bufs, sems):
        self.p, self.parts, self.total = place, parts, total
        (self.mine, self.from_core, self.out1, self.keep1, self.in1, self.out2, self.keep2, self.in2,
         self.out3, self.in3) = bufs
        self.sems = sems

    def hop(self, i, src, dst, to):
        return pltpu.make_async_remote_copy(src_ref=src, dst_ref=dst, send_sem=self.sems.at[0, i], recv_sem=self.sems.at[1, i],
                                            device_id=to, device_id_type=MESH)

    def copies(self):
        p = self.p
        local = pltpu.make_async_copy(self.parts.at[:, p.c], self.mine, self.sems.at[0, 0])
        core = self.hop(1, self.parts.at[:, 1 - p.c], self.from_core, p.partner)
        h1 = self.hop(2, self.out1, self.in1, p.first2)
        h2 = self.hop(3, self.out2, self.in2, p.second2)
        h3 = [self.hop(3 + k, self.out3.at[k - 1], self.in3.at[k - 1], p.id(z=p.z_at(k))) for k in (1, 2, 3)]
        return local, core, h1, h2, h3

    def t0(self):
        local, core, *_ = self.copies()
        core.start()
        local.start()

    def t1(self):
        p = self.p
        local, core, h1, _, _ = self.copies()
        local.wait()
        core.wait_recv()
        def add(b, carry):
            s, z = b // 4, b % 4
            away, here = p.block(1, s, z), p.block(0, s, z)
            self.out1[b] = (self.mine[away].astype(F32) + self.from_core[away].astype(F32)).astype(BF16)
            return carry
        lax.fori_loop(0, 8, add, 0)
        h1.start()
        def add2(b, carry):
            here = p.block(0, b // 4, b % 4)
            self.keep1[b] = self.mine[here].astype(F32) + self.from_core[here].astype(F32)
            return carry
        lax.fori_loop(0, 8, add2, 0)

    def t2(self):
        _, _, h1, h2, _ = self.copies()
        h1.wait_recv()
        def add(z, carry):
            self.out2[z] = (self.keep1[4 + z] + self.in1[4 + z].astype(F32)).astype(BF16)
            return carry
        lax.fori_loop(0, 4, add, 0)
        h2.start()
        def add2(z, carry):
            self.keep2[z] = self.keep1[z] + self.in1[z].astype(F32)
            return carry
        lax.fori_loop(0, 4, add2, 0)

    def t3(self):
        p = self.p
        _, _, _, h2, h3 = self.copies()
        h2.wait_recv()
        for k in (1, 2, 3):
            z = p.z_at(k)
            self.out3[k - 1] = (self.keep2[z] + self.in2[z].astype(F32)).astype(BF16)
            h3[k - 1].start()
        self.keep2[p.z] = self.keep2[p.z] + self.in2[p.z].astype(F32)

    def t4(self):
        p = self.p
        _, core, h1, h2, h3 = self.copies()
        for h in h3:
            h.wait_recv()
        total = self.keep2[p.z]
        for k in (1, 2, 3):
            total = total + self.in3[k - 1].astype(F32)
        self.total[...] = total
        for h in [core, h1, h2] + h3:
            h.wait_send()


class ReducePlace(Place):
    def __init__(self):
        super().__init__()
        self.first2, self.second2 = self.second, self.first

    def block(self, df, ds, z):
        return self.slot_of(ds, df, z) // 2


def reduce_scratch(shape):
    R, C = shape
    b = lambda n, d=BF16: pltpu.VMEM((n, R, C), d)
    return [b(16), b(16), b(8), b(8, F32), b(8), b(4), b(4, F32), b(4), b(3), b(3)]


class Sum:
    def __init__(self, place, stat, total, stage, came, sems):
        self.p, self.stat, self.total, self.stage, self.came, self.sems = place, stat, total, stage, came, sems

    def copies(self):
        p = self.p
        to = [p.partner, p.first2, p.second2] + [p.id(z=p.z_at(k)) for k in (1, 2, 3)]
        return [pltpu.make_async_remote_copy(src_ref=self.stage.at[min(i, 3)], dst_ref=self.came.at[i], send_sem=self.sems.at[0, i],
                                             recv_sem=self.sems.at[1, i], device_id=to[i], device_id_type=MESH) for i in range(6)]

    def t0(self):
        self.stage[0] = self.stat[...]
        self.copies()[0].start()

    def step(self, i):
        cs = self.copies()
        cs[i].wait_recv()
        self.stage[i + 1] = self.stage[i] + self.came[i]
        for c in cs[i + 1:i + 2] if i < 2 else cs[3:]:
            c.start()

    def t1(self):
        self.step(0)

    def t2(self):
        self.step(1)

    def t3(self):
        self.step(2)

    def t4(self):
        cs = self.copies()
        for c in cs[3:]:
            c.wait_recv()
        self.total[...] = self.stage[3] + self.came[3] + self.came[4] + self.came[5]
        for c in cs:
            c.wait_send()


def reduce_kernel(shapes, *refs):
    n = len(shapes)
    parts, stat, totals, stat_total = refs[:n], refs[n], refs[n + 1:2 * n + 1], refs[2 * n + 1]
    scr = refs[2 * n + 2:]
    bufs, (stage, came, sems, stat_sems) = scr[:-4], scr[-4:]
    place = ReducePlace()
    enter(place)
    jobs = [Sum(place, stat, stat_total, stage, came, stat_sems)]
    jobs += [Reduce(place, parts[i], totals[i], bufs[10 * i:10 * i + 10], sems.at[i]) for i in range(n)]
    n += 1
    for job in jobs:
        job.t0()
    for t in range(n + 3):
        for lag, name in enumerate(("t1", "t2", "t3", "t4")):
            if 0 <= t - lag < n:
                getattr(jobs[t - lag], name)()


def reduce_all(parts, stat, collective_id=1):
    n = len(parts)
    shapes = [p.shape[1:] for p in parts]
    parts = [p.reshape((16, 2) + p.shape[1:]) for p in parts]
    scratch = sum([reduce_scratch(s) for s in shapes], [])
    return pl.pallas_call(
        functools.partial(reduce_kernel, shapes),
        out_shape=[jax.ShapeDtypeStruct(s, F32) for s in shapes] + [jax.ShapeDtypeStruct(stat.shape, F32)],
        in_specs=[pl.BlockSpec(memory_space=pl.ANY)] * n + [pl.BlockSpec(memory_space=pltpu.VMEM)],
        out_specs=[pl.BlockSpec(memory_space=pltpu.VMEM)] * (n + 1),
        scratch_shapes=scratch + [pltpu.VMEM((4,) + stat.shape, F32), pltpu.VMEM((6,) + stat.shape, F32),
                                  pltpu.SemaphoreType.DMA((n, 2, 7)), pltpu.SemaphoreType.DMA((2, 6))],
        compiler_params=pltpu.CompilerParams(collective_id=collective_id, has_side_effects=True, vmem_limit_bytes=64000 << 10),
        name="reduce_grads",
    )(*parts, stat)


VMEM_BYTES = 64000 << 10
TILE = 512
EPS = 1e-5
GELU_C = 0.7978845608028654
GELU_A = 0.044715


def dot(a, b):
    return jnp.dot(a, b, preferred_element_type=F32)


def dot_nt(a, b):
    return lax.dot_general(a, b, (((1,), (1,)), ((), ())), preferred_element_type=F32)


def dot_tn(a, b):
    return lax.dot_general(a, b, (((0,), (0,)), ((), ())), preferred_element_type=F32)


def normalise(v):
    centred = v - jnp.mean(v, axis=-1, keepdims=True)
    rstd = lax.rsqrt(jnp.mean(centred * centred, axis=-1, keepdims=True) + EPS)
    return centred * rstd, rstd


def norm_back(g, xhat, rstd, gain):
    gh = g * gain
    return rstd * (gh - jnp.mean(gh, axis=-1, keepdims=True) - xhat * jnp.mean(gh * xhat, axis=-1, keepdims=True))


def gelu_both(u, grad):
    sq = u * u
    t = jnp.tanh(u * (GELU_C + (GELU_C * GELU_A) * sq))
    half = 0.5 + 0.5 * t
    act = u * half
    slope = half + act * (1.0 - half) * (2.0 * GELU_C + (6.0 * GELU_C * GELU_A) * sq)
    return act, grad * slope


def tile_at(t):
    return pl.ds(pl.multiple_of(t * TILE, TILE), TILE)


def qkv_kernel(tok_ref, skip_ref, w_ref, gs_ref, q_ref, k_ref, v_ref):
    width, half = tok_ref.shape[1], skip_ref.shape[1]
    xhat, _ = normalise(tok_ref[...].astype(F32))
    normed = (xhat * gs_ref[0:1, :] + gs_ref[2:3, :]).astype(BF16)
    q_ref[...] = (dot(normed, w_ref[:, :width]) * 0.125).astype(BF16)
    k_ref[...] = dot(normed, w_ref[:, width:2 * width]).astype(BF16)
    v_ref[:, :half] = dot(normed, w_ref[:, 2 * width:]).astype(BF16)
    v_ref[:, half:] = skip_ref[...]


def project(tokens, skip, w, gs):
    n, width = tokens.shape
    row = lambda c: pl.BlockSpec((TILE, c), lambda t: (t, 0))
    whole = lambda a: pl.BlockSpec(a.shape, lambda t: (0, 0))
    out = jax.ShapeDtypeStruct((n, width), BF16)
    return pl.pallas_call(
        qkv_kernel, grid=(n // TILE,), in_specs=[row(width), row(skip.shape[1]), whole(w), whole(gs)],
        out_specs=[row(width)] * 3, out_shape=[out] * 3,
        compiler_params=pltpu.CompilerParams(vmem_limit_bytes=VMEM_BYTES), name="project",
    )(tokens, skip, w, gs)


def mlp_kernel(tok_h, att_h, cot_h, wout_h, wfc_h, wproj_h, gs_ref,
               lout_h, ghid_h, gatt_h, gproj_h, gfc_h, gout_h, stat_ref,
               tok, att, cot, hidden, oacc, gacc, n2, wout, wfc, wproj, act, gi, gw, insem, wsem, gsem, osem):
    n, width = tok.shape
    n_ff = wfc_h.shape[1] // width
    n_t = n // TILE
    gain, shift = gs_ref[1:2, :], gs_ref[3:4, :]
    loads = [pltpu.make_async_copy(h, v, insem.at[i]) for i, (h, v) in enumerate([(wout_h, wout), (att_h, att), (tok_h, tok), (cot_h, cot)])]

    def chunk(j, slot):
        cols = pl.ds(pl.multiple_of(j * width, width), width)
        return (pltpu.make_async_copy(wfc_h.at[:, cols], wfc.at[slot], wsem.at[0, slot]),
                pltpu.make_async_copy(wproj_h.at[cols, :], wproj.at[slot], wsem.at[1, slot]))

    def grads(j):
        cols = pl.ds(pl.multiple_of(j * width, width), width)
        return (pltpu.make_async_copy(gw.at[0], gproj_h.at[cols, :], gsem.at[0]),
                pltpu.make_async_copy(gw.at[1], gfc_h.at[:, cols], gsem.at[1]))

    for c in loads:
        c.start()
    for c in chunk(0, 0):
        c.start()
    for c in loads[:3]:
        c.wait()

    def forward(t, carry):
        r = tile_at(t)
        h = tok[r, :].astype(F32) + dot(att[r, :], wout[...])
        hidden[r, :] = h
        oacc[r, :] = h
        gacc[r, :] = jnp.zeros_like(h)
        xhat, _ = normalise(h)
        n2[r, :] = (xhat * gain + shift).astype(BF16)
        return carry
    lax.fori_loop(0, n_t, forward, 0)
    loads[3].wait()

    def ff(j, carry):
        slot = j % 2
        for c in chunk(j, slot):
            c.wait()

        @pl.when(j + 1 < n_ff)
        def _():
            for c in chunk(j + 1, 1 - slot):
                c.start()

        def tile(t, carry):
            r = tile_at(t)
            a, g = gelu_both(dot(n2[r, :], wfc[slot]), dot_nt(cot[r, :], wproj[slot]))
            a, g = a.astype(BF16), g.astype(BF16)
            act[r, :] = a
            gi[r, :] = g
            oacc[r, :] += dot(a, wproj[slot])
            gacc[r, :] += dot_nt(g, wfc[slot])
            return carry
        lax.fori_loop(0, n_t, tile, 0)

        @pl.when(j > 0)
        def _():
            for c in grads(j - 1):
                c.wait()
        gw[0] = dot_tn(act[...], cot[...]).astype(BF16)
        gw[1] = dot_tn(n2[...], gi[...]).astype(BF16)
        for c in grads(j):
            c.start()
        return carry
    lax.fori_loop(0, n_ff, ff, 0)

    def out(t):
        r = tile_at(t)
        return (pltpu.make_async_copy(tok.at[r, :], lout_h.at[r, :], osem.at[0]),
                pltpu.make_async_copy(hidden.at[r, :], ghid_h.at[r, :], osem.at[1]),
                pltpu.make_async_copy(act.at[r, :], gatt_h.at[r, :], osem.at[2]))
    for c in grads(n_ff - 1):
        c.wait()
    stat_ref[...] = jnp.zeros_like(stat_ref)

    def backward(t, carry):
        r = tile_at(t)
        tok[r, :] = oacc[r, :].astype(BF16)
        xhat, rstd = normalise(hidden[r, :])
        g = gacc[r, :]
        stat_ref[1:2, :] += jnp.sum(g * xhat, axis=0, keepdims=True)
        stat_ref[3:4, :] += jnp.sum(g, axis=0, keepdims=True)
        gh = cot[r, :].astype(F32) + norm_back(g, xhat, rstd, gain)
        hidden[r, :] = gh
        gb = gh.astype(BF16)
        gi[r, :] = gb
        act[r, :] = dot_nt(gb, wout[...]).astype(BF16)
        for c in out(t):
            c.start()
        return carry
    lax.fori_loop(0, n_t, backward, 0)
    gw[0] = dot_tn(att[...], gi[...]).astype(BF16)
    last = pltpu.make_async_copy(gw.at[0], gout_h, gsem.at[0])
    last.start()
    last.wait()
    for i, (v, h) in enumerate([(tok, lout_h), (hidden, ghid_h), (act, gatt_h)]):
        pltpu.make_async_copy(v, h, osem.at[i]).wait()


def mlp(tokens, att, cot, wout, wfc, wproj, gs):
    n, width = tokens.shape
    ff = wfc.shape[1]
    s = jax.ShapeDtypeStruct
    any_, vm = pl.BlockSpec(memory_space=pl.ANY), pl.BlockSpec(memory_space=pltpu.VMEM)
    big = lambda d: pltpu.VMEM((n, width), d)
    sq = lambda k: pltpu.VMEM((k, width, width), BF16)
    return pl.pallas_call(
        mlp_kernel, in_specs=[any_] * 6 + [vm], out_specs=[any_] * 6 + [vm],
        out_shape=[s((n, width), BF16), s((n, width), F32), s((n, width), BF16), s((ff, width), BF16), s((width, ff), BF16),
                   s((width, width), BF16), s((8, width), F32)],
        scratch_shapes=[big(BF16), big(BF16), big(BF16), big(F32), big(F32), big(F32), big(BF16), pltpu.VMEM((width, width), BF16),
                        sq(2), sq(2), big(BF16), big(BF16), sq(2),
                        pltpu.SemaphoreType.DMA((4,)), pltpu.SemaphoreType.DMA((2, 2)), pltpu.SemaphoreType.DMA((2,)), pltpu.SemaphoreType.DMA((3,))],
        compiler_params=pltpu.CompilerParams(vmem_limit_bytes=VMEM_BYTES), name="mlp",
    )(tokens, att, cot, wout, wfc, wproj, gs)


def qkv_back_kernel(tok_h, ghid_h, gq_h, gk_h, gv_h, w_h, gs_ref, gtok_h, gskip_h, gw_h, stat_ref,
                    tok, ghid, gq, gk, gv, w, normed, gskip, gw, insem, osem):
    n, width = tok.shape
    half = gskip.shape[1]
    n_t = n // TILE
    gain, shift = gs_ref[0:1, :], gs_ref[2:3, :]
    loads = [pltpu.make_async_copy(h, v, insem.at[i]) for i, (h, v) in enumerate([(tok_h, tok), (w_h, w), (gq_h, gq), (gk_h, gk), (gv_h, gv), (ghid_h, ghid)])]
    for c in loads:
        c.start()
    for c in loads:
        c.wait()
    stat_ref[...] = jnp.zeros_like(stat_ref)

    def out(t):
        r = tile_at(t)
        return (pltpu.make_async_copy(ghid.at[r, :], gtok_h.at[r, :], osem.at[0]),
                pltpu.make_async_copy(gskip.at[r, :], gskip_h.at[r, :], osem.at[1]))

    def tile(t, carry):
        r = tile_at(t)
        xhat, rstd = normalise(tok[r, :].astype(F32))
        normed[r, :] = (xhat * gain + shift).astype(BF16)
        gskip[r, :] = gv[r, half:].astype(F32)
        g = (dot_nt(gq[r, :], w[:, :width]) + dot_nt(gk[r, :], w[:, width:2 * width])
             + dot_nt(gv[r, :half], w[:, 2 * width:]))
        stat_ref[0:1, :] += jnp.sum(g * xhat, axis=0, keepdims=True)
        stat_ref[2:3, :] += jnp.sum(g, axis=0, keepdims=True)
        ghid[r, :] += norm_back(g, xhat, rstd, gain)
        for c in out(t):
            c.start()
        return carry
    lax.fori_loop(0, n_t, tile, 0)
    gw[:, :width] = dot_tn(normed[...], gq[...]).astype(BF16)
    gw[:, width:2 * width] = dot_tn(normed[...], gk[...]).astype(BF16)
    gw[:, 2 * width:] = dot_tn(normed[...], gv[:, :half]).astype(BF16)
    last = pltpu.make_async_copy(gw, gw_h, insem.at[0])
    last.start()
    last.wait()
    pltpu.make_async_copy(ghid, gtok_h, osem.at[0]).wait()
    pltpu.make_async_copy(gskip, gskip_h, osem.at[1]).wait()


def project_back(tokens, ghid, gq, gk, gv, w, gs):
    n, width = tokens.shape
    fresh = w.shape[1] - 2 * width
    half = width - fresh
    s = jax.ShapeDtypeStruct
    any_, vm = pl.BlockSpec(memory_space=pl.ANY), pl.BlockSpec(memory_space=pltpu.VMEM)
    big = lambda d: pltpu.VMEM((n, width), d)
    return pl.pallas_call(
        qkv_back_kernel, in_specs=[any_] * 6 + [vm], out_specs=[any_] * 3 + [vm],
        out_shape=[s((n, width), F32), s((n, half), F32), s(w.shape, BF16), s((8, width), F32)],
        scratch_shapes=[big(BF16), big(F32), big(BF16), big(BF16), big(BF16), pltpu.VMEM(w.shape, BF16), big(BF16), pltpu.VMEM((n, half), F32),
                        pltpu.VMEM(w.shape, BF16), pltpu.SemaphoreType.DMA((6,)), pltpu.SemaphoreType.DMA((2,))],
        compiler_params=pltpu.CompilerParams(vmem_limit_bytes=VMEM_BYTES), name="project_back",
    )(tokens, ghid, gq, gk, gv, w, gs)


AXES = ("dp", "fsdp")


def body(direct, tokens, skip_values, w_qkv, w_out, w_fc, w_proj, norm_gains, norm_shifts, segment_ids, pad_mask, cotangent):
    micro, rows, length, width = tokens.shape
    half, ff = skip_values.shape[3], w_fc.shape[1]
    seqs = micro * rows
    n = seqs * length
    n_dev, own = width // norm_gains.shape[1], norm_gains.shape[1]
    slot = lax.axis_index(AXES)
    flat = lambda a: a.reshape(n, a.shape[-1])
    seq = lambda a: a.reshape(seqs, length, a.shape[-1])
    tok, skip, cot = flat(tokens), flat(skip_values), flat(cotangent)
    seg, pad = segment_ids.reshape(seqs, length), pad_mask.reshape(seqs, length)
    rows8 = jnp.concatenate([norm_gains, norm_shifts, jnp.zeros((4, own), BF16)], axis=0)
    if direct:
        place = lax.dynamic_update_slice(jnp.zeros((8, width), BF16), rows8, (0, slot * own))
        gs_all, qkv, out, fc, proj = gather_all([place, w_qkv, w_out, w_fc, w_proj])
        gs = jnp.sum(gs_all.astype(F32), axis=0)
        qkv, out, fc, proj = [a.reshape(-1, a.shape[2]) for a in (qkv, out, fc, proj)]
    else:
        qkv, out, fc, proj = [lax.all_gather(w, AXES, axis=0, tiled=True) for w in (w_qkv, w_out, w_fc, w_proj)]
        gs = lax.all_gather(rows8, AXES, axis=1, tiled=True).astype(F32)
    q, k, v = project(tok, skip, qkv, gs)
    att, lse = attend(seq(q), seq(k), seq(v), seg, pad)
    lout, ghid, gatt, gproj, gfc, gout, stat_two = mlp(tok, flat(att), cot, out, fc, proj, gs)
    gq, gk, gv = attend_back(seq(q), seq(k), seq(v), seq(gatt), lse, seg, pad)
    gtok, gskip, gqkv, stat_one = project_back(tok, ghid, flat(gq), flat(gk), flat(gv), qkv, gs)
    stat = stat_one + stat_two
    if direct:
        split = lambda a: a.reshape(n_dev, a.shape[0] // n_dev, a.shape[1])
        fcs, projs = split(gfc), split(gproj)
        h1, h2 = ff // 2, width // 2
        p = reduce_all([projs[:, :, :h2], projs[:, :, h2:], fcs[:, :, :h1], fcs[:, :, h1:], split(gout), split(gqkv)], stat)
        total_proj = jnp.concatenate(p[0:2], axis=1)
        total_fc = jnp.concatenate(p[2:4], axis=1)
        total_out, total_qkv = p[4], p[5]
        sums = lax.dynamic_slice(p[6], (0, slot * own), (8, own))
        gains, shifts = sums[0:2], sums[2:4]
    else:
        total_qkv, total_out, total_fc, total_proj = [
            lax.psum_scatter(g.astype(F32), AXES, scatter_dimension=0, tiled=True) for g in (gqkv, gout, gfc, gproj)]
        gains = lax.psum_scatter(stat[0:2], AXES, scatter_dimension=1, tiled=True)
        shifts = lax.psum_scatter(stat[2:4], AXES, scatter_dimension=1, tiled=True)
    shape4 = lambda a: a.reshape(micro, rows, length, a.shape[-1])
    return (shape4(lout), shape4(gtok), shape4(gskip), total_qkv, total_out, total_fc, total_proj, gains, shifts)


def solution(mesh):
    tok, mat, row, ids = P(None, AXES, None, None), P(AXES, None), P(None, AXES), P(None, AXES, None)
    direct = dict(mesh.shape) == {"dp": 2, "fsdp": 16}
    return jax.shard_map(
        functools.partial(body, direct), mesh=mesh,
        in_specs=(tok, tok, mat, mat, mat, mat, row, row, ids, ids, tok),
        out_specs=(tok, tok, tok, mat, mat, mat, mat, row, row), check_vma=False)
```

```python
import functools
import jax
import jax.numpy as jnp
from jax import lax
from jax.experimental import pallas as pl
from jax.experimental.pallas import tpu as pltpu
from jax.sharding import PartitionSpec as P

F32, BF16 = jnp.float32, jnp.bfloat16

HEAD = 64
BLK = 128
WIN = 5
MASKED = -1e9
PAIRS_FWD, PAIRS_BWD = 6, 6


def build_bias(seg_row, pad_row, bias_ref, n_blk):
    code = jnp.where(pad_row == 1, seg_row, -1)
    key = lax.broadcasted_iota(jnp.int32, (BLK, BLK), 0)
    row = lax.broadcasted_iota(jnp.int32, (BLK, BLK), 1)
    for kb in range(n_blk):
        code_k = jnp.broadcast_to(code[:, kb * BLK:(kb + 1) * BLK], (BLK, BLK)).T
        for qb in range(kb, min(kb + WIN, n_blk)):
            vis = code_k == seg_row[:, qb * BLK:(qb + 1) * BLK]
            if kb == qb:
                vis = (vis & (key < row)) | (key == row)
            t = kb - qb + WIN - 1
            bias_ref[qb, t * BLK:(t + 1) * BLK, :] = jnp.where(vis, 0.0, MASKED)


def stack_heads(x):
    low = lax.broadcasted_iota(jnp.int32, x.shape, 1) < HEAD
    zero = jnp.zeros_like(x)
    return jnp.concatenate([jnp.where(low, x, zero), jnp.where(low, zero, x)], axis=0)


def join_heads(x2):
    return jnp.concatenate([x2[:HEAD, :BLK], x2[HEAD:, BLK:]], axis=0)


def twice(x):
    return jnp.concatenate([x, x], axis=1)


def visible_blocks(seg_s, row, qb):
    first = seg_s[row, qb * BLK]
    n = jnp.int32(1)
    for back in range(1, WIN):
        kb = jnp.maximum(qb - back, 0)
        seen = (qb >= back) & (seg_s[row, kb * BLK + BLK - 1] == first)
        n = n + seen.astype(jnp.int32)
    return n


def over_queries(seg_s, row, n_blk, one):
    def step(qb, carry):
        n_vis = visible_blocks(seg_s, row, qb)
        for n in range(1, WIN + 1):
            @pl.when(n_vis == n)
            def _():
                one(n, qb)
        return carry
    lax.fori_loop(0, n_blk, step, 0)


def block(i, n=1):
    return pl.ds(pl.multiple_of(i * BLK, BLK), n * BLK)


def attend_nt(a, b):
    return lax.dot_general(a, b, (((1,), (1,)), ((), ())), preferred_element_type=F32)


def fwd_kernel(n_blk, pairs, seg_s, seg_ref, pad_ref, q_ref, k_ref, v_ref, o_ref, lse_ref, bias_ref, vt_ref):
    row = pl.program_id(0)

    @pl.when(pl.program_id(1) == 0)
    def _():
        build_bias(seg_ref[...], pad_ref[...], bias_ref, n_blk)

    lanes = [slice(i * BLK, (i + 1) * BLK) for i in range(pairs)]
    for kb in range(n_blk):
        for h in lanes:
            vt_ref[h, kb * BLK:(kb + 1) * BLK] = v_ref[kb * BLK:(kb + 1) * BLK, h].T

    def one(n, qb):
        keys, here = block(qb - n + 1, n), block(qb)
        b = twice(bias_ref[qb, (WIN - n) * BLK:, :])
        s = [attend_nt(k_ref[keys, h], stack_heads(q_ref[here, h])) + b for h in lanes]
        for i, h in enumerate(lanes):
            m = jnp.max(s[i], axis=0, keepdims=True)
            p = jnp.exp(s[i] - m)
            total = jnp.sum(p, axis=0, keepdims=True)
            o2 = jnp.dot(vt_ref[h, keys], p.astype(BF16), preferred_element_type=F32) * (1.0 / total)
            o_ref[here, h] = join_heads(o2).astype(BF16).T
            lse_ref[i, qb] = m + jnp.log(total)
    over_queries(seg_s, row, n_blk, one)


def attend(q, k, v, seg, pad):
    rows, length, width = q.shape
    n_blk, pairs = length // BLK, PAIRS_FWD
    groups = width // 128 // pairs
    tok = pl.BlockSpec((None, length, pairs * 128), lambda r, h, s: (r, 0, h))
    ids = pl.BlockSpec((None, 1, length), lambda r, h, s: (r, 0, 0))
    return pl.pallas_call(
        functools.partial(fwd_kernel, n_blk, pairs),
        grid_spec=pltpu.PrefetchScalarGridSpec(
            num_scalar_prefetch=1, grid=(rows, groups),
            in_specs=[ids, ids, tok, tok, tok],
            out_specs=[tok, pl.BlockSpec((None, pairs, n_blk, 1, 2 * BLK), lambda r, h, s: (r, h, 0, 0, 0))],
            scratch_shapes=[pltpu.VMEM((n_blk, WIN * BLK, BLK), F32), pltpu.VMEM((pairs * BLK, length), BF16)]),
        out_shape=[jax.ShapeDtypeStruct((rows, length, width), BF16), jax.ShapeDtypeStruct((rows, width // 128, n_blk, 1, 2 * BLK), F32)],
        compiler_params=pltpu.CompilerParams(dimension_semantics=("arbitrary", "arbitrary"), vmem_limit_bytes=64000 << 10),
        name="attend",
    )(seg, seg[:, None, :], pad[:, None, :], q, k, v)


def bwd_kernel(n_blk, pairs, seg_s, seg_ref, pad_ref, q_ref, k_ref, v_ref, g_ref, lse_ref, dq_ref, dk_ref, dv_ref,
               bias_ref, kt_ref, dk_acc, dv_acc):
    row = pl.program_id(0)

    @pl.when(pl.program_id(1) == 0)
    def _():
        build_bias(seg_ref[...], pad_ref[...], bias_ref, n_blk)

    lanes = [slice(i * BLK, (i + 1) * BLK) for i in range(pairs)]
    for kb in range(n_blk):
        for h in lanes:
            kt_ref[h, kb * BLK:(kb + 1) * BLK] = k_ref[kb * BLK:(kb + 1) * BLK, h].T
    dk_acc[...] = jnp.zeros_like(dk_acc)
    dv_acc[...] = jnp.zeros_like(dv_acc)

    def one(n, qb):
        keys, here = block(qb - n + 1, n), block(qb)
        b = twice(bias_ref[qb, (WIN - n) * BLK:, :])
        for i, h in enumerate(lanes):
            q2, g2 = stack_heads(q_ref[here, h]), stack_heads(g_ref[here, h])
            p = jnp.exp(attend_nt(k_ref[keys, h], q2) + b - lse_ref[i, qb])
            dp = attend_nt(v_ref[keys, h], g2)
            inner = jnp.sum(p * dp, axis=0, keepdims=True)
            ds = (p * (dp - inner)).astype(BF16)
            dv_acc[keys, h] += jnp.dot(p.astype(BF16), g2, preferred_element_type=F32)
            dk_acc[keys, h] += jnp.dot(ds, q2, preferred_element_type=F32)
            dq2 = jnp.dot(kt_ref[h, keys], ds, preferred_element_type=F32)
            dq_ref[here, h] = (join_heads(dq2) * 0.125).astype(BF16).T
    over_queries(seg_s, row, n_blk, one)
    dk_ref[...] = dk_acc[...].astype(BF16)
    dv_ref[...] = dv_acc[...].astype(BF16)


def attend_back(q, k, v, g, lse, seg, pad):
    rows, length, width = q.shape
    n_blk, pairs = length // BLK, PAIRS_BWD
    groups = width // 128 // pairs
    tok = pl.BlockSpec((None, length, pairs * 128), lambda r, h, s: (r, 0, h))
    ids = pl.BlockSpec((None, 1, length), lambda r, h, s: (r, 0, 0))
    out = jax.ShapeDtypeStruct((rows, length, width), BF16)
    return pl.pallas_call(
        functools.partial(bwd_kernel, n_blk, pairs),
        grid_spec=pltpu.PrefetchScalarGridSpec(
            num_scalar_prefetch=1, grid=(rows, groups),
            in_specs=[ids, ids, tok, tok, tok, tok, pl.BlockSpec((None, pairs, n_blk, 1, 2 * BLK), lambda r, h, s: (r, h, 0, 0, 0))],
            out_specs=[tok, tok, tok],
            scratch_shapes=[pltpu.VMEM((n_blk, WIN * BLK, BLK), F32), pltpu.VMEM((pairs * BLK, length), BF16),
                            pltpu.VMEM((length, pairs * BLK), F32), pltpu.VMEM((length, pairs * BLK), F32)]),
        out_shape=[out, out, out],
        compiler_params=pltpu.CompilerParams(dimension_semantics=("arbitrary", "arbitrary"), vmem_limit_bytes=64000 << 10),
        name="attend_back",
    )(seg, seg[:, None, :], pad[:, None, :], q, k, v, g, lse)


MESH = pl.DeviceIdType.MESH
NZ = 4


class Place:
    def __init__(self):
        dp, fs = lax.axis_index("dp"), lax.axis_index("fsdp")
        self.x, self.z, self.y, self.c = dp, fs // 4, (fs // 2) % 2, fs % 2
        self.slot = self.x * 16 + fs
        self.first = self.id(x=jnp.where(self.c == 0, 1 - self.x, self.x), y=jnp.where(self.c == 0, self.y, 1 - self.y))
        self.second = self.id(x=jnp.where(self.c == 0, self.x, 1 - self.x), y=jnp.where(self.c == 0, 1 - self.y, self.y))
        self.partner = self.id(c=1 - self.c)

    def id(self, x=None, y=None, z=None, c=None):
        x = self.x if x is None else x
        y = self.y if y is None else y
        z = self.z if z is None else z
        c = self.c if c is None else c
        return (x, z * 4 + y * 2 + c)

    def z_at(self, k):
        return (self.z + k) % NZ

    def peers(self):
        return [self.partner, self.first, self.second] + [self.id(z=self.z_at(k)) for k in (1, 2, 3)]

    def slot_of(self, df, ds, z):
        dx = jnp.where(self.c == 0, df, ds)
        dy = jnp.where(self.c == 0, ds, df)
        x = jnp.where(dx == 1, 1 - self.x, self.x)
        y = jnp.where(dy == 1, 1 - self.y, self.y)
        return x * 16 + z * 4 + y * 2 + self.c


def enter(place):
    bar = pltpu.get_barrier_semaphore()
    for peer in place.peers():
        pl.semaphore_signal(bar, inc=1, device_id=peer, device_id_type=MESH)
    pl.semaphore_wait(bar, 6)


class Gather:
    SENDS = 31

    def __init__(self, place, shard, out, send, recv, own):
        self.p, self.shard, self.out, self.send, self.recv, self.own = place, shard, out, send, recv, own
        self.size = shard.shape[0]

    def at(self, slot, n=1):
        return self.out.at[pl.ds(pl.multiple_of(slot * self.size, 8), n * self.size), :]

    def push(self, src, slot, to):
        pltpu.make_async_remote_copy(src_ref=src, dst_ref=self.at(slot), send_sem=self.send, recv_sem=self.recv.at[slot],
                                     device_id=to, device_id_type=MESH).start()

    def arrived(self, slot):
        pltpu.make_async_copy(self.at(slot), self.at(slot), self.recv.at[slot]).wait()

    def keep(self, slot):
        return pltpu.make_async_copy(self.shard, self.at(slot), self.own)

    def s1(self):
        p = self.p
        self.keep(p.slot).start()
        for k in (1, 3, 2):
            self.push(self.shard, p.slot, p.id(z=p.z_at(k)))
        for to in (p.first, p.partner, p.second):
            self.push(self.shard, p.slot, to)

    def s2(self):
        p = self.p
        for k in (1, 3, 2):
            slot = p.slot_of(0, 0, p.z_at(k))
            self.arrived(slot)
            for to in (p.first, p.second, p.partner):
                self.push(self.at(slot), slot, to)

    def s3(self):
        p = self.p
        for k in (0, 1, 3, 2):
            slot = p.slot_of(1, 0, p.z_at(k))
            self.arrived(slot)
            for to in (p.second, p.partner):
                self.push(self.at(slot), slot, to)

    def s4(self):
        p = self.p
        for df in (0, 1):
            for k in (0, 1, 3, 2):
                slot = p.slot_of(df, 1, p.z_at(k))
                self.arrived(slot)
                self.push(self.at(slot), slot, p.partner)

    def s5(self):
        for k in range(16):
            self.arrived(2 * k + 1 - self.p.c)
        self.keep(self.p.slot).wait()

    def drain(self):
        done = self.at(0, self.SENDS)
        pltpu.make_async_copy(done, done, self.send).wait()


class GatherPart:
    def __init__(self, place, j, shard, out, send, recv, own):
        self.p, self.shard, self.out, self.send, self.recv, self.own = place, shard, out, send, recv, own
        self.size = shard.shape[0]
        self.x, self.zs = j // 2, (j % 2 * 2, j % 2 * 2 + 1)

    def at(self, i, n=1):
        return self.out.at[pl.ds(pl.multiple_of(i * self.size, 8), n * self.size), :]

    def push(self, src, i, to):
        pltpu.make_async_remote_copy(src_ref=src, dst_ref=self.at(i), send_sem=self.send.at[i], recv_sem=self.recv.at[i],
                                     device_id=to, device_id_type=MESH).start()

    def each(self, stage, do):
        p = self.p
        for zi in (0, 1):
            for y in (0, 1):
                dx, dy, dz = p.x != self.x, p.y != y, p.z != self.zs[zi]
                df, ds = jnp.where(p.c == 0, dx, dy), jnp.where(p.c == 0, dy, dx)
                near = jnp.logical_not(dx | dy)
                when = {1: near & jnp.logical_not(dz), 2: near & dz, 3: df & jnp.logical_not(ds), 4: ds}[stage]
                i = zi * 4 + y * 2 + p.c

                @pl.when(when)
                def _():
                    do(i)

    def keep(self, i):
        return pltpu.make_async_copy(self.shard, self.at(i), self.own)

    def arrived(self, i):
        pltpu.make_async_copy(self.at(i), self.at(i), self.recv.at[i]).wait()

    def pass_on(self, stage, targets):
        def do(i):
            self.arrived(i)
            for to in targets:
                self.push(self.at(i), i, to)
        self.each(stage, do)

    def s1(self):
        p = self.p

        def do(i):
            self.keep(i).start()
            for to in [p.id(z=p.z_at(k)) for k in (1, 3, 2)] + [p.first, p.partner, p.second]:
                self.push(self.shard, i, to)
        self.each(1, do)

    def s2(self):
        self.pass_on(2, (self.p.first, self.p.second, self.p.partner))

    def s3(self):
        self.pass_on(3, (self.p.second, self.p.partner))

    def s4(self):
        self.pass_on(4, (self.p.partner,))

    def s5(self):
        for k in range(4):
            self.arrived(2 * k + 1 - self.p.c)
        self.each(1, lambda i: self.keep(i).wait())

    def drain(self):
        for stage, n in ((1, 6), (2, 3), (3, 2), (4, 1)):
            def do(i):
                done = self.at(0, n)
                pltpu.make_async_copy(done, done, self.send.at[i]).wait()
            self.each(stage, do)


VMEM_BYTES = 64000 << 10
TILE = 512
EPS = 1e-5
GELU_C = 0.7978845608028654
GELU_A = 0.044715


def dot(a, b):
    return jnp.dot(a, b, preferred_element_type=F32)


def dot_nt(a, b):
    return lax.dot_general(a, b, (((1,), (1,)), ((), ())), preferred_element_type=F32)


def dot_tn(a, b):
    return lax.dot_general(a, b, (((0,), (0,)), ((), ())), preferred_element_type=F32)


def normalise(v):
    centred = v - jnp.mean(v, axis=-1, keepdims=True)
    rstd = lax.rsqrt(jnp.mean(centred * centred, axis=-1, keepdims=True) + EPS)
    return centred * rstd, rstd


def norm_back(g, xhat, rstd, gain):
    gh = g * gain
    return rstd * (gh - jnp.mean(gh, axis=-1, keepdims=True) - xhat * jnp.mean(gh * xhat, axis=-1, keepdims=True))


def gelu_both(u, grad):
    sq = u * u
    t = jnp.tanh(u * (GELU_C + (GELU_C * GELU_A) * sq))
    half = 0.5 + 0.5 * t
    act = u * half
    slope = half + act * (1.0 - half) * (2.0 * GELU_C + (6.0 * GELU_C * GELU_A) * sq)
    return act, grad * slope


def tile_at(t):
    return pl.ds(pl.multiple_of(t * TILE, TILE), TILE)


def qkv_kernel(tok_ref, skip_ref, w_ref, gs_ref, q_ref, k_ref, v_ref):
    width, half = tok_ref.shape[1], skip_ref.shape[1]
    xhat, _ = normalise(tok_ref[...].astype(F32))
    normed = (xhat * gs_ref[0:1, :] + gs_ref[2:3, :]).astype(BF16)
    q_ref[...] = (dot(normed, w_ref[:, :width]) * 0.125).astype(BF16)
    k_ref[...] = dot(normed, w_ref[:, width:2 * width]).astype(BF16)
    v_ref[:, :half] = dot(normed, w_ref[:, 2 * width:]).astype(BF16)
    v_ref[:, half:] = skip_ref[...]


def project(tokens, skip, w, gs):
    n, width = tokens.shape
    row = lambda c: pl.BlockSpec((TILE, c), lambda t: (t, 0))
    whole = lambda a: pl.BlockSpec(a.shape, lambda t: (0, 0))
    out = jax.ShapeDtypeStruct((n, width), BF16)
    return pl.pallas_call(
        qkv_kernel, grid=(n // TILE,), in_specs=[row(width), row(skip.shape[1]), whole(w), whole(gs)],
        out_specs=[row(width)] * 3, out_shape=[out] * 3,
        compiler_params=pltpu.CompilerParams(vmem_limit_bytes=VMEM_BYTES), name="project",
    )(tokens, skip, w, gs)


def first_gather(place, shards, outs, sems):
    send, recv, own, psend, precv, pown = sems
    jobs = [Gather(place, shards[i], outs[i], send.at[i], recv.at[i], own.at[i]) for i in range(4)]
    return jobs + [GatherPart(place, 0, shards[4], outs[4], psend, precv, pown)]


def start_kernel(tok_h, skip_h, rows_ref, qkv_ref, out_ref, fc_ref, proj_ref,
                 q_h, k_h, v_h, gs_ref, gs_all, qkv_all, out_all, fc_all, proj_all,
                 tok, skip, xhat, w, gsb, q, k, v, insem, osem, *sems):
    n, width = tok.shape
    half = skip.shape[1]
    n_t = n // TILE
    place = Place()
    loads = [pltpu.make_async_copy(tok_h, tok, insem.at[0]), pltpu.make_async_copy(skip_h, skip, insem.at[1])]
    for c in loads:
        c.start()
    enter(place)
    shards = (rows_ref, qkv_ref, out_ref, fc_ref.at[:, pl.ds(0, width)], proj_ref)
    jobs = first_gather(place, shards, (gs_all, qkv_all, out_all, fc_all, proj_all), sems)
    rows, qkv, out, fc, proj = jobs
    for job in jobs:
        job.s1()
    for c in loads:
        c.wait()

    def centre(t, carry):
        r = tile_at(t)
        xhat[r, :], _ = normalise(tok[r, :].astype(F32))
        return carry
    lax.fori_loop(0, n_t, centre, 0)
    rows.s2(), qkv.s2(), rows.s3(), qkv.s3(), out.s2(), rows.s4(), qkv.s4()
    fc.s2(), proj.s2(), out.s3(), rows.s5(), qkv.s5()
    wload = pltpu.make_async_copy(qkv_all, w, insem.at[2])
    gload = pltpu.make_async_copy(gs_all, gsb, insem.at[3])
    wload.start(), gload.start()
    fc.s3(), proj.s3()
    gload.wait()
    gs_ref[...] = jnp.sum(gsb[...].astype(F32).reshape(gsb.shape[0] // 8, 8, width), axis=0)
    wload.wait()

    def copies(r):
        return [pltpu.make_async_copy(s.at[r, :], h.at[r, :], osem.at[i]) for i, (s, h) in enumerate([(q, q_h), (k, k_h), (v, v_h)])]

    plan = {0: [out.s4, fc.s4], 1: [proj.s4, out.s5], 2: [fc.s5], 3: [proj.s5]}

    def tile(t, carry):
        r = tile_at(t)
        normed = (xhat[r, :] * gs_ref[0:1, :] + gs_ref[2:3, :]).astype(BF16)
        q[r, :] = (dot(normed, w[:, :width]) * 0.125).astype(BF16)
        k[r, :] = dot(normed, w[:, width:2 * width]).astype(BF16)
        v[r, :half] = dot(normed, w[:, 2 * width:]).astype(BF16)
        v[r, half:] = skip[r, :]
        for c in copies(r):
            c.start()
        for when, steps in plan.items():
            @pl.when(t == when)
            def _():
                for s in steps:
                    s()
        return carry
    lax.fori_loop(0, n_t, tile, 0)
    for job in jobs:
        job.drain()
    for c in copies(pl.ds(0, n)):
        c.wait()


def start(tokens, skip, rows, qkv, out, fc, proj):
    n, width = tokens.shape
    n_dev = width // out.shape[0]
    s, dma = jax.ShapeDtypeStruct, pltpu.SemaphoreType.DMA
    any_, vm = pl.BlockSpec(memory_space=pl.ANY), pl.BlockSpec(memory_space=pltpu.VMEM)
    big = lambda d: pltpu.VMEM((n, width), d)
    act = s((n, width), BF16)
    gathered = [(8 * n_dev, width), (width, qkv.shape[1]), (width, width), (width, width), (8 * proj.shape[0], width)]
    return pl.pallas_call(
        start_kernel, in_specs=[any_, any_] + [vm] * 5, out_specs=[any_] * 3 + [vm] + [any_] * 5,
        out_shape=[act] * 3 + [s((8, width), F32)] + [s(g, BF16) for g in gathered],
        scratch_shapes=[big(BF16), pltpu.VMEM(skip.shape, BF16), big(F32), pltpu.VMEM((width, qkv.shape[1]), BF16), pltpu.VMEM((8 * n_dev, width), BF16),
                        big(BF16), big(BF16), big(BF16), dma((4,)), dma((3,)),
                        dma((4,)), dma((4, n_dev)), dma((4,)), dma((8,)), dma((8,)), dma(())],
        compiler_params=pltpu.CompilerParams(vmem_limit_bytes=VMEM_BYTES, collective_id=0, has_side_effects=True), name="start",
    )(tokens, skip, rows, qkv, out, fc, proj)


FF_ORDER = (0, 2, 1, 3)


def ff_at(i):
    return 2 * (i % 2) + i // 2


def mlp_kernel(remote, tok_h, att_h, cot_h, wout_h, *refs):
    if remote:
        fc0_h, proj0_h, fc_ref, proj_ref, *refs = refs
    else:
        wfc_h, wproj_h, *refs = refs
    (gs_ref, lout_h, ghid_h, gatt_h, n2_h, gb_h, act_h, gi_h, stat_ref), refs = refs[:9], refs[9:]
    if remote:
        (fc_all, proj_all), refs = refs[:2], refs[2:]
    (tok, att, cot, hidden, oacc, gacc, n2, gb, wout, wfc, wproj, act, gi, insem, wsem, asem, osem), sems = refs[:17], refs[17:]
    n, width = tok.shape
    n_ff = 4
    n_t = n // TILE
    gain, shift = gs_ref[1:2, :], gs_ref[3:4, :]

    def load(src_fc, src_proj, slot):
        return (pltpu.make_async_copy(src_fc, wfc.at[slot], wsem.at[0, slot]), pltpu.make_async_copy(src_proj, wproj.at[slot], wsem.at[1, slot]))

    loads = [pltpu.make_async_copy(h, v, insem.at[i]) for i, (h, v) in enumerate([(wout_h, wout), (att_h, att), (tok_h, tok), (cot_h, cot)])]
    for c in loads:
        c.start()
    plan = {}
    if remote:
        fsend, frecv, fown, psend, precv, pown = sems
        place = Place()
        enter(place)
        size = proj_ref.shape[0]
        sets = []
        for i in range(1, n_ff):
            j = FF_ORDER[i]
            sets.append([Gather(place, fc_ref.at[:, pl.ds(j * width, width)], fc_all.at[i - 1], fsend.at[i - 1], frecv.at[i - 1], fown.at[i - 1]),
                         GatherPart(place, j, proj_ref, proj_all.at[i - 1], psend.at[i - 1], precv.at[i - 1], pown.at[i - 1])])

        def run(i, step):
            return lambda: [getattr(job, step)() for job in sets[i - 1]]

        def fetch(i):
            def go():
                for c in load(fc_all.at[i - 1], proj_all.at[i - 1], i % 2):
                    c.start()
            return go
        run(1, "s1")()
        early = [run(1, "s2"), run(2, "s1")]
        for i in range(1, n_ff):
            last = (i - 1) * n_t
            steps = {last: ["s3"], last + 2: ["s4"], last + 3: ["s5"]}
            if i > 1:
                steps[last - 3] = ["s2"]
            if i > 2:
                steps[last - 5] = ["s1"]
            for when, names in steps.items():
                plan.setdefault(when, []).extend(run(i, s) for s in names)
            plan[last + 3].append(fetch(i))
        for c in load(fc0_h, proj0_h, 0):
            c.start()
    else:
        early = []
        cols = lambda j: pl.ds(j * width, width)
        for i in range(1, n_ff):
            def fetch(i=i):
                for c in load(wfc_h.at[:, cols(FF_ORDER[i])], wproj_h.at[cols(FF_ORDER[i]), :], i % 2):
                    c.start()
            plan[(i - 1) * n_t + 3] = [fetch]
        for c in load(wfc_h.at[:, cols(0)], wproj_h.at[cols(0), :], 0):
            c.start()
    for c in loads[:3]:
        c.wait()

    def out_copy(v, h, r, i):
        return pltpu.make_async_copy(v.at[r, :], h.at[r, :], osem.at[i])

    def forward(t, carry):
        r = tile_at(t)
        h = tok[r, :].astype(F32) + dot(att[r, :], wout[...])
        hidden[r, :] = h
        oacc[r, :] = h
        gacc[r, :] = jnp.zeros_like(h)
        xhat, _ = normalise(h)
        n2[r, :] = (xhat * gain + shift).astype(BF16)
        out_copy(n2, n2_h, r, 3).start()
        return carry
    lax.fori_loop(0, n_t, forward, 0)
    for step in early:
        step()
    loads[3].wait()

    def saves(i, t, slot):
        j = ff_at(i)
        return (pltpu.make_async_copy(act.at[slot], act_h.at[j, tile_at(t), :], asem.at[0, slot]),
                pltpu.make_async_copy(gi.at[slot], gi_h.at[j, tile_at(t), :], asem.at[1, slot]))

    def tile(step, carry):
        i, t, slot = step // n_t, step % n_t, step % 2
        ws = i % 2
        r = tile_at(t)

        @pl.when(t == 0)
        def _():
            for c in load(wfc.at[ws], wproj.at[ws], ws):
                c.wait()

        @pl.when(step >= 2)
        def _():
            for c in saves(i, t, slot):
                c.wait()
        a, g = gelu_both(dot(n2[r, :], wfc[ws]), dot_nt(cot[r, :], wproj[ws]))
        a, g = a.astype(BF16), g.astype(BF16)
        act[slot] = a
        gi[slot] = g
        oacc[r, :] += dot(a, wproj[ws])
        gacc[r, :] += dot_nt(g, wfc[ws])
        for c in saves(i, t, slot):
            c.start()
        for when, steps in plan.items():
            @pl.when(step == when)
            def _():
                for s in steps:
                    s()
        return carry
    lax.fori_loop(0, n_ff * n_t, tile, 0)
    stat_ref[...] = jnp.zeros_like(stat_ref)

    def backward(t, carry):
        r = tile_at(t)
        tok[r, :] = oacc[r, :].astype(BF16)
        xhat, rstd = normalise(hidden[r, :])
        g = gacc[r, :]
        stat_ref[1:2, :] += jnp.sum(g * xhat, axis=0, keepdims=True)
        stat_ref[3:4, :] += jnp.sum(g, axis=0, keepdims=True)
        gh = cot[r, :].astype(F32) + norm_back(g, xhat, rstd, gain)
        hidden[r, :] = gh
        b = gh.astype(BF16)
        gb[r, :] = b
        att[r, :] = dot_nt(b, wout[...]).astype(BF16)
        for i, (v, h) in enumerate([(tok, lout_h), (hidden, ghid_h), (att, gatt_h)]):
            out_copy(v, h, r, i).start()
        out_copy(gb, gb_h, r, 4).start()
        return carry
    lax.fori_loop(0, n_t, backward, 0)
    if remote:
        for pair in sets:
            for job in pair:
                job.drain()
    for slot in range(2):
        for c in saves(0, 0, slot):
            c.wait()
    for i, (v, h) in enumerate([(tok, lout_h), (hidden, ghid_h), (att, gatt_h), (n2, n2_h), (gb, gb_h)]):
        out_copy(v, h, pl.ds(0, n), i).wait()


def mlp(remote, tokens, att, cot, wout, weights, gs):
    n, width = tokens.shape
    s, dma = jax.ShapeDtypeStruct, pltpu.SemaphoreType.DMA
    any_, vm = pl.BlockSpec(memory_space=pl.ANY), pl.BlockSpec(memory_space=pltpu.VMEM)
    big = lambda d: pltpu.VMEM((n, width), d)
    sq = pltpu.VMEM((2, width, width), BF16)
    part = pltpu.VMEM((2, TILE, width), BF16)
    rows = lambda d: s((n, width), d)
    outs = [rows(BF16), rows(F32), rows(BF16), rows(BF16), rows(BF16), s((4, n, width), BF16), s((4, n, width), BF16), s((8, width), F32)]
    out_specs = [any_] * 7 + [vm]
    scratch = [big(BF16), big(BF16), big(BF16), big(F32), big(F32), big(F32), big(BF16), big(BF16), pltpu.VMEM((width, width), BF16),
               sq, sq, part, part, dma((4,)), dma((2, 2)), dma((2, 2)), dma((5,))]
    params = dict(vmem_limit_bytes=VMEM_BYTES)
    if remote:
        n_dev = width // weights[2].shape[0]
        outs += [s((3, width, width), BF16), s((3, 8 * weights[3].shape[0], width), BF16)]
        out_specs += [any_] * 2
        scratch += [dma((3,)), dma((3, n_dev)), dma((3,)), dma((3, 8)), dma((3, 8)), dma((3,))]
        params.update(collective_id=1, has_side_effects=True)
    return pl.pallas_call(
        functools.partial(mlp_kernel, remote), in_specs=[any_] * 6 + ([vm] * 2 if remote else []) + [vm], out_specs=out_specs, out_shape=outs,
        scratch_shapes=scratch, compiler_params=pltpu.CompilerParams(**params), name="mlp",
    )(tokens, att, cot, wout, *weights, gs)[:8]


class Piece:
    def __init__(self, place, parts, total, recv, local, sems):
        self.p, self.parts, self.total, self.sems = place, parts, total, sems
        self.from_core, self.in1, self.in2, self.in3 = recv
        self.out1, self.keep1, self.out2, self.keep2, self.out3 = local

    def hop(self, i, src, dst, to):
        return pltpu.make_async_remote_copy(src_ref=src, dst_ref=dst, send_sem=self.sems.at[0, i], recv_sem=self.sems.at[1, i],
                                            device_id=to, device_id_type=MESH)

    def core(self):
        return self.hop(0, self.parts.at[:, 1 - self.p.c], self.from_core, self.p.partner)

    def h1(self):
        return self.hop(1, self.out1, self.in1, self.p.first2)

    def h2(self):
        return self.hop(2, self.out2, self.in2, self.p.second2)

    def h3(self, k):
        return self.hop(2 + k, self.out3.at[k - 1], self.in3.at[k - 1], self.p.id(z=self.p.z_at(k)))

    def t0(self):
        self.core().start()

    def t1(self):
        p = self.p
        self.core().wait_recv()

        def both(k):
            return self.parts[k, p.c].astype(F32) + self.from_core[k].astype(F32)

        def away(b, carry):
            self.out1[b] = both(p.block(1, b // 4, b % 4)).astype(BF16)
            return carry
        lax.fori_loop(0, 8, away, 0)
        self.h1().start()

        def here(b, carry):
            self.keep1[b] = both(p.block(0, b // 4, b % 4))
            return carry
        lax.fori_loop(0, 8, here, 0)
        self.core().wait_send()

    def t2(self):
        self.h1().wait_recv()

        def away(z, carry):
            self.out2[z] = (self.keep1[4 + z] + self.in1[4 + z].astype(F32)).astype(BF16)
            return carry
        lax.fori_loop(0, 4, away, 0)
        self.h2().start()

        def here(z, carry):
            self.keep2[z] = self.keep1[z] + self.in1[z].astype(F32)
            return carry
        lax.fori_loop(0, 4, here, 0)
        self.h1().wait_send()

    def t3(self):
        p = self.p
        self.h2().wait_recv()
        for k in (2, 1, 3):
            z = p.z_at(k)
            self.out3[k - 1] = (self.keep2[z] + self.in2[z].astype(F32)).astype(BF16)
            self.h3(k).start()
        self.keep2[p.z] = self.keep2[p.z] + self.in2[p.z].astype(F32)
        self.h2().wait_send()

    def t4(self):
        total = self.keep2[self.p.z]
        for k in (1, 3, 2):
            self.h3(k).wait_recv()
            total = total + self.in3[k - 1].astype(F32)
        self.total[...] = total
        for k in (1, 2, 3):
            self.h3(k).wait_send()


class Sum:
    def __init__(self, place, stage, came, sems):
        self.p, self.stage, self.came, self.sems = place, stage, came, sems

    def hop(self, i):
        p = self.p
        to = [p.partner, p.first2, p.second2] + [p.id(z=p.z_at(k)) for k in (1, 2, 3)]
        return pltpu.make_async_remote_copy(src_ref=self.stage.at[min(i, 3)], dst_ref=self.came.at[i], send_sem=self.sems.at[0, i],
                                            recv_sem=self.sems.at[1, i], device_id=to[i], device_id_type=MESH)

    def step(self, i):
        self.hop(i).wait_recv()
        self.stage[i + 1] = self.stage[i] + self.came[i]
        for k in (i + 1,) if i < 2 else (3, 4, 5):
            self.hop(k).start()

    def finish(self):
        for i in (3, 4, 5):
            self.hop(i).wait_recv()
        for i in range(6):
            self.hop(i).wait_send()
        return self.stage[3] + self.came[3] + self.came[4] + self.came[5]


class ReducePlace(Place):
    def __init__(self):
        super().__init__()
        self.first2, self.second2 = self.second, self.first

    def block(self, df, ds, z):
        return self.slot_of(ds, df, z) // 2


N_PROJ = 3
RECV, LOCAL = (16, 8, 4, 3), ((8, BF16), (8, F32), (4, BF16), (4, F32), (3, BF16))
STEPS_A = [(p, p + 1, p + 2, p + 3, p + 4) for p in range(5)] + [(9, 10, 12, 13, 14), (10, 11, 13, 15, 16), (11, 12, 14, 16, 17)]
STEPS_B = [(8, 8, 10, 11, 12), (8, 9, 11, 12, 13), (8, 10, 12, 13, 14)]


def reduce_shapes(width, ff, qkv):
    s, dma = jax.ShapeDtypeStruct, pltpu.SemaphoreType.DMA
    small, tall = width // 32, ff // 32
    outs = [s((small, ff), F32), s((tall, width), F32), s((small, width), F32), s((small, qkv), F32)]
    kinds = ((len(STEPS_A), small, width), (N_PROJ, tall, width // N_PROJ))
    scratch = []
    for n, r, c in kinds:
        scratch += [pltpu.VMEM((n, k, r, c), BF16) for k in RECV] + [pltpu.VMEM((2, k, r, c), d) for k, d in LOCAL]
    scratch += [pltpu.VMEM((4, 8, width), F32), pltpu.VMEM((6, 8, width), F32),
                dma((len(STEPS_A) + N_PROJ, 2, 6)), dma((2, 6))]
    return outs, [pl.BlockSpec(memory_space=pltpu.VMEM)] * 4, scratch


def reduce_plan(plan, gw, gproj, totals, refs):
    fc_t, proj_t, out_t, qkv_t = totals
    bufs, (stage, came, sems, ssem) = (refs[:9], refs[9:18]), refs[18:]
    width = out_t.shape[1]
    place = ReducePlace()
    enter(place)
    units = [0, 1, 2, 3, U_OUT, U_Q, U_Q + 1, U_Q + 2]
    dest = [fc_t.at[:, pl.ds(u * width, width)] for u in range(N_FC)] + [out_t] + [
        qkv_t.at[:, pl.ds(0, width)], qkv_t.at[:, pl.ds(width, width)], qkv_t.at[:, pl.ds(2 * width, qkv_t.shape[1] - 2 * width)]]
    pieces = []
    for i, u in enumerate(units):
        cols = dest[i].shape[1]
        pick = lambda ref, k: ref.at[k] if cols == width else ref.at[k, :, :, pl.ds(0, cols)]
        parts = gw.at[u % 2] if cols == width else gw.at[u % 2, :, :, :, pl.ds(0, cols)]
        pieces.append((STEPS_A[i], Piece(place, parts, dest[i], [pick(b, i) for b in bufs[0][:4]], [pick(b, i % 2) for b in bufs[0][4:]], sems.at[i])))
    part = width // N_PROJ
    for i in range(N_PROJ):
        cols = pl.ds(i * part, part)
        pieces.append((STEPS_B[i], Piece(place, gproj.at[:, :, :, cols], proj_t.at[:, cols], [b.at[i] for b in bufs[1][:4]], [b.at[i % 2] for b in bufs[1][4:]],
                                         sems.at[len(units) + i])))
    todo = [(when, -stage_no, i, piece) for i, (steps, piece) in enumerate(pieces) for stage_no, when in enumerate(steps)]
    todo.sort(key=lambda e: (e[0], e[1] if e[1] else -9, e[2]))
    for when, neg, _, piece in todo:
        plan.setdefault(when, []).append(getattr(piece, "t%d" % -neg))
    sums = Sum(place, stage, came, ssem)

    def late(stat, stat_two, stat_ref):
        stage[0] = stat[...] + stat_two[...]
        sums.hop(0).start()
        rest = [s for when in sorted(w for w in plan if w >= 16) for s in plan[when]]
        between = [lambda: sums.step(0), lambda: sums.step(1), lambda: sums.step(2)]
        while rest or between:
            if rest:
                rest.pop(0)()
            if between:
                between.pop(0)()
        stat_ref[...] = sums.finish()
    return late


N_FC = 4
U_OUT, U_PROJ, U_Q, U_END = 4, 5, 9, 12


def grads_kernel(remote, tok_h, ghid_h, gq_h, gk_h, gv_h, w_h, act_h, gi_h, n2_h, cot_h, att_h, gb_h, gs_ref, stat_two, *refs):
    if remote:
        (gtok_h, gskip_h, fc_t, proj_t, out_t, qkv_t, stat_ref), refs = refs[:7], refs[7:]
    else:
        (gtok_h, gskip_h, gfc_h, gproj_h, gout_h, gqkv_h, stat_ref), refs = refs[:7], refs[7:]
    (pool, gw, gproj, w, ghid, gskip, stat, insem, tsem, osem, gsem), refs = refs[:11], refs[11:]
    n, width = pool.shape[1:]
    half = gskip.shape[2]
    n_t = n // TILE
    n_dev = 2 * gw.shape[1]
    gain, shift = gs_ref[0:1, :], gs_ref[2:3, :]

    def load(src, i):
        return pltpu.make_async_copy(src, pool.at[i], insem.at[i])

    def loaded(i):
        load(pool.at[i], i).wait()
    wload = pltpu.make_async_copy(w_h, w, insem.at[6])
    load(n2_h, 0).start()
    load(gi_h.at[0], 1).start()
    load(gi_h.at[1], 2).start()
    load(att_h, 3).start()
    load(gb_h, 4).start()
    load(tok_h, 5).start()
    wload.start()
    plan = {}
    if remote:
        late = reduce_plan(plan, gw, gproj, (fc_t, proj_t, out_t, qkv_t), refs)
    loaded(0)

    def normalised():
        loaded(5)

        def tile(t, carry):
            r = tile_at(t)
            xhat, _ = normalise(pool[5, r, :].astype(F32))
            pool[3, r, :] = (xhat * gain + shift).astype(BF16)
            return carry
        lax.fori_loop(0, n_t, tile, 0)

    def put(u, slot):
        return [pltpu.make_async_copy(gw.at[slot, k // 2, k % 2], u(k), gsem.at[slot]) for k in range(n_dev)]

    def unit(u, carry):
        slot = u % 2
        ring = 1 + jnp.where(u < U_OUT, u, u - U_PROJ) % 2
        proj = (u >= U_PROJ) & (u < U_Q)
        lhs = jnp.where(u < U_OUT, 0, jnp.where(proj, ring, 3))
        rhs = jnp.where(u < U_OUT, ring, jnp.where((u == U_OUT) | (u == U_Q), 4, jnp.where(proj | (u == U_Q + 1), 0, 2)))

        @pl.when((u < U_OUT) | proj)
        def _():
            loaded(ring)

        for when, bufs in {U_OUT: (3, 4), U_PROJ: (0,), U_Q: (4,), U_Q + 1: (0,), U_Q + 2: (2,)}.items():
            @pl.when(u == when)
            def _():
                for b in bufs:
                    loaded(b)

        def rows(m, carry):
            c = pl.ds(pl.multiple_of(m * 384, 128), 384)
            g = dot_tn(pool[lhs, :, c], pool[rhs])

            @pl.when(proj)
            def _():
                gproj[pl.ds((u - U_PROJ) * 4 + m * 2, 2)] = g.reshape(2, 2, 96, width).astype(BF16)

            @pl.when(jnp.logical_not(proj))
            def _():
                gw[slot, pl.ds(m * 8, 8)] = g.reshape(8, 2, 24, width).astype(BF16)
            return carry
        lax.fori_loop(0, 2, rows, 0)
        after = {0: [load(gi_h.at[2], 1).start], 1: [load(gi_h.at[3], 2).start], 2: [load(act_h.at[0], 1).start],
                 3: [load(act_h.at[1], 2).start, load(cot_h, 0).start], U_OUT: [load(gq_h, 4).start, normalised],
                 5: [load(act_h.at[2], 1).start], 6: [load(act_h.at[3], 2).start],
                 8: [load(gk_h, 0).start, load(gv_h, 2).start]}
        for when in range(U_END):
            steps = after.get(when, []) + plan.get(when, [])
            if steps:
                @pl.when(u == when)
                def _():
                    for s in steps:
                        s()
        return carry

    if not remote:
        width_v = w.shape[1] - 2 * width
        row = lambda k: pl.ds(k * 24, 24)
        dest = {u: (lambda k, u=u: gfc_h.at[row(k), pl.ds(u * width, width)]) for u in range(N_FC)}
        dest[U_OUT] = lambda k: gout_h.at[row(k), :]
        dest[U_Q] = lambda k: gqkv_h.at[row(k), pl.ds(0, width)]
        dest[U_Q + 1] = lambda k: gqkv_h.at[row(k), pl.ds(width, width)]
        def emit(u):
            def go():
                if u == U_Q + 2:
                    cs = [pltpu.make_async_copy(gw.at[u % 2, k // 2, k % 2, :, pl.ds(0, width_v)], gqkv_h.at[row(k), pl.ds(2 * width, width_v)], gsem.at[u % 2]) for k in range(n_dev)]
                else:
                    cs = put(dest[u], u % 2)
                for c in cs:
                    c.start()
                for c in cs:
                    c.wait()
            return go
        for u in list(dest) + [U_Q + 2]:
            plan[u] = [emit(u)]

        def emit_proj():
            cs = [pltpu.make_async_copy(gproj.at[k // 2, k % 2], gproj_h.at[pl.ds(k * 96, 96), :], gsem.at[0]) for k in range(n_dev)]
            for c in cs:
                c.start()
            for c in cs:
                c.wait()
        plan[U_Q - 1] = [emit_proj]
    lax.fori_loop(0, U_END, unit, 0)
    wload.wait()
    stat[...] = jnp.zeros_like(stat)

    def gin(t):
        return pltpu.make_async_copy(ghid_h.at[tile_at(t), :], ghid.at[t % 2], tsem.at[t % 2])

    def gout(t):
        return (pltpu.make_async_copy(ghid.at[t % 2], gtok_h.at[tile_at(t), :], osem.at[0, t % 2]),
                pltpu.make_async_copy(gskip.at[t % 2], gskip_h.at[tile_at(t), :], osem.at[1, t % 2]))

    gin(0).start()

    def tile(t, carry):
        r, slot = tile_at(t), t % 2
        g = (dot_nt(pool[4, r, :], w[:, :width]) + dot_nt(pool[0, r, :], w[:, width:2 * width])
             + dot_nt(pool[2, r, :half], w[:, 2 * width:]))
        gin(t).wait()

        @pl.when(t > 0)
        def _():
            for c in gout(t - 1):
                c.wait()

        @pl.when(t + 1 < n_t)
        def _():
            gin(t + 1).start()
        xhat, rstd = normalise(pool[5, r, :].astype(F32))
        gskip[slot] = pool[2, r, half:].astype(F32)
        stat[0:1, :] += jnp.sum(g * xhat, axis=0, keepdims=True)
        stat[2:3, :] += jnp.sum(g, axis=0, keepdims=True)
        ghid[slot] += norm_back(g, xhat, rstd, gain)
        for c in gout(t):
            c.start()
        if remote:
            for when in range(n_t):
                @pl.when(t == when)
                def _():
                    for s in plan.get(U_END + when, []):
                        s()
        return carry
    lax.fori_loop(0, n_t, tile, 0)
    if remote:
        late(stat, stat_two, stat_ref)
    else:
        stat_ref[...] = stat[...] + stat_two[...]
    for c in gout(n_t - 1):
        c.wait()


def grads(remote, tokens, ghid, gq, gk, gv, w, act, gi, n2, cot, att, gb, gs, stat):
    n, width = tokens.shape
    half = 2 * width - (w.shape[1] - width)
    ff = act.shape[0] * width
    s, dma = jax.ShapeDtypeStruct, pltpu.SemaphoreType.DMA
    any_, vm = pl.BlockSpec(memory_space=pl.ANY), pl.BlockSpec(memory_space=pltpu.VMEM)
    outs = [s((n, width), F32), s((n, half), F32)]
    scratch = [pltpu.VMEM((6, n, width), BF16), pltpu.VMEM((2, 16, 2, width // 32, width), BF16), pltpu.VMEM((16, 2, ff // 32, width), BF16),
               pltpu.VMEM(w.shape, BF16), pltpu.VMEM((2, TILE, width), F32), pltpu.VMEM((2, TILE, half), F32), pltpu.VMEM((8, width), F32),
               dma((7,)), dma((2,)), dma((2, 2)), dma((2,))]
    params = dict(vmem_limit_bytes=VMEM_BYTES)
    if remote:
        more, specs, extra = reduce_shapes(width, ff, w.shape[1])
        scratch += extra
        params.update(collective_id=2, has_side_effects=True)
    else:
        more = [s((width, ff), BF16), s((ff, width), BF16), s((width, width), BF16), s(w.shape, BF16)]
        specs = [any_] * 4
    return pl.pallas_call(
        functools.partial(grads_kernel, remote), in_specs=[any_] * 12 + [vm] * 2, out_specs=[any_] * 2 + specs + [vm],
        out_shape=outs + more + [s((8, width), F32)], scratch_shapes=scratch,
        compiler_params=pltpu.CompilerParams(**params), name="grads",
    )(tokens, ghid, gq, gk, gv, w, act, gi, n2, cot, att, gb, gs, stat)


AXES = ("dp", "fsdp")


def body(direct, tokens, skip_values, w_qkv, w_out, w_fc, w_proj, norm_gains, norm_shifts, segment_ids, pad_mask, cotangent):
    micro, rows, length, width = tokens.shape
    half, ff = skip_values.shape[3], w_fc.shape[1]
    seqs = micro * rows
    n = seqs * length
    n_dev, own = width // norm_gains.shape[1], norm_gains.shape[1]
    slot = lax.axis_index(AXES)
    flat = lambda a: a.reshape(n, a.shape[-1])
    seq = lambda a: a.reshape(seqs, length, a.shape[-1])
    tok, skip, cot = flat(tokens), flat(skip_values), flat(cotangent)
    seg, pad = segment_ids.reshape(seqs, length), pad_mask.reshape(seqs, length)
    rows8 = jnp.concatenate([norm_gains, norm_shifts, jnp.zeros((4, own), BF16)], axis=0)
    if direct:
        place = lax.dynamic_update_slice(jnp.zeros((8, width), BF16), rows8, (0, slot * own))
        q, k, v, gs, _, qkv, out, fc0, proj0 = start(tok, skip, place, w_qkv, w_out, w_fc, w_proj)
        weights = (fc0, proj0, w_fc, w_proj)
    else:
        qkv, out, *weights = [lax.all_gather(w, AXES, axis=0, tiled=True) for w in (w_qkv, w_out, w_fc, w_proj)]
        gs = lax.all_gather(rows8, AXES, axis=1, tiled=True).astype(F32)
        q, k, v = project(tok, skip, qkv, gs)
    att, lse = attend(seq(q), seq(k), seq(v), seg, pad)
    att = flat(att)
    lout, ghid, gatt, n2, gb, act, gi, stat = mlp(direct, tok, att, cot, out, weights, gs)
    gq, gk, gv = attend_back(seq(q), seq(k), seq(v), seq(gatt), lse, seg, pad)
    gtok, gskip, gfc, gproj, gout, gqkv, stat = grads(
        direct, tok, ghid, flat(gq), flat(gk), flat(gv), qkv, act, gi, n2, cot, att, gb, gs, stat)
    if direct:
        total_fc, total_proj, total_out, total_qkv = gfc, gproj, gout, gqkv
        sums = lax.dynamic_slice(stat, (0, slot * own), (8, own))
        gains, shifts = sums[0:2], sums[2:4]
    else:
        total_qkv, total_out, total_fc, total_proj = [
            lax.psum_scatter(g.astype(F32), AXES, scatter_dimension=0, tiled=True) for g in (gqkv, gout, gfc, gproj)]
        gains = lax.psum_scatter(stat[0:2], AXES, scatter_dimension=1, tiled=True)
        shifts = lax.psum_scatter(stat[2:4], AXES, scatter_dimension=1, tiled=True)
    shape4 = lambda a: a.reshape(micro, rows, length, a.shape[-1])
    return (shape4(lout), shape4(gtok), shape4(gskip), total_qkv, total_out, total_fc, total_proj, gains, shifts)


def solution(mesh):
    tok, mat, row, ids = P(None, AXES, None, None), P(AXES, None), P(None, AXES), P(None, AXES, None)
    direct = dict(mesh.shape) == {"dp": 2, "fsdp": 16}
    return jax.shard_map(
        functools.partial(body, direct), mesh=mesh,
        in_specs=(tok, tok, mat, mat, mat, mat, row, row, ids, ids, tok),
        out_specs=(tok, tok, tok, mat, mat, mat, mat, row, row), check_vma=False)
```

```python
import functools
import jax
import jax.numpy as jnp
from jax import lax
from jax.experimental import pallas as pl
from jax.experimental.pallas import tpu as pltpu
from jax.sharding import PartitionSpec as P

F32, BF16 = jnp.float32, jnp.bfloat16

HEAD = 64
BLK = 128
WIN = 5
MASKED = -1e9
PAIRS_FWD, PAIRS_BWD = 6, 6


def build_bias(seg_row, pad_row, bias_ref, n_blk):
    code = jnp.where(pad_row == 1, seg_row, -1)
    key = lax.broadcasted_iota(jnp.int32, (BLK, BLK), 0)
    row = lax.broadcasted_iota(jnp.int32, (BLK, BLK), 1)
    for kb in range(n_blk):
        code_k = jnp.broadcast_to(code[:, kb * BLK:(kb + 1) * BLK], (BLK, BLK)).T
        for qb in range(kb, min(kb + WIN, n_blk)):
            vis = code_k == seg_row[:, qb * BLK:(qb + 1) * BLK]
            if kb == qb:
                vis = (vis & (key < row)) | (key == row)
            t = kb - qb + WIN - 1
            bias_ref[qb, t * BLK:(t + 1) * BLK, :] = jnp.where(vis, 0.0, MASKED)


def stack_heads(x):
    low = lax.broadcasted_iota(jnp.int32, x.shape, 1) < HEAD
    zero = jnp.zeros_like(x)
    return jnp.concatenate([jnp.where(low, x, zero), jnp.where(low, zero, x)], axis=0)


def join_heads(x2):
    return jnp.concatenate([x2[:HEAD, :BLK], x2[HEAD:, BLK:]], axis=0)


def twice(x):
    return jnp.concatenate([x, x], axis=1)


def visible_blocks(seg_s, row, qb):
    first = seg_s[row, qb * BLK]
    n = jnp.int32(1)
    for back in range(1, WIN):
        kb = jnp.maximum(qb - back, 0)
        seen = (qb >= back) & (seg_s[row, kb * BLK + BLK - 1] == first)
        n = n + seen.astype(jnp.int32)
    return n


def over_queries(seg_s, row, n_blk, one):
    def step(qb, carry):
        n_vis = visible_blocks(seg_s, row, qb)
        for n in range(1, WIN + 1):
            @pl.when(n_vis == n)
            def _():
                one(n, qb)
        return carry
    lax.fori_loop(0, n_blk, step, 0)


def block(i, n=1):
    return pl.ds(pl.multiple_of(i * BLK, BLK), n * BLK)


def attend_nt(a, b):
    return lax.dot_general(a, b, (((1,), (1,)), ((), ())), preferred_element_type=F32)


def fwd_kernel(n_blk, pairs, seg_s, seg_ref, pad_ref, q_ref, k_ref, v_ref, o_ref, lse_ref, bias_ref, vt_ref):
    row = pl.program_id(0)

    @pl.when(pl.program_id(1) == 0)
    def _():
        build_bias(seg_ref[...], pad_ref[...], bias_ref, n_blk)

    lanes = [slice(i * BLK, (i + 1) * BLK) for i in range(pairs)]
    for kb in range(n_blk):
        for h in lanes:
            vt_ref[h, kb * BLK:(kb + 1) * BLK] = v_ref[kb * BLK:(kb + 1) * BLK, h].T

    def one(n, qb):
        keys, here = block(qb - n + 1, n), block(qb)
        b = twice(bias_ref[qb, (WIN - n) * BLK:, :])
        s = [attend_nt(k_ref[keys, h], stack_heads(q_ref[here, h])) + b for h in lanes]
        for i, h in enumerate(lanes):
            m = jnp.max(s[i], axis=0, keepdims=True)
            p = jnp.exp(s[i] - m)
            total = jnp.sum(p, axis=0, keepdims=True)
            o2 = jnp.dot(vt_ref[h, keys], p.astype(BF16), preferred_element_type=F32) * (1.0 / total)
            o_ref[here, h] = join_heads(o2).astype(BF16).T
            lse_ref[i, qb] = m + jnp.log(total)
    over_queries(seg_s, row, n_blk, one)


def attend(q, k, v, seg, pad):
    rows, length, width = q.shape
    n_blk, pairs = length // BLK, PAIRS_FWD
    groups = width // 128 // pairs
    tok = pl.BlockSpec((None, length, pairs * 128), lambda r, h, s: (r, 0, h))
    ids = pl.BlockSpec((None, 1, length), lambda r, h, s: (r, 0, 0))
    return pl.pallas_call(
        functools.partial(fwd_kernel, n_blk, pairs),
        grid_spec=pltpu.PrefetchScalarGridSpec(
            num_scalar_prefetch=1, grid=(rows, groups),
            in_specs=[ids, ids, tok, tok, tok],
            out_specs=[tok, pl.BlockSpec((None, pairs, n_blk, 1, 2 * BLK), lambda r, h, s: (r, h, 0, 0, 0))],
            scratch_shapes=[pltpu.VMEM((n_blk, WIN * BLK, BLK), F32), pltpu.VMEM((pairs * BLK, length), BF16)]),
        out_shape=[jax.ShapeDtypeStruct((rows, length, width), BF16), jax.ShapeDtypeStruct((rows, width // 128, n_blk, 1, 2 * BLK), F32)],
        compiler_params=pltpu.CompilerParams(dimension_semantics=("arbitrary", "arbitrary"), vmem_limit_bytes=64000 << 10),
        name="attend",
    )(seg, seg[:, None, :], pad[:, None, :], q, k, v)


def bwd_kernel(n_blk, pairs, seg_s, seg_ref, pad_ref, q_ref, k_ref, v_ref, g_ref, lse_ref, dq_ref, dk_ref, dv_ref,
               bias_ref, kt_ref, dk_acc, dv_acc):
    row = pl.program_id(0)

    @pl.when(pl.program_id(1) == 0)
    def _():
        build_bias(seg_ref[...], pad_ref[...], bias_ref, n_blk)

    lanes = [slice(i * BLK, (i + 1) * BLK) for i in range(pairs)]
    for kb in range(n_blk):
        for h in lanes:
            kt_ref[h, kb * BLK:(kb + 1) * BLK] = k_ref[kb * BLK:(kb + 1) * BLK, h].T
    dk_acc[...] = jnp.zeros_like(dk_acc)
    dv_acc[...] = jnp.zeros_like(dv_acc)

    def one(n, qb):
        keys, here = block(qb - n + 1, n), block(qb)
        b = twice(bias_ref[qb, (WIN - n) * BLK:, :])
        for i, h in enumerate(lanes):
            q2, g2 = stack_heads(q_ref[here, h]), stack_heads(g_ref[here, h])
            p = jnp.exp(attend_nt(k_ref[keys, h], q2) + b - lse_ref[i, qb])
            dp = attend_nt(v_ref[keys, h], g2)
            inner = jnp.sum(p * dp, axis=0, keepdims=True)
            ds = (p * (dp - inner)).astype(BF16)
            dv_acc[keys, h] += jnp.dot(p.astype(BF16), g2, preferred_element_type=F32)
            dk_acc[keys, h] += jnp.dot(ds, q2, preferred_element_type=F32)
            dq2 = jnp.dot(kt_ref[h, keys], ds, preferred_element_type=F32)
            dq_ref[here, h] = (join_heads(dq2) * 0.125).astype(BF16).T
    over_queries(seg_s, row, n_blk, one)
    dk_ref[...] = dk_acc[...].astype(BF16)
    dv_ref[...] = dv_acc[...].astype(BF16)


def attend_back(q, k, v, g, lse, seg, pad):
    rows, length, width = q.shape
    n_blk, pairs = length // BLK, PAIRS_BWD
    groups = width // 128 // pairs
    tok = pl.BlockSpec((None, length, pairs * 128), lambda r, h, s: (r, 0, h))
    ids = pl.BlockSpec((None, 1, length), lambda r, h, s: (r, 0, 0))
    out = jax.ShapeDtypeStruct((rows, length, width), BF16)
    return pl.pallas_call(
        functools.partial(bwd_kernel, n_blk, pairs),
        grid_spec=pltpu.PrefetchScalarGridSpec(
            num_scalar_prefetch=1, grid=(rows, groups),
            in_specs=[ids, ids, tok, tok, tok, tok, pl.BlockSpec((None, pairs, n_blk, 1, 2 * BLK), lambda r, h, s: (r, h, 0, 0, 0))],
            out_specs=[tok, tok, tok],
            scratch_shapes=[pltpu.VMEM((n_blk, WIN * BLK, BLK), F32), pltpu.VMEM((pairs * BLK, length), BF16),
                            pltpu.VMEM((length, pairs * BLK), F32), pltpu.VMEM((length, pairs * BLK), F32)]),
        out_shape=[out, out, out],
        compiler_params=pltpu.CompilerParams(dimension_semantics=("arbitrary", "arbitrary"), vmem_limit_bytes=64000 << 10),
        name="attend_back",
    )(seg, seg[:, None, :], pad[:, None, :], q, k, v, g, lse)


MESH = pl.DeviceIdType.MESH
NZ = 4


class Place:
    def __init__(self):
        dp, fs = lax.axis_index("dp"), lax.axis_index("fsdp")
        self.x, self.z, self.y, self.c = dp, fs // 4, (fs // 2) % 2, fs % 2
        self.slot = self.x * 16 + fs
        self.first = self.id(x=jnp.where(self.c == 0, 1 - self.x, self.x), y=jnp.where(self.c == 0, self.y, 1 - self.y))
        self.second = self.id(x=jnp.where(self.c == 0, self.x, 1 - self.x), y=jnp.where(self.c == 0, 1 - self.y, self.y))
        self.partner = self.id(c=1 - self.c)

    def id(self, x=None, y=None, z=None, c=None):
        x = self.x if x is None else x
        y = self.y if y is None else y
        z = self.z if z is None else z
        c = self.c if c is None else c
        return (x, z * 4 + y * 2 + c)

    def z_at(self, k):
        return (self.z + k) % NZ

    def peers(self):
        return [self.partner, self.first, self.second] + [self.id(z=self.z_at(k)) for k in (1, 2, 3)]

    def slot_of(self, df, ds, z):
        dx = jnp.where(self.c == 0, df, ds)
        dy = jnp.where(self.c == 0, ds, df)
        x = jnp.where(dx == 1, 1 - self.x, self.x)
        y = jnp.where(dy == 1, 1 - self.y, self.y)
        return x * 16 + z * 4 + y * 2 + self.c


def enter(place):
    bar = pltpu.get_barrier_semaphore()
    for peer in place.peers():
        pl.semaphore_signal(bar, inc=1, device_id=peer, device_id_type=MESH)
    pl.semaphore_wait(bar, 6)


class Gather:
    SENDS = 31

    def __init__(self, place, shard, out, send, recv, own):
        self.p, self.shard, self.out, self.send, self.recv, self.own = place, shard, out, send, recv, own
        self.size = shard.shape[0]

    def at(self, slot, n=1):
        return self.out.at[pl.ds(pl.multiple_of(slot * self.size, 8), n * self.size), :]

    def push(self, src, slot, to):
        pltpu.make_async_remote_copy(src_ref=src, dst_ref=self.at(slot), send_sem=self.send, recv_sem=self.recv.at[slot],
                                     device_id=to, device_id_type=MESH).start()

    def arrived(self, slot):
        pltpu.make_async_copy(self.at(slot), self.at(slot), self.recv.at[slot]).wait()

    def keep(self, slot):
        return pltpu.make_async_copy(self.shard, self.at(slot), self.own)

    def s1(self):
        p = self.p
        self.keep(p.slot).start()
        for k in (1, 3, 2):
            self.push(self.shard, p.slot, p.id(z=p.z_at(k)))
        for to in (p.first, p.partner, p.second):
            self.push(self.shard, p.slot, to)

    def s2(self):
        p = self.p
        for k in (1, 3, 2):
            slot = p.slot_of(0, 0, p.z_at(k))
            self.arrived(slot)
            for to in (p.first, p.second, p.partner):
                self.push(self.at(slot), slot, to)

    def s3(self):
        p = self.p
        for k in (0, 1, 3, 2):
            slot = p.slot_of(1, 0, p.z_at(k))
            self.arrived(slot)
            for to in (p.second, p.partner):
                self.push(self.at(slot), slot, to)

    def s4(self):
        p = self.p
        for df in (0, 1):
            for k in (0, 1, 3, 2):
                slot = p.slot_of(df, 1, p.z_at(k))
                self.arrived(slot)
                self.push(self.at(slot), slot, p.partner)

    def s5(self):
        for k in range(16):
            self.arrived(2 * k + 1 - self.p.c)
        self.keep(self.p.slot).wait()

    def drain(self):
        done = self.at(0, self.SENDS)
        pltpu.make_async_copy(done, done, self.send).wait()


VMEM_BYTES = 64000 << 10
TILE = 512
EPS = 1e-5
GELU_C = 0.7978845608028654
GELU_A = 0.044715


def dot(a, b):
    return jnp.dot(a, b, preferred_element_type=F32)


def dot_nt(a, b):
    return lax.dot_general(a, b, (((1,), (1,)), ((), ())), preferred_element_type=F32)


def dot_tn(a, b):
    return lax.dot_general(a, b, (((0,), (0,)), ((), ())), preferred_element_type=F32)


def normalise(v):
    centred = v - jnp.mean(v, axis=-1, keepdims=True)
    rstd = lax.rsqrt(jnp.mean(centred * centred, axis=-1, keepdims=True) + EPS)
    return centred * rstd, rstd


def norm_back(g, xhat, rstd, gain):
    gh = g * gain
    return rstd * (gh - jnp.mean(gh, axis=-1, keepdims=True) - xhat * jnp.mean(gh * xhat, axis=-1, keepdims=True))


def gelu_both(u, grad):
    sq = u * u
    t = jnp.tanh(u * (GELU_C + (GELU_C * GELU_A) * sq))
    half = 0.5 + 0.5 * t
    act = u * half
    slope = half + act * (1.0 - half) * (2.0 * GELU_C + (6.0 * GELU_C * GELU_A) * sq)
    return act, grad * slope


def tile_at(t):
    return pl.ds(pl.multiple_of(t * TILE, TILE), TILE)


def qkv_kernel(tok_ref, skip_ref, w_ref, gs_ref, q_ref, k_ref, v_ref):
    width, half = tok_ref.shape[1], skip_ref.shape[1]
    xhat, _ = normalise(tok_ref[...].astype(F32))
    normed = (xhat * gs_ref[0:1, :] + gs_ref[2:3, :]).astype(BF16)
    q_ref[...] = (dot(normed, w_ref[:, :width]) * 0.125).astype(BF16)
    k_ref[...] = dot(normed, w_ref[:, width:2 * width]).astype(BF16)
    v_ref[:, :half] = dot(normed, w_ref[:, 2 * width:]).astype(BF16)
    v_ref[:, half:] = skip_ref[...]


def project(tokens, skip, w, gs):
    n, width = tokens.shape
    row = lambda c: pl.BlockSpec((TILE, c), lambda t: (t, 0))
    whole = lambda a: pl.BlockSpec(a.shape, lambda t: (0, 0))
    out = jax.ShapeDtypeStruct((n, width), BF16)
    return pl.pallas_call(
        qkv_kernel, grid=(n // TILE,), in_specs=[row(width), row(skip.shape[1]), whole(w), whole(gs)],
        out_specs=[row(width)] * 3, out_shape=[out] * 3,
        compiler_params=pltpu.CompilerParams(vmem_limit_bytes=VMEM_BYTES), name="project",
    )(tokens, skip, w, gs)


def lane_mod(x, period):
    return lax.rem(lax.broadcasted_iota(jnp.int32, x.shape, 1), jnp.int32(period))


def gather_groups(x, groups, size, parts):
    out = []
    total = x.shape[1]
    for j in range(parts):
        y = pltpu.roll(x, total - j * size, 1) if j else x
        span = size
        while span < groups * size:
            m = lane_mod(y, 2 * parts * span)
            y = jnp.where((m >= span) & (m < 2 * span), pltpu.roll(y, total - (parts - 1) * span, 1), y)
            span *= 2
        out.append(y[:, :groups * size])
    return out


def spread_groups(pieces, groups, size):
    parts = len(pieces)
    out = None
    for j, piece in enumerate(pieces):
        y = jnp.concatenate([piece] + [jnp.zeros_like(piece)] * (parts - 1), axis=1)
        span = groups * size
        while span > size:
            span //= 2
            m = lane_mod(y, 2 * parts * span)
            y = jnp.where((m >= parts * span) & (m < (parts + 1) * span), pltpu.roll(y, (parts - 1) * span, 1), y)
        y = pltpu.roll(y, j * size, 1) if j else y
        m = lane_mod(y, parts * size)
        y = jnp.where((m >= j * size) & (m < (j + 1) * size), y, 0.0)
        out = y if out is None else out + y
    return out


N_FF = 4


def start_kernel(tok_h, skip_h, rows_ref, qkv_ref, out_ref, fc_ref, proj_h,
                 q_h, k_h, v_h, gs_ref, fcp_ref, gs_all, qkv_all, out_all, fc_all, proj_all,
                 tok, skip, xhat, w, gsb, q, k, v, insem, osem, send, recv, own):
    n, width = tok.shape
    half = skip.shape[1]
    n_t = n // TILE
    n_dev = qkv_all.shape[0] // qkv_ref.shape[0]
    size = proj_h.shape[0] // N_FF
    place = Place()
    loads = [pltpu.make_async_copy(tok_h, tok, insem.at[0]), pltpu.make_async_copy(skip_h, skip, insem.at[1])]
    for c in loads:
        c.start()
    enter(place)
    shards = (rows_ref, qkv_ref, out_ref, fcp_ref.at[0], proj_h.at[pl.ds(0, size), :])
    outs = (gs_all, qkv_all, out_all, fc_all, proj_all)
    jobs = [Gather(place, s, o, send.at[i], recv.at[i], own.at[i]) for i, (s, o) in enumerate(zip(shards, outs))]
    rows, qkv, out, fc, proj = jobs
    rows.s1(), qkv.s1()
    for j, piece in enumerate(gather_groups(fc_ref[...].astype(F32), n_dev, size, N_FF)):
        fcp_ref[j] = piece.astype(BF16)
    for c in loads:
        c.wait()

    def centre(t, carry):
        r = tile_at(t)
        xhat[r, :], _ = normalise(tok[r, :].astype(F32))
        return carry
    lax.fori_loop(0, n_t // 2, centre, 0)
    rows.s2(), qkv.s2(), out.s1()
    lax.fori_loop(n_t // 2, n_t, centre, 0)
    rows.s3(), qkv.s3(), fc.s1(), proj.s1()
    out.s2(), rows.s4(), qkv.s4(), fc.s2(), proj.s2(), rows.s5(), qkv.s5()
    wload = pltpu.make_async_copy(qkv_all, w, insem.at[2])
    gload = pltpu.make_async_copy(gs_all, gsb, insem.at[3])
    wload.start(), gload.start()
    out.s3(), fc.s3()
    gload.wait()
    gs_ref[...] = jnp.sum(gsb[...].astype(F32).reshape(n_dev, 8, width), axis=0)
    wload.wait()

    def copies(r):
        return [pltpu.make_async_copy(s.at[r, :], h.at[r, :], osem.at[i]) for i, (s, h) in enumerate([(q, q_h), (k, k_h), (v, v_h)])]

    plan = {0: [proj.s3, out.s4], 1: [fc.s4], 2: [out.s5, proj.s4], 3: [fc.s5, proj.s5]}

    def tile(t, carry):
        r = tile_at(t)
        normed = (xhat[r, :] * gs_ref[0:1, :] + gs_ref[2:3, :]).astype(BF16)
        q[r, :] = (dot(normed, w[:, :width]) * 0.125).astype(BF16)
        k[r, :] = dot(normed, w[:, width:2 * width]).astype(BF16)
        v[r, :half] = dot(normed, w[:, 2 * width:]).astype(BF16)
        v[r, half:] = skip[r, :]
        for c in copies(r):
            c.start()
        for when, steps in plan.items():
            @pl.when(t == when)
            def _():
                for s in steps:
                    s()
        return carry
    lax.fori_loop(0, n_t, tile, 0)
    for job in jobs:
        job.drain()
    for c in copies(pl.ds(0, n)):
        c.wait()


def start(tokens, skip, rows, qkv, out, fc, proj):
    n, width = tokens.shape
    n_dev = width // out.shape[0]
    s, dma = jax.ShapeDtypeStruct, pltpu.SemaphoreType.DMA
    any_, vm = pl.BlockSpec(memory_space=pl.ANY), pl.BlockSpec(memory_space=pltpu.VMEM)
    big = lambda d: pltpu.VMEM((n, width), d)
    act = s((n, width), BF16)
    gathered = [(8 * n_dev, width), (width, qkv.shape[1]), (width, width), (width, width), (width, width)]
    return pl.pallas_call(
        start_kernel, in_specs=[any_, any_] + [vm] * 4 + [any_], out_specs=[any_] * 3 + [vm] * 2 + [any_] * 5,
        out_shape=[act] * 3 + [s((8, width), F32), s((N_FF, fc.shape[0], width), BF16)] + [s(g, BF16) for g in gathered],
        scratch_shapes=[big(BF16), pltpu.VMEM(skip.shape, BF16), big(F32), pltpu.VMEM((width, qkv.shape[1]), BF16), pltpu.VMEM((8 * n_dev, width), BF16),
                        big(BF16), big(BF16), big(BF16), dma((4,)), dma((3,)), dma((5,)), dma((5, n_dev)), dma((5,))],
        compiler_params=pltpu.CompilerParams(vmem_limit_bytes=VMEM_BYTES, collective_id=0, has_side_effects=True), name="start",
    )(tokens, skip, rows, qkv, out, fc, proj)


MLP_STEPS = {1: (-1, 0, 1, 2), 2: (0, 2, 4, 6), 3: (2, 4, 6, 8)}


def mlp_kernel(remote, tok_h, att_h, cot_h, wout_h, *refs):
    if remote:
        fc0_h, proj0_h, fcp_ref, proj_ref, *refs = refs
    else:
        wfc_h, wproj_h, *refs = refs
    (gs_ref, lout_h, ghid_h, gatt_h, n2_h, gb_h, act_h, gi_h, stat_ref), refs = refs[:9], refs[9:]
    if remote:
        (fc_all, proj_all), refs = refs[:2], refs[2:]
    (tok, att, cot, hidden, oacc, gacc, n2, gb, wout, wfc, wproj, act, gi, insem, wsem, asem, osem), sems = refs[:17], refs[17:]
    n, width = tok.shape
    n_ff = N_FF
    n_t = n // TILE
    gain, shift = gs_ref[1:2, :], gs_ref[3:4, :]

    def load(src_fc, src_proj, slot):
        return (pltpu.make_async_copy(src_fc, wfc.at[slot], wsem.at[0, slot]), pltpu.make_async_copy(src_proj, wproj.at[slot], wsem.at[1, slot]))

    loads = [pltpu.make_async_copy(h, v, insem.at[i]) for i, (h, v) in enumerate([(wout_h, wout), (att_h, att), (tok_h, tok), (cot_h, cot)])]
    for c in loads:
        c.start()
    plan = {}
    if remote:
        send, recv, own = sems
        place = Place()
        enter(place)
        size = proj_ref.shape[0] // n_ff
        sets = []
        for i in range(1, n_ff):
            srcs = (fcp_ref.at[i], proj_ref.at[pl.ds(i * size, size), :])
            sets.append([Gather(place, srcs[k], (fc_all, proj_all)[k].at[i - 1], send.at[i - 1, k], recv.at[i - 1, k], own.at[i - 1, k]) for k in range(2)])

        def run(i, step):
            return lambda: [getattr(job, step)() for job in sets[i - 1]]

        def fetch(i):
            def go():
                for c in load(fc_all.at[i - 1], proj_all.at[i - 1], i % 2):
                    c.start()
            return go
        for i in range(1, n_ff):
            run(i, "s1")()
        early = []
        for i, steps in MLP_STEPS.items():
            for when, name in zip(steps, ("s2", "s3", "s4", "s5")):
                (early if when < 0 else plan.setdefault(when, [])).append(run(i, name))
            plan[steps[3]].append(fetch(i))
        for c in load(fc0_h, proj0_h, 0):
            c.start()
    else:
        early = []
        cols = lambda j: pl.ds(j * width, width)
        for i in range(1, n_ff):
            def fetch(i=i):
                for c in load(wfc_h.at[:, cols(i)], wproj_h.at[cols(i), :], i % 2):
                    c.start()
            plan[(i - 1) * n_t + 3] = [fetch]
        for c in load(wfc_h.at[:, cols(0)], wproj_h.at[cols(0), :], 0):
            c.start()
    for c in loads[:3]:
        c.wait()

    def out_copy(v, h, r, i):
        return pltpu.make_async_copy(v.at[r, :], h.at[r, :], osem.at[i])

    def forward(t, carry):
        r = tile_at(t)
        h = tok[r, :].astype(F32) + dot(att[r, :], wout[...])
        hidden[r, :] = h
        oacc[r, :] = h
        gacc[r, :] = jnp.zeros_like(h)
        xhat, _ = normalise(h)
        n2[r, :] = (xhat * gain + shift).astype(BF16)
        out_copy(n2, n2_h, r, 3).start()
        return carry
    lax.fori_loop(0, n_t, forward, 0)
    for step in early:
        step()
    loads[3].wait()

    def saves(i, t, slot):
        return (pltpu.make_async_copy(act.at[slot], act_h.at[i, tile_at(t), :], asem.at[0, slot]),
                pltpu.make_async_copy(gi.at[slot], gi_h.at[i, tile_at(t), :], asem.at[1, slot]))

    def tile(step, carry):
        i, t, slot = step // n_t, step % n_t, step % 2
        ws = i % 2
        r = tile_at(t)

        @pl.when(t == 0)
        def _():
            for c in load(wfc.at[ws], wproj.at[ws], ws):
                c.wait()

        @pl.when(step >= 2)
        def _():
            for c in saves(i, t, slot):
                c.wait()
        a, g = gelu_both(dot(n2[r, :], wfc[ws]), dot_nt(cot[r, :], wproj[ws]))
        a, g = a.astype(BF16), g.astype(BF16)
        act[slot] = a
        gi[slot] = g
        oacc[r, :] += dot(a, wproj[ws])
        gacc[r, :] += dot_nt(g, wfc[ws])
        for c in saves(i, t, slot):
            c.start()
        for when, steps in plan.items():
            @pl.when(step == when)
            def _():
                for s in steps:
                    s()
        return carry
    lax.fori_loop(0, n_ff * n_t, tile, 0)
    stat_ref[...] = jnp.zeros_like(stat_ref)

    def backward(t, carry):
        r = tile_at(t)
        tok[r, :] = oacc[r, :].astype(BF16)
        xhat, rstd = normalise(hidden[r, :])
        g = gacc[r, :]
        stat_ref[1:2, :] += jnp.sum(g * xhat, axis=0, keepdims=True)
        stat_ref[3:4, :] += jnp.sum(g, axis=0, keepdims=True)
        gh = cot[r, :].astype(F32) + norm_back(g, xhat, rstd, gain)
        hidden[r, :] = gh
        b = gh.astype(BF16)
        gb[r, :] = b
        att[r, :] = dot_nt(b, wout[...]).astype(BF16)
        for i, (v, h) in enumerate([(tok, lout_h), (hidden, ghid_h), (att, gatt_h)]):
            out_copy(v, h, r, i).start()
        out_copy(gb, gb_h, r, 4).start()
        return carry
    lax.fori_loop(0, n_t, backward, 0)
    if remote:
        for job in sets[0] + sets[1] + sets[2]:
            job.drain()
    for slot in range(2):
        for c in saves(0, 0, slot):
            c.wait()
    for i, (v, h) in enumerate([(tok, lout_h), (hidden, ghid_h), (att, gatt_h), (n2, n2_h), (gb, gb_h)]):
        out_copy(v, h, pl.ds(0, n), i).wait()


def mlp(remote, tokens, att, cot, wout, weights, gs):
    n, width = tokens.shape
    s, dma = jax.ShapeDtypeStruct, pltpu.SemaphoreType.DMA
    any_, vm = pl.BlockSpec(memory_space=pl.ANY), pl.BlockSpec(memory_space=pltpu.VMEM)
    big = lambda d: pltpu.VMEM((n, width), d)
    sq = pltpu.VMEM((2, width, width), BF16)
    part = pltpu.VMEM((2, TILE, width), BF16)
    rows = lambda d: s((n, width), d)
    outs = [rows(BF16), rows(F32), rows(BF16), rows(BF16), rows(BF16), s((4, n, width), BF16), s((4, n, width), BF16), s((8, width), F32)]
    out_specs = [any_] * 7 + [vm]
    scratch = [big(BF16), big(BF16), big(BF16), big(F32), big(F32), big(F32), big(BF16), big(BF16), pltpu.VMEM((width, width), BF16),
               sq, sq, part, part, dma((4,)), dma((2, 2)), dma((2, 2)), dma((5,))]
    params = dict(vmem_limit_bytes=VMEM_BYTES)
    if remote:
        n_dev = width // weights[2].shape[1]
        outs += [s((3, width, width), BF16), s((3, width, width), BF16)]
        out_specs += [any_] * 2
        scratch += [dma((3, 2)), dma((3, 2, n_dev)), dma((3, 2))]
        params.update(collective_id=1, has_side_effects=True)
    return pl.pallas_call(
        functools.partial(mlp_kernel, remote), in_specs=[any_] * 6 + ([vm, any_] if remote else []) + [vm], out_specs=out_specs, out_shape=outs,
        scratch_shapes=scratch, compiler_params=pltpu.CompilerParams(**params), name="mlp",
    )(tokens, att, cot, wout, *weights, gs)[:8]


class Piece:
    def __init__(self, place, parts, total, recv, local, sems):
        self.p, self.parts, self.total, self.sems = place, parts, total, sems
        self.from_core, self.in1, self.in2, self.in3 = recv
        self.out1, self.keep1, self.out2, self.keep2, self.out3 = local

    def hop(self, i, src, dst, to):
        return pltpu.make_async_remote_copy(src_ref=src, dst_ref=dst, send_sem=self.sems.at[0, i], recv_sem=self.sems.at[1, i],
                                            device_id=to, device_id_type=MESH)

    def core(self):
        return self.hop(0, self.parts.at[:, 1 - self.p.c], self.from_core, self.p.partner)

    def h1(self):
        return self.hop(1, self.out1, self.in1, self.p.first2)

    def h2(self):
        return self.hop(2, self.out2, self.in2, self.p.second2)

    def h3(self, k):
        return self.hop(2 + k, self.out3.at[k - 1], self.in3.at[k - 1], self.p.id(z=self.p.z_at(k)))

    def t0(self):
        self.core().start()

    def t1(self):
        p = self.p
        self.core().wait_recv()

        def both(k):
            return self.parts[k, p.c].astype(F32) + self.from_core[k].astype(F32)

        def away(b, carry):
            self.out1[b] = both(p.block(1, b // 4, b % 4)).astype(BF16)
            return carry
        lax.fori_loop(0, 8, away, 0)
        self.h1().start()

        def here(b, carry):
            self.keep1[b] = both(p.block(0, b // 4, b % 4))
            return carry
        lax.fori_loop(0, 8, here, 0)
        self.core().wait_send()

    def t2(self):
        self.h1().wait_recv()

        def away(z, carry):
            self.out2[z] = (self.keep1[4 + z] + self.in1[4 + z].astype(F32)).astype(BF16)
            return carry
        lax.fori_loop(0, 4, away, 0)
        self.h2().start()

        def here(z, carry):
            self.keep2[z] = self.keep1[z] + self.in1[z].astype(F32)
            return carry
        lax.fori_loop(0, 4, here, 0)
        self.h1().wait_send()

    def t3(self):
        p = self.p
        self.h2().wait_recv()
        for k in (2, 1, 3):
            z = p.z_at(k)
            self.out3[k - 1] = (self.keep2[z] + self.in2[z].astype(F32)).astype(BF16)
            self.h3(k).start()
        self.keep2[p.z] = self.keep2[p.z] + self.in2[p.z].astype(F32)
        self.h2().wait_send()

    def t4(self):
        total = self.keep2[self.p.z]
        for k in (1, 3, 2):
            self.h3(k).wait_recv()
            total = total + self.in3[k - 1].astype(F32)
        rows, half = self.total.shape[0], total.shape[1]
        for i in range(self.total.shape[1] // half):
            self.total[:, i * half:(i + 1) * half] = total[i * rows:(i + 1) * rows]
        for k in (1, 2, 3):
            self.h3(k).wait_send()


class Sum:
    def __init__(self, place, stage, came, sems):
        self.p, self.stage, self.came, self.sems = place, stage, came, sems

    def hop(self, i):
        p = self.p
        to = [p.partner, p.first2, p.second2] + [p.id(z=p.z_at(k)) for k in (1, 2, 3)]
        return pltpu.make_async_remote_copy(src_ref=self.stage.at[min(i, 3)], dst_ref=self.came.at[i], send_sem=self.sems.at[0, i],
                                            recv_sem=self.sems.at[1, i], device_id=to[i], device_id_type=MESH)

    def step(self, i):
        self.hop(i).wait_recv()
        self.stage[i + 1] = self.stage[i] + self.came[i]
        for k in (i + 1,) if i < 2 else (3, 4, 5):
            self.hop(k).start()

    def finish(self):
        for i in (3, 4, 5):
            self.hop(i).wait_recv()
        for i in range(6):
            self.hop(i).wait_send()
        return self.stage[3] + self.came[3] + self.came[4] + self.came[5]


class ReducePlace(Place):
    def __init__(self):
        super().__init__()
        self.first2, self.second2 = self.second, self.first

    def block(self, df, ds, z):
        return self.slot_of(ds, df, z) // 2


U_OUT, U_PROJ, U_Q, U_END = 4, 5, 9, 12
LAST_ROWS = 32
DELAYS = (0, 1, 4, 6, 8)
RING_1, RING_2 = 4, 6
RECV = (16, 8, 4, 3)


def pack(g):
    half = g.shape[-1] // 2
    return jnp.concatenate([g[..., :half], g[..., half:]], axis=-2)


def grads_kernel(remote, tok_h, ghid_h, gq_h, gk_h, gv_h, w_h, act_h, gi_h, n2_h, cot_h, att_h, gb_h, gs_ref, stat_two, gtok_h, gskip_h, *refs):
    outs, (pool, gw, w, ghid, gskip, stat, insem, tsem, osem), refs = refs[:5], refs[5:14], refs[14:]
    stat_ref = outs[4]
    n, width = pool.shape[1:]
    half = gskip.shape[2]
    n_t = n // TILE
    gain, shift = gs_ref[0:1, :], gs_ref[2:3, :]

    def load(src, i):
        return pltpu.make_async_copy(src, pool.at[i], insem.at[i])

    def loaded(i):
        load(pool.at[i], i).wait()
    wload = pltpu.make_async_copy(w_h, w, insem.at[6])
    for i, src in enumerate((n2_h, gi_h.at[0], gi_h.at[1], att_h, gb_h, tok_h)):
        load(src, i).start()
    wload.start()
    if remote:
        plan, late = reduce_plan(gw, outs, refs)
    else:
        plan, late = collect_plan(gw, outs, refs)
    loaded(0)

    def normalised():
        loaded(5)

        def tile(t, carry):
            r = tile_at(t)
            xhat, _ = normalise(pool[5, r, :].astype(F32))
            pool[3, r, :] = (xhat * gain + shift).astype(BF16)
            return carry
        lax.fori_loop(0, n_t, tile, 0)

    after = {0: [load(gi_h.at[2], 1).start], 1: [load(gi_h.at[3], 2).start], 2: [load(act_h.at[0], 1).start],
             3: [load(act_h.at[1], 2).start, load(cot_h, 0).start], U_OUT: [load(gq_h, 4).start, normalised],
             5: [load(act_h.at[2], 1).start], 6: [load(act_h.at[3], 2).start],
             8: [load(gk_h, 0).start, load(gv_h, 2).start]}

    def unit(u, carry):
        slot = u % 2
        ring = 1 + jnp.where(u < U_OUT, u, u - U_PROJ) % 2
        proj = (u >= U_PROJ) & (u < U_Q)
        lhs = jnp.where(u < U_OUT, 0, jnp.where(proj, ring, 3))
        rhs = jnp.where(u < U_OUT, ring, jnp.where((u == U_OUT) | (u == U_Q), 4, jnp.where(proj | (u == U_Q + 1), 0, 2)))

        @pl.when((u < U_OUT) | proj)
        def _():
            loaded(ring)

        for when, bufs in {U_OUT: (3, 4), U_PROJ: (0,), U_Q: (4,), U_Q + 1: (0,), U_Q + 2: (2,)}.items():
            @pl.when(u == when)
            def _():
                for b in bufs:
                    loaded(b)

        def rows(m, carry):
            c = pl.ds(pl.multiple_of(m * 384, 128), 384)
            g = dot_tn(pool[lhs, :, c], pool[rhs])
            gw[slot, pl.ds(m * 8, 8)] = pack(g.reshape(8, 2, 24, width)).astype(BF16)
            return carry
        lax.fori_loop(0, 2, rows, 0)
        for when in range(U_END):
            steps = after.get(when, []) + plan.get(when, [])
            if steps:
                @pl.when(u == when)
                def _():
                    for s in steps:
                        s()
        return carry
    lax.fori_loop(0, U_END, unit, 0)
    wload.wait()
    stat[...] = jnp.zeros_like(stat)

    def gin(t):
        return pltpu.make_async_copy(ghid_h.at[tile_at(t), :], ghid.at[t % 2], tsem.at[t % 2])

    def gout(t):
        return (pltpu.make_async_copy(ghid.at[t % 2], gtok_h.at[tile_at(t), :], osem.at[0, t % 2]),
                pltpu.make_async_copy(gskip.at[t % 2], gskip_h.at[tile_at(t), :], osem.at[1, t % 2]))

    gin(0).start()

    def tile(t, carry):
        r, slot = tile_at(t), t % 2
        g = (dot_nt(pool[4, r, :], w[:, :width]) + dot_nt(pool[0, r, :], w[:, width:2 * width])
             + dot_nt(pool[2, r, :half], w[:, 2 * width:]))
        gin(t).wait()

        @pl.when(t > 0)
        def _():
            for c in gout(t - 1):
                c.wait()

        @pl.when(t + 1 < n_t)
        def _():
            gin(t + 1).start()
        xhat, rstd = normalise(pool[5, r, :].astype(F32))
        gskip[slot] = pool[2, r, half:].astype(F32)
        stat[0:1, :] += jnp.sum(g * xhat, axis=0, keepdims=True)
        stat[2:3, :] += jnp.sum(g, axis=0, keepdims=True)
        ghid[slot] += norm_back(g, xhat, rstd, gain)
        for c in gout(t):
            c.start()
        for when in range(n_t):
            steps = plan.get(U_END + when, [])
            if steps:
                @pl.when(t == when)
                def _():
                    for s in steps:
                        s()
        return carry
    lax.fori_loop(0, n_t, tile, 0)
    stat[...] = stat[...] + stat_two[...]
    late(stat)
    for c in gout(n_t - 1):
        c.wait()


def collect_plan(gw, outs, refs):
    parts, stat_ref = outs[0], outs[4]
    sem = refs[0]

    def emit(u):
        def go():
            c = pltpu.make_async_copy(gw.at[u % 2], parts.at[u], sem)
            c.start()
            c.wait()
        return go

    def late(stat):
        stat_ref[...] = stat[...]
    return {u: [emit(u)] for u in range(U_END)}, late


def reduce_plan(gw, outs, refs):
    fc_t, proj_t, out_t, qkv_t, stat_ref = outs
    recv, local, (fcp, stage, came, sems, ssem) = refs[:4], refs[4:9], refs[9:]
    small, width = out_t.shape
    last = qkv_t.shape[1] - 2 * width
    place = ReducePlace()
    enter(place)
    dest = [fcp.at[u] for u in range(N_FF)] + [out_t] + [proj_t.at[pl.ds(u * small, small), :] for u in range(N_FF)] + [
        qkv_t.at[:, pl.ds(0, width)], qkv_t.at[:, pl.ds(width, width)], qkv_t.at[:, pl.ds(2 * width, last)]]
    pieces = []
    for u in range(U_END):
        whole = dest[u].shape[1] == width
        pick = lambda ref, *at: ref.at[at] if whole else ref.at[at + (slice(None),) * (len(ref.shape) - len(at) - 2) + (pl.ds(0, LAST_ROWS),)]
        bufs = [pick(b, u) for b in recv], [pick(b, u % (RING_1 if i < 2 else RING_2)) for i, b in enumerate(local)]
        pieces.append(Piece(place, pick(gw, u % 2), dest[u], *bufs, sems.at[u]))
    todo = [(u + d, -k, u) for u in range(U_END) for k, d in enumerate(DELAYS)]
    todo.sort(key=lambda e: (e[0], e[1] if e[1] else -9, e[2]))
    plan, rest = {}, []
    for when, neg, u in todo:
        step = getattr(pieces[u], "t%d" % -neg)
        if when < U_END + 4:
            plan.setdefault(when, []).append(step)
        else:
            rest.append(step)
    sums = Sum(place, stage, came, ssem)

    def late(stat):
        stage[0] = stat[...]
        sums.hop(0).start()
        between = [lambda: sums.step(0), lambda: sums.step(1), lambda: sums.step(2)]
        fc_t[...] = spread_groups([fcp[j] for j in range(N_FF)], width // small, small)
        for step in rest:
            step()
            if between:
                between.pop(0)()
        for step in between:
            step()
        stat_ref[...] = sums.finish()
    return plan, late


def grads(remote, tokens, ghid, gq, gk, gv, w, act, gi, n2, cot, att, gb, gs, stat):
    n, width = tokens.shape
    fresh = w.shape[1] - 2 * width
    half = width - fresh
    small = 24
    ff = act.shape[0] * width
    s, dma = jax.ShapeDtypeStruct, pltpu.SemaphoreType.DMA
    any_, vm = pl.BlockSpec(memory_space=pl.ANY), pl.BlockSpec(memory_space=pltpu.VMEM)
    block = (2 * small, width // 2)
    outs = [s((n, width), F32), s((n, half), F32)]
    scratch = [pltpu.VMEM((6, n, width), BF16), pltpu.VMEM((2, 16, 2) + block, BF16), pltpu.VMEM(w.shape, BF16), pltpu.VMEM((2, TILE, width), F32),
               pltpu.VMEM((2, TILE, half), F32), pltpu.VMEM((8, width), F32), dma((7,)), dma((2,)), dma((2, 2))]
    params = dict(vmem_limit_bytes=VMEM_BYTES)
    if remote:
        outs += [s((small, ff), F32), s((ff // 32, width), F32), s((small, width), F32), s((small, w.shape[1]), F32)]
        specs = [vm] * 4
        scratch += [pltpu.VMEM((U_END, k) + block, BF16) for k in RECV]
        scratch += [pltpu.VMEM((r, k) + block, d) for r, k, d in ((RING_1, 8, BF16), (RING_1, 8, F32), (RING_2, 4, BF16), (RING_2, 4, F32), (RING_2, 3, BF16))]
        scratch += [pltpu.VMEM((N_FF, small, width), F32), pltpu.VMEM((4, 8, width), F32), pltpu.VMEM((6, 8, width), F32), dma((U_END, 2, 6)), dma((2, 6))]
        params.update(collective_id=2, has_side_effects=True)
    else:
        outs += [s((U_END, 16, 2) + block, BF16)] + [s((8, 128), F32)] * 3
        specs = [any_] * 4
        scratch += [dma(())]
    return pl.pallas_call(
        functools.partial(grads_kernel, remote), in_specs=[any_] * 12 + [vm] * 2, out_specs=[any_] * 2 + specs + [vm],
        out_shape=outs + [s((8, width), F32)], scratch_shapes=scratch,
        compiler_params=pltpu.CompilerParams(**params), name="grads",
    )(tokens, ghid, gq, gk, gv, w, act, gi, n2, cot, att, gb, gs, stat)


def unpack_parts(parts, width, fresh):
    p = parts.astype(F32).reshape(U_END, width // 24, 2, 24, width // 2).transpose(0, 1, 3, 2, 4).reshape(U_END, width, width)
    return (jnp.concatenate([p[U_Q], p[U_Q + 1], p[U_Q + 2, :, :fresh]], axis=1), p[U_OUT], jnp.concatenate(list(p[:N_FF]), axis=1),
            p[U_PROJ:U_Q].reshape(-1, width))


AXES = ("dp", "fsdp")


def body(direct, tokens, skip_values, w_qkv, w_out, w_fc, w_proj, norm_gains, norm_shifts, segment_ids, pad_mask, cotangent):
    micro, rows, length, width = tokens.shape
    half, ff = skip_values.shape[3], w_fc.shape[1]
    seqs = micro * rows
    n = seqs * length
    n_dev, own = width // norm_gains.shape[1], norm_gains.shape[1]
    slot = lax.axis_index(AXES)
    flat = lambda a: a.reshape(n, a.shape[-1])
    seq = lambda a: a.reshape(seqs, length, a.shape[-1])
    tok, skip, cot = flat(tokens), flat(skip_values), flat(cotangent)
    seg, pad = segment_ids.reshape(seqs, length), pad_mask.reshape(seqs, length)
    rows8 = jnp.concatenate([norm_gains, norm_shifts, jnp.zeros((4, own), BF16)], axis=0)
    if direct:
        place = lax.dynamic_update_slice(jnp.zeros((8, width), BF16), rows8, (0, slot * own))
        q, k, v, gs, fcp, _, qkv, out, fc0, proj0 = start(tok, skip, place, w_qkv, w_out, w_fc, w_proj)
        weights = (fc0, proj0, fcp, w_proj)
    else:
        qkv, out, *weights = [lax.all_gather(w, AXES, axis=0, tiled=True) for w in (w_qkv, w_out, w_fc, w_proj)]
        gs = lax.all_gather(rows8, AXES, axis=1, tiled=True).astype(F32)
        q, k, v = project(tok, skip, qkv, gs)
    att, lse = attend(seq(q), seq(k), seq(v), seg, pad)
    att = flat(att)
    lout, ghid, gatt, n2, gb, act, gi, stat = mlp(direct, tok, att, cot, out, weights, gs)
    gq, gk, gv = attend_back(seq(q), seq(k), seq(v), seq(gatt), lse, seg, pad)
    gtok, gskip, gfc, gproj, gout, gqkv, stat = grads(
        direct, tok, ghid, flat(gq), flat(gk), flat(gv), qkv, act, gi, n2, cot, att, gb, gs, stat)
    if direct:
        total_fc, total_proj, total_out, total_qkv = gfc, gproj, gout, gqkv
        sums = lax.dynamic_slice(stat, (0, slot * own), (8, own))
        gains, shifts = sums[0:2], sums[2:4]
    else:
        total_qkv, total_out, total_fc, total_proj = [
            lax.psum_scatter(g, AXES, scatter_dimension=0, tiled=True) for g in unpack_parts(gfc, width, width - half)]
        gains = lax.psum_scatter(stat[0:2], AXES, scatter_dimension=1, tiled=True)
        shifts = lax.psum_scatter(stat[2:4], AXES, scatter_dimension=1, tiled=True)
    shape4 = lambda a: a.reshape(micro, rows, length, a.shape[-1])
    return (shape4(lout), shape4(gtok), shape4(gskip), total_qkv, total_out, total_fc, total_proj, gains, shifts)


def solution(mesh):
    tok, mat, row, ids = P(None, AXES, None, None), P(AXES, None), P(None, AXES), P(None, AXES, None)
    direct = dict(mesh.shape) == {"dp": 2, "fsdp": 16}
    return jax.shard_map(
        functools.partial(body, direct), mesh=mesh,
        in_specs=(tok, tok, mat, mat, mat, mat, row, row, ids, ids, tok),
        out_specs=(tok, tok, tok, mat, mat, mat, mat, row, row), check_vma=False)
```

```python
import functools
import jax
import jax.numpy as jnp
from jax import lax
from jax.experimental import pallas as pl
from jax.experimental.pallas import tpu as pltpu
from jax.sharding import PartitionSpec as P

F32, BF16 = jnp.float32, jnp.bfloat16

HEAD = 64
BLK = 128
WIN = 5
MASKED = -1e9
PAIRS_FWD, PAIRS_BWD = 6, 3


def build_bias(seg_row, pad_row, bias_ref, n_blk):
    code = jnp.where(pad_row == 1, seg_row, -1)
    key = lax.broadcasted_iota(jnp.int32, (BLK, BLK), 0)
    row = lax.broadcasted_iota(jnp.int32, (BLK, BLK), 1)
    for kb in range(n_blk):
        code_k = jnp.broadcast_to(code[:, kb * BLK:(kb + 1) * BLK], (BLK, BLK)).T
        for qb in range(kb, min(kb + WIN, n_blk)):
            vis = code_k == seg_row[:, qb * BLK:(qb + 1) * BLK]
            if kb == qb:
                vis = (vis & (key < row)) | (key == row)
            t = kb - qb + WIN - 1
            bias_ref[qb, t * BLK:(t + 1) * BLK, :] = jnp.where(vis, 0.0, MASKED)


def stack_heads(x):
    low = lax.broadcasted_iota(jnp.int32, x.shape, 1) < HEAD
    zero = jnp.zeros_like(x)
    return jnp.concatenate([jnp.where(low, x, zero), jnp.where(low, zero, x)], axis=0)


def join_heads(x2):
    return jnp.concatenate([x2[:HEAD, :BLK], x2[HEAD:, BLK:]], axis=0)


def twice(x):
    return jnp.concatenate([x, x], axis=1)


def visible_blocks(seg_s, row, qb):
    first = seg_s[row, 0, qb * BLK]
    n = jnp.int32(1)
    for back in range(1, WIN):
        kb = jnp.maximum(qb - back, 0)
        seen = (qb >= back) & (seg_s[row, 0, kb * BLK + BLK - 1] == first)
        n = n + seen.astype(jnp.int32)
    return n


def over_queries(seg_s, row, n_blk, one):
    def step(qb, carry):
        n_vis = visible_blocks(seg_s, row, qb)
        for n in range(1, WIN + 1):
            @pl.when(n_vis == n)
            def _():
                one(n, qb)
        return carry
    lax.fori_loop(0, n_blk, step, 0)


def block(i, n=1):
    return pl.ds(pl.multiple_of(i * BLK, BLK), n * BLK)


def attend_nt(a, b):
    return lax.dot_general(a, b, (((1,), (1,)), ((), ())), preferred_element_type=F32)


def fwd_kernel(n_blk, pairs, seg_s, seg_ref, pad_ref, q_ref, k_ref, v_ref, o_ref, lse_ref, bias_ref, vt_ref):
    row = pl.program_id(0)

    @pl.when(pl.program_id(1) == 0)
    def _():
        build_bias(seg_ref[...], pad_ref[...], bias_ref, n_blk)

    lanes = [slice(i * BLK, (i + 1) * BLK) for i in range(pairs)]
    for kb in range(n_blk):
        for h in lanes:
            vt_ref[h, kb * BLK:(kb + 1) * BLK] = v_ref[kb * BLK:(kb + 1) * BLK, h].T

    def one(n, qb):
        keys, here = block(qb - n + 1, n), block(qb)
        b = twice(bias_ref[qb, (WIN - n) * BLK:, :])
        s = [attend_nt(k_ref[keys, h], stack_heads(q_ref[here, h])) + b for h in lanes]
        for i, h in enumerate(lanes):
            m = jnp.max(s[i], axis=0, keepdims=True)
            p = jnp.exp(s[i] - m)
            total = jnp.sum(p, axis=0, keepdims=True)
            o2 = jnp.dot(vt_ref[h, keys], p.astype(BF16), preferred_element_type=F32) * (1.0 / total)
            o_ref[here, h] = join_heads(o2).astype(BF16).T
            lse_ref[i, qb] = m + jnp.log(total)
    over_queries(seg_s, row, n_blk, one)


def attend(q, k, v, seg, pad):
    rows, length, width = q.shape
    n_blk, pairs = length // BLK, PAIRS_FWD
    groups = width // 128 // pairs
    tok = pl.BlockSpec((None, length, pairs * 128), lambda r, h, s: (r, 0, h))
    ids = pl.BlockSpec((None, 1, length), lambda r, h, s: (r, 0, 0))
    return pl.pallas_call(
        functools.partial(fwd_kernel, n_blk, pairs),
        grid_spec=pltpu.PrefetchScalarGridSpec(
            num_scalar_prefetch=1, grid=(rows, groups),
            in_specs=[ids, ids, tok, tok, tok],
            out_specs=[tok, pl.BlockSpec((None, pairs, n_blk, 1, 2 * BLK), lambda r, h, s: (r, h, 0, 0, 0))],
            scratch_shapes=[pltpu.VMEM((n_blk, WIN * BLK, BLK), F32), pltpu.VMEM((pairs * BLK, length), BF16)]),
        out_shape=[jax.ShapeDtypeStruct((rows, length, width), BF16), jax.ShapeDtypeStruct((rows, width // 128, n_blk, 1, 2 * BLK), F32)],
        compiler_params=pltpu.CompilerParams(dimension_semantics=("arbitrary", "arbitrary"), vmem_limit_bytes=64000 << 10),
        name="attend",
    )(seg, seg, pad, q, k, v)


def bwd_kernel(n_blk, pairs, seg_s, seg_ref, pad_ref, q_ref, k_ref, v_ref, g_ref, lse_ref, result_ref, dq_ref, dk_ref, dv_ref, dskip_ref, result_out,
               bias_ref, kt_ref, dk_acc, dv_acc):
    row = pl.program_id(0)
    result_out[...] = result_ref[...]

    @pl.when(pl.program_id(1) == 0)
    def _():
        build_bias(seg_ref[...], pad_ref[...], bias_ref, n_blk)

    lanes = [slice(i * BLK, (i + 1) * BLK) for i in range(pairs)]
    for kb in range(n_blk):
        for h in lanes:
            kt_ref[h, kb * BLK:(kb + 1) * BLK] = k_ref[kb * BLK:(kb + 1) * BLK, h].T
    dk_acc[...] = jnp.zeros_like(dk_acc)
    dv_acc[...] = jnp.zeros_like(dv_acc)

    def one(n, qb):
        keys, here = block(qb - n + 1, n), block(qb)
        b = twice(bias_ref[qb, (WIN - n) * BLK:, :])
        for i, h in enumerate(lanes):
            q2, g2 = stack_heads(q_ref[here, h]), stack_heads(g_ref[here, h])
            p = jnp.exp(attend_nt(k_ref[keys, h], q2) + b - lse_ref[i, qb])
            dp = attend_nt(v_ref[keys, h], g2)
            inner = jnp.sum(p * dp, axis=0, keepdims=True)
            ds = (p * (dp - inner)).astype(BF16)
            dv_acc[keys, h] += jnp.dot(p.astype(BF16), g2, preferred_element_type=F32)
            dk_acc[keys, h] += jnp.dot(ds, q2, preferred_element_type=F32)
            dq2 = jnp.dot(kt_ref[h, keys], ds, preferred_element_type=F32)
            dq_ref[here, h] = (join_heads(dq2) * 0.125).astype(BF16).T
    over_queries(seg_s, row, n_blk, one)
    dk_ref[...] = dk_acc[...].astype(BF16)
    dv_ref[...] = dv_acc[...].astype(BF16)

    @pl.when(pl.program_id(1) == pl.num_programs(1) - 1)
    def _():
        dskip_ref[...] = dv_ref[:, dv_ref.shape[1] - dskip_ref.shape[1]:].astype(F32)


def attend_back(q, k, v, g, lse, seg, pad, result, half):
    rows, length, width = q.shape
    n_blk, pairs = length // BLK, PAIRS_BWD
    groups = width // 128 // pairs
    tok = pl.BlockSpec((None, length, pairs * 128), lambda r, h, s: (r, 0, h))
    ids = pl.BlockSpec((None, 1, length), lambda r, h, s: (r, 0, 0))
    out = jax.ShapeDtypeStruct((rows, length, width), BF16)
    return pl.pallas_call(
        functools.partial(bwd_kernel, n_blk, pairs),
        grid_spec=pltpu.PrefetchScalarGridSpec(
            num_scalar_prefetch=1, grid=(rows, groups),
            in_specs=[ids, ids, tok, tok, tok, tok, pl.BlockSpec((None, pairs, n_blk, 1, 2 * BLK), lambda r, h, s: (r, h, 0, 0, 0)), tok],
            out_specs=[tok, tok, tok, pl.BlockSpec((None, length, half), lambda r, h, s: (r, 0, 0)), tok],
            scratch_shapes=[pltpu.VMEM((n_blk, WIN * BLK, BLK), F32), pltpu.VMEM((pairs * BLK, length), BF16),
                            pltpu.VMEM((length, pairs * BLK), F32), pltpu.VMEM((length, pairs * BLK), F32)]),
        out_shape=[out, out, out, jax.ShapeDtypeStruct((rows, length, half), F32), out],
        compiler_params=pltpu.CompilerParams(dimension_semantics=("arbitrary", "arbitrary"), vmem_limit_bytes=64000 << 10),
        name="attend_back",
    )(seg, seg, pad, q, k, v, g, lse, result)


MESH = pl.DeviceIdType.MESH
NZ = 4


class Place:
    def __init__(self):
        dp, fs = lax.axis_index("dp"), lax.axis_index("fsdp")
        self.x, self.z, self.y, self.c = dp, fs // 4, (fs // 2) % 2, fs % 2
        self.slot = self.x * 16 + fs
        self.first = self.id(x=jnp.where(self.c == 0, 1 - self.x, self.x), y=jnp.where(self.c == 0, self.y, 1 - self.y))
        self.second = self.id(x=jnp.where(self.c == 0, self.x, 1 - self.x), y=jnp.where(self.c == 0, 1 - self.y, self.y))
        self.partner = self.id(c=1 - self.c)

    def id(self, x=None, y=None, z=None, c=None):
        x = self.x if x is None else x
        y = self.y if y is None else y
        z = self.z if z is None else z
        c = self.c if c is None else c
        return (x, z * 4 + y * 2 + c)

    def z_at(self, k):
        return (self.z + k) % NZ

    def peers(self):
        return [self.partner, self.first, self.second] + [self.id(z=self.z_at(k)) for k in (1, 2, 3)]

    def slot_of(self, df, ds, z):
        dx = jnp.where(self.c == 0, df, ds)
        dy = jnp.where(self.c == 0, ds, df)
        x = jnp.where(dx == 1, 1 - self.x, self.x)
        y = jnp.where(dy == 1, 1 - self.y, self.y)
        return x * 16 + z * 4 + y * 2 + self.c


def enter(place):
    bar = pltpu.get_barrier_semaphore()
    for peer in place.peers():
        pl.semaphore_signal(bar, inc=1, device_id=peer, device_id_type=MESH)
    pl.semaphore_wait(bar, 6)


class Gather:
    SENDS = 31

    def __init__(self, place, shard, out, send, recv, own):
        self.p, self.shard, self.out, self.send, self.recv, self.own = place, shard, out, send, recv, own
        self.size = shard.shape[0]

    def at(self, slot, n=1):
        return self.out.at[pl.ds(pl.multiple_of(slot * self.size, 8), n * self.size), :]

    def push(self, src, slot, to):
        pltpu.make_async_remote_copy(src_ref=src, dst_ref=self.at(slot), send_sem=self.send, recv_sem=self.recv.at[slot],
                                     device_id=to, device_id_type=MESH).start()

    def arrived(self, slot):
        pltpu.make_async_copy(self.at(slot), self.at(slot), self.recv.at[slot]).wait()

    def keep(self, slot):
        return pltpu.make_async_copy(self.shard, self.at(slot), self.own)

    def s1(self):
        p = self.p
        self.keep(p.slot).start()
        for k in (1, 3, 2):
            self.push(self.shard, p.slot, p.id(z=p.z_at(k)))
        for to in (p.first, p.partner, p.second):
            self.push(self.shard, p.slot, to)

    def s2(self):
        p = self.p
        for k in (1, 3, 2):
            slot = p.slot_of(0, 0, p.z_at(k))
            self.arrived(slot)
            for to in (p.first, p.second, p.partner):
                self.push(self.at(slot), slot, to)

    def s3(self):
        p = self.p
        for k in (0, 1, 3, 2):
            slot = p.slot_of(1, 0, p.z_at(k))
            self.arrived(slot)
            for to in (p.second, p.partner):
                self.push(self.at(slot), slot, to)

    def s4(self):
        p = self.p
        for df in (0, 1):
            for k in (0, 1, 3, 2):
                slot = p.slot_of(df, 1, p.z_at(k))
                self.arrived(slot)
                self.push(self.at(slot), slot, p.partner)

    def s5(self):
        for k in range(16):
            self.arrived(2 * k + 1 - self.p.c)
        self.keep(self.p.slot).wait()

    def drain(self):
        done = self.at(0, self.SENDS)
        pltpu.make_async_copy(done, done, self.send).wait()


VMEM_BYTES = 64000 << 10
TILE = 512
EPS = 1e-5
GELU_C = 0.7978845608028654
GELU_A = 0.044715


def dot(a, b):
    return jnp.dot(a, b, preferred_element_type=F32)


def dot_nt(a, b):
    return lax.dot_general(a, b, (((1,), (1,)), ((), ())), preferred_element_type=F32)


def dot_tn(a, b):
    return lax.dot_general(a, b, (((0,), (0,)), ((), ())), preferred_element_type=F32)


def normalise(v):
    centred = v - jnp.mean(v, axis=-1, keepdims=True)
    rstd = lax.rsqrt(jnp.mean(centred * centred, axis=-1, keepdims=True) + EPS)
    return centred * rstd, rstd


def norm_back(g, xhat, rstd, gain):
    gh = g * gain
    return rstd * (gh - jnp.mean(gh, axis=-1, keepdims=True) - xhat * jnp.mean(gh * xhat, axis=-1, keepdims=True))


def gelu_both(u, grad):
    sq = u * u
    t = jnp.tanh(u * (GELU_C + (GELU_C * GELU_A) * sq))
    half = 0.5 + 0.5 * t
    act = u * half
    slope = half + act * (1.0 - half) * (2.0 * GELU_C + (6.0 * GELU_C * GELU_A) * sq)
    return act, grad * slope


def tile_at(t):
    return pl.ds(pl.multiple_of(t * TILE, TILE), TILE)


def qkv_kernel(tok_ref, skip_ref, w_ref, gs_ref, q_ref, k_ref, v_ref):
    width, half = tok_ref.shape[1], skip_ref.shape[1]
    xhat, _ = normalise(tok_ref[...].astype(F32))
    normed = (xhat * gs_ref[0:1, :] + gs_ref[2:3, :]).astype(BF16)
    q_ref[...] = (dot(normed, w_ref[:, :width]) * 0.125).astype(BF16)
    k_ref[...] = dot(normed, w_ref[:, width:2 * width]).astype(BF16)
    v_ref[:, :half] = dot(normed, w_ref[:, 2 * width:]).astype(BF16)
    v_ref[:, half:] = skip_ref[...]


def project(tokens, skip, w, gs):
    n, width = tokens.shape
    row = lambda c: pl.BlockSpec((TILE, c), lambda t: (t, 0))
    whole = lambda a: pl.BlockSpec(a.shape, lambda t: (0, 0))
    out = jax.ShapeDtypeStruct((n, width), BF16)
    return pl.pallas_call(
        qkv_kernel, grid=(n // TILE,), in_specs=[row(width), row(skip.shape[1]), whole(w), whole(gs)],
        out_specs=[row(width)] * 3, out_shape=[out] * 3,
        compiler_params=pltpu.CompilerParams(vmem_limit_bytes=VMEM_BYTES), name="project",
    )(tokens, skip, w, gs)


def lane_mod(x, period):
    return lax.rem(lax.broadcasted_iota(jnp.int32, x.shape, 1), jnp.int32(period))


def gather_groups(x, groups, size, parts):
    out = []
    total = x.shape[1]
    for j in range(parts):
        y = pltpu.roll(x, total - j * size, 1) if j else x
        span = size
        while span < groups * size:
            m = lane_mod(y, 2 * parts * span)
            y = jnp.where((m >= span) & (m < 2 * span), pltpu.roll(y, total - (parts - 1) * span, 1), y)
            span *= 2
        out.append(y[:, :groups * size])
    return out


def spread_groups(pieces, groups, size):
    parts = len(pieces)
    out = None
    for j, piece in enumerate(pieces):
        y = jnp.concatenate([piece] + [jnp.zeros_like(piece)] * (parts - 1), axis=1)
        span = groups * size
        while span > size:
            span //= 2
            m = lane_mod(y, 2 * parts * span)
            y = jnp.where((m >= parts * span) & (m < (parts + 1) * span), pltpu.roll(y, (parts - 1) * span, 1), y)
        y = pltpu.roll(y, j * size, 1) if j else y
        m = lane_mod(y, parts * size)
        y = jnp.where((m >= j * size) & (m < (j + 1) * size), y, 0.0)
        out = y if out is None else out + y
    return out


N_FF = 4


def start_kernel(tok_h, skip_h, gain_ref, shift_ref, qkv_ref, out_ref, fc_ref, proj_h,
                 q_h, k_h, v_h, gs_ref, fcp_ref, gs_all, qkv_all, out_all, fc_all, proj_all,
                 tok, skip, xhat, w, gsb, q, k, v, normed, rows_ref, insem, osem, send, recv, own):
    n, width = tok.shape
    half = skip.shape[1]
    n_t = n // TILE
    n_dev = qkv_all.shape[0] // qkv_ref.shape[0]
    size = proj_h.shape[0] // N_FF
    place = Place()
    loads = [pltpu.make_async_copy(tok_h, tok, insem.at[0]), pltpu.make_async_copy(skip_h, skip, insem.at[1])]
    for c in loads:
        c.start()
    enter(place)
    cols = [pl.ds(0, width), pl.ds(width, width), pl.ds(2 * width, half)]
    shards = (rows_ref, *[qkv_ref.at[:, c] for c in cols], out_ref, fcp_ref.at[0], proj_h.at[pl.ds(0, size), :])
    outs = (gs_all, *[qkv_all.at[:, c] for c in cols], out_all, fc_all, proj_all)
    jobs = [Gather(place, s, o, send.at[i], recv.at[i], own.at[i]) for i, (s, o) in enumerate(zip(shards, outs))]
    rows, wq, wk, wv, out, fc, proj = jobs
    wq.s1()
    mine = jnp.concatenate([gain_ref[...], shift_ref[...]], axis=0)
    lane = lax.broadcasted_iota(jnp.int32, (mine.shape[1], width), 1) - mine.shape[1] * place.slot
    spot = (lane == lax.broadcasted_iota(jnp.int32, lane.shape, 0)).astype(BF16)
    rows_ref[0:4, :] = dot(mine, spot).astype(BF16)
    rows_ref[4:8, :] = jnp.zeros((4, width), BF16)
    wk.s1(), wv.s1()
    for c in loads:
        c.wait()

    def centre(t, carry):
        r = tile_at(t)
        xhat[r, :], _ = normalise(tok[r, :].astype(F32))
        return carry
    lax.fori_loop(0, n_t // 2, centre, 0)
    rows.s1()
    wq.s2()
    for j, piece in enumerate(gather_groups(fc_ref[...].astype(F32), n_dev, size, N_FF)):
        fcp_ref[j] = piece.astype(BF16)
    wk.s2(), wv.s2()
    out.s1()
    lax.fori_loop(n_t // 2, n_t, centre, 0)
    fc.s1(), proj.s1()
    rows.s2(), wq.s3(), rows.s3(), wk.s3(), wv.s3(), wq.s4(), rows.s4(), wk.s4(), out.s2(), wq.s5(), rows.s5()
    wloads = [pltpu.make_async_copy(qkv_all.at[:, c], w.at[:, c], insem.at[4 + i]) for i, c in enumerate(cols)]
    gload = pltpu.make_async_copy(gs_all, gsb, insem.at[3])
    wloads[0].start(), gload.start()
    wv.s4(), fc.s2(), proj.s2()
    gload.wait()
    gs_ref[...] = jnp.sum(gsb[...].astype(F32).reshape(n_dev, 8, width), axis=0)
    wloads[0].wait()

    def copies(r):
        return [pltpu.make_async_copy(s.at[r, :], h.at[r, :], osem.at[i]) for i, (s, h) in enumerate([(q, q_h), (k, k_h), (v, v_h)])]

    def third(i, put):
        def tile(t, carry):
            r = tile_at(t)
            put(r)
            copies(r)[i].start()
            return carry
        lax.fori_loop(0, n_t, tile, 0)

    def put_q(r):
        normed[r, :] = (xhat[r, :] * gs_ref[0:1, :] + gs_ref[2:3, :]).astype(BF16)
        q[r, :] = (dot(normed[r, :], w[:, :width]) * 0.125).astype(BF16)

    def put_k(r):
        k[r, :] = dot(normed[r, :], w[:, width:2 * width]).astype(BF16)

    def put_v(r):
        v[r, :half] = dot(normed[r, :], w[:, 2 * width:]).astype(BF16)
        v[r, half:] = skip[r, :]
    third(0, put_q)
    out.s3(), wk.s5()
    wloads[1].start()
    wv.s5()
    wloads[2].start()
    fc.s3()
    wloads[1].wait()
    third(1, put_k)
    proj.s3(), out.s4()
    wloads[2].wait()
    third(2, put_v)
    fc.s4(), out.s5(), proj.s4(), fc.s5(), proj.s5()
    for job in jobs:
        job.drain()
    for c in copies(pl.ds(0, n)):
        c.wait()


def start(tokens, skip, gains, shifts, qkv, out, fc, proj):
    n, width = tokens.shape
    n_dev = width // out.shape[0]
    s, dma = jax.ShapeDtypeStruct, pltpu.SemaphoreType.DMA
    any_, vm = pl.BlockSpec(memory_space=pl.ANY), pl.BlockSpec(memory_space=pltpu.VMEM)
    big = lambda d: pltpu.VMEM((n, width), d)
    act = s((n, width), BF16)
    gathered = [(8 * n_dev, width), (width, qkv.shape[1]), (width, width), (width, width), (width, width)]
    return pl.pallas_call(
        start_kernel, in_specs=[any_, any_] + [vm] * 5 + [any_], out_specs=[any_] * 3 + [vm] * 2 + [any_] * 5,
        out_shape=[act] * 3 + [s((8, width), F32), s((N_FF, fc.shape[0], width), BF16)] + [s(g, BF16) for g in gathered],
        scratch_shapes=[big(BF16), pltpu.VMEM(skip.shape, BF16), big(F32), pltpu.VMEM((width, qkv.shape[1]), BF16), pltpu.VMEM((8 * n_dev, width), BF16),
                        big(BF16), big(BF16), big(BF16), big(BF16), pltpu.VMEM((8, width), BF16), dma((7,)), dma((3,)), dma((7,)), dma((7, n_dev)), dma((7,))],
        compiler_params=pltpu.CompilerParams(vmem_limit_bytes=VMEM_BYTES, collective_id=0, has_side_effects=True), name="start",
    )(tokens, skip, gains, shifts, qkv, out, fc, proj)


MLP_STEPS = {1: (-1, 0, 1, 2), 2: (0, 2, 4, 6), 3: (2, 4, 6, 8)}


def mlp_kernel(remote, tok_h, att_h, cot_h, wout_h, *refs):
    if remote:
        fc0_h, proj0_h, fcp_ref, proj_ref, *refs = refs
    else:
        wfc_h, wproj_h, *refs = refs
    (gs_ref, lout_h, ghid_h, gatt_h, n2_h, gb_h, act_h, gi_h, stat_ref), refs = refs[:9], refs[9:]
    if remote:
        (fc_all, proj_all), refs = refs[:2], refs[2:]
    (tok, att, cot, hidden, oacc, gacc, n2, gb, wout, wfc, wproj, act, gi, insem, wsem, asem, osem), sems = refs[:17], refs[17:]
    n, width = tok.shape
    n_ff = N_FF
    n_t = n // TILE
    gain, shift = gs_ref[1:2, :], gs_ref[3:4, :]

    def load(src_fc, src_proj, slot):
        return (pltpu.make_async_copy(src_fc, wfc.at[slot], wsem.at[0, slot]), pltpu.make_async_copy(src_proj, wproj.at[slot], wsem.at[1, slot]))

    loads = [pltpu.make_async_copy(h, v, insem.at[i]) for i, (h, v) in enumerate([(wout_h, wout), (att_h, att), (tok_h, tok), (cot_h, cot)])]
    for c in loads:
        c.start()
    plan = {}
    if remote:
        send, recv, own = sems
        place = Place()
        enter(place)
        size = proj_ref.shape[0] // n_ff
        sets = []
        for i in range(1, n_ff):
            srcs = (fcp_ref.at[i], proj_ref.at[pl.ds(i * size, size), :])
            sets.append([Gather(place, srcs[k], (fc_all, proj_all)[k].at[i - 1], send.at[i - 1, k], recv.at[i - 1, k], own.at[i - 1, k]) for k in range(2)])

        def run(i, step):
            return lambda: [getattr(job, step)() for job in sets[i - 1]]

        def fetch(i):
            def go():
                for c in load(fc_all.at[i - 1], proj_all.at[i - 1], i % 2):
                    c.start()
            return go
        for i in range(1, n_ff):
            run(i, "s1")()
        early = []
        for i, steps in MLP_STEPS.items():
            for when, name in zip(steps, ("s2", "s3", "s4", "s5")):
                (early if when < 0 else plan.setdefault(when, [])).append(run(i, name))
            plan[steps[3]].append(fetch(i))
        for c in load(fc0_h, proj0_h, 0):
            c.start()
    else:
        early = []
        cols = lambda j: pl.ds(j * width, width)
        for i in range(1, n_ff):
            def fetch(i=i):
                for c in load(wfc_h.at[:, cols(i)], wproj_h.at[cols(i), :], i % 2):
                    c.start()
            plan[(i - 1) * n_t + 3] = [fetch]
        for c in load(wfc_h.at[:, cols(0)], wproj_h.at[cols(0), :], 0):
            c.start()
    for c in loads[:3]:
        c.wait()

    def out_copy(v, h, r, i):
        return pltpu.make_async_copy(v.at[r, :], h.at[r, :], osem.at[i])

    def forward(t, carry):
        r = tile_at(t)
        h = tok[r, :].astype(F32) + dot(att[r, :], wout[...])
        hidden[r, :] = h
        oacc[r, :] = h
        gacc[r, :] = jnp.zeros_like(h)
        xhat, _ = normalise(h)
        n2[r, :] = (xhat * gain + shift).astype(BF16)
        out_copy(n2, n2_h, r, 3).start()
        return carry
    lax.fori_loop(0, n_t, forward, 0)
    for step in early:
        step()
    loads[3].wait()

    def saves(i, t, slot):
        return (pltpu.make_async_copy(act.at[slot], act_h.at[i, tile_at(t), :], asem.at[0, slot]),
                pltpu.make_async_copy(gi.at[slot], gi_h.at[i, tile_at(t), :], asem.at[1, slot]))

    def tile(step, carry):
        i, t, slot = step // n_t, step % n_t, step % 2
        ws = i % 2
        r = tile_at(t)

        @pl.when(t == 0)
        def _():
            for c in load(wfc.at[ws], wproj.at[ws], ws):
                c.wait()

        @pl.when(step >= 2)
        def _():
            for c in saves(i, t, slot):
                c.wait()
        a, g = gelu_both(dot(n2[r, :], wfc[ws]), dot_nt(cot[r, :], wproj[ws]))
        a, g = a.astype(BF16), g.astype(BF16)
        act[slot] = a
        gi[slot] = g
        oacc[r, :] += dot(a, wproj[ws])
        gacc[r, :] += dot_nt(g, wfc[ws])
        for c in saves(i, t, slot):
            c.start()
        for when, steps in plan.items():
            @pl.when(step == when)
            def _():
                for s in steps:
                    s()
        return carry
    lax.fori_loop(0, n_ff * n_t, tile, 0)
    stat_ref[...] = jnp.zeros_like(stat_ref)

    def backward(t, carry):
        r = tile_at(t)
        tok[r, :] = oacc[r, :].astype(BF16)
        xhat, rstd = normalise(hidden[r, :])
        g = gacc[r, :]
        stat_ref[1:2, :] += jnp.sum(g * xhat, axis=0, keepdims=True)
        stat_ref[3:4, :] += jnp.sum(g, axis=0, keepdims=True)
        gh = cot[r, :].astype(F32) + norm_back(g, xhat, rstd, gain)
        hidden[r, :] = gh
        b = gh.astype(BF16)
        gb[r, :] = b
        att[r, :] = dot_nt(b, wout[...]).astype(BF16)
        for i, (v, h) in enumerate([(tok, lout_h), (hidden, ghid_h), (att, gatt_h)]):
            out_copy(v, h, r, i).start()
        out_copy(gb, gb_h, r, 4).start()
        return carry
    lax.fori_loop(0, n_t, backward, 0)
    if remote:
        for job in sets[0] + sets[1] + sets[2]:
            job.drain()
    for slot in range(2):
        for c in saves(0, 0, slot):
            c.wait()
    for i, (v, h) in enumerate([(tok, lout_h), (hidden, ghid_h), (att, gatt_h), (n2, n2_h), (gb, gb_h)]):
        out_copy(v, h, pl.ds(0, n), i).wait()


def mlp(remote, tokens, att, cot, wout, weights, gs):
    n, width = tokens.shape
    s, dma = jax.ShapeDtypeStruct, pltpu.SemaphoreType.DMA
    any_, vm = pl.BlockSpec(memory_space=pl.ANY), pl.BlockSpec(memory_space=pltpu.VMEM)
    big = lambda d: pltpu.VMEM((n, width), d)
    sq = pltpu.VMEM((2, width, width), BF16)
    part = pltpu.VMEM((2, TILE, width), BF16)
    rows = lambda d: s((n, width), d)
    outs = [rows(BF16), rows(F32), rows(BF16), rows(BF16), rows(BF16), s((4, n, width), BF16), s((4, n, width), BF16), s((8, width), F32)]
    out_specs = [any_] * 7 + [vm]
    scratch = [big(BF16), big(BF16), big(BF16), big(F32), big(F32), big(F32), big(BF16), big(BF16), pltpu.VMEM((width, width), BF16),
               sq, sq, part, part, dma((4,)), dma((2, 2)), dma((2, 2)), dma((5,))]
    params = dict(vmem_limit_bytes=VMEM_BYTES)
    if remote:
        n_dev = width // weights[2].shape[1]
        outs += [s((3, width, width), BF16), s((3, width, width), BF16)]
        out_specs += [any_] * 2
        scratch += [dma((3, 2)), dma((3, 2, n_dev)), dma((3, 2))]
        params.update(collective_id=1, has_side_effects=True)
    return pl.pallas_call(
        functools.partial(mlp_kernel, remote), in_specs=[any_] * 6 + ([vm, any_] if remote else []) + [vm], out_specs=out_specs, out_shape=outs,
        scratch_shapes=scratch, compiler_params=pltpu.CompilerParams(**params), name="mlp",
    )(tokens, att, cot, wout, *weights, gs)[:8]


class Piece:
    def __init__(self, place, parts, total, recv, local, sems):
        self.p, self.parts, self.total, self.sems = place, parts, total, sems
        self.from_core, self.in1, self.in2, self.in3 = recv
        self.out1, self.keep1, self.out2, self.keep2, self.out3 = local

    def hop(self, i, src, dst, to):
        return pltpu.make_async_remote_copy(src_ref=src, dst_ref=dst, send_sem=self.sems.at[0, i], recv_sem=self.sems.at[1, i],
                                            device_id=to, device_id_type=MESH)

    def core(self):
        return self.hop(0, self.parts.at[:, 1 - self.p.c], self.from_core, self.p.partner)

    def h1(self):
        return self.hop(1, self.out1, self.in1, self.p.first2)

    def h2(self):
        return self.hop(2, self.out2, self.in2, self.p.second2)

    def h3(self, k):
        return self.hop(2 + k, self.out3.at[k - 1], self.in3.at[k - 1], self.p.id(z=self.p.z_at(k)))

    def t0(self):
        self.core().start()

    def t1(self):
        p = self.p
        self.core().wait_recv()

        def both(k):
            return self.parts[k, p.c].astype(F32) + self.from_core[k].astype(F32)

        def away(b, carry):
            self.out1[b] = both(p.block(1, b // 4, b % 4)).astype(BF16)
            return carry
        lax.fori_loop(0, 8, away, 0)
        self.h1().start()

        def here(b, carry):
            self.keep1[b] = both(p.block(0, b // 4, b % 4))
            return carry
        lax.fori_loop(0, 8, here, 0)
        self.core().wait_send()

    def t2(self):
        self.h1().wait_recv()

        def away(z, carry):
            self.out2[z] = (self.keep1[4 + z] + self.in1[4 + z].astype(F32)).astype(BF16)
            return carry
        lax.fori_loop(0, 4, away, 0)
        self.h2().start()

        def here(z, carry):
            self.keep2[z] = self.keep1[z] + self.in1[z].astype(F32)
            return carry
        lax.fori_loop(0, 4, here, 0)
        self.h1().wait_send()

    def t3(self):
        p = self.p
        self.h2().wait_recv()
        for k in (2, 1, 3):
            z = p.z_at(k)
            self.out3[k - 1] = (self.keep2[z] + self.in2[z].astype(F32)).astype(BF16)
            self.h3(k).start()
        self.keep2[p.z] = self.keep2[p.z] + self.in2[p.z].astype(F32)
        self.h2().wait_send()

    def t4(self):
        total = self.keep2[self.p.z]
        for k in (1, 3, 2):
            self.h3(k).wait_recv()
            total = total + self.in3[k - 1].astype(F32)
        rows, half = self.total.shape[0], total.shape[1]
        for i in range(self.total.shape[1] // half):
            self.total[:, i * half:(i + 1) * half] = total[i * rows:(i + 1) * rows]
        for k in (1, 2, 3):
            self.h3(k).wait_send()


class Sum:
    def __init__(self, place, stage, came, sems):
        self.p, self.stage, self.came, self.sems = place, stage, came, sems

    def hop(self, i):
        p = self.p
        to = [p.partner, p.first2, p.second2] + [p.id(z=p.z_at(k)) for k in (1, 2, 3)]
        return pltpu.make_async_remote_copy(src_ref=self.stage.at[min(i, 3)], dst_ref=self.came.at[i], send_sem=self.sems.at[0, i],
                                            recv_sem=self.sems.at[1, i], device_id=to[i], device_id_type=MESH)

    def step(self, i):
        self.hop(i).wait_recv()
        self.stage[i + 1] = self.stage[i] + self.came[i]
        for k in (i + 1,) if i < 2 else (3, 4, 5):
            self.hop(k).start()

    def finish(self):
        for i in (3, 4, 5):
            self.hop(i).wait_recv()
        for i in range(6):
            self.hop(i).wait_send()
        return self.stage[3] + self.came[3] + self.came[4] + self.came[5]


class ReducePlace(Place):
    def __init__(self):
        super().__init__()
        self.first2, self.second2 = self.second, self.first

    def block(self, df, ds, z):
        return self.slot_of(ds, df, z) // 2


AXES = ("dp", "fsdp")
U_OUT, U_PROJ, U_Q, U_END = 4, 5, 9, 12
LAST_ROWS = 32
DELAYS = (0, 1, 4, 6, 8)
RING_1, RING_2 = 4, 6
RECV = (16, 8, 4, 3)


def pack(g):
    half = g.shape[-1] // 2
    return jnp.concatenate([g[..., :half], g[..., half:]], axis=-2)


def grads_kernel(remote, tok_h, ghid_h, gq_h, gk_h, gv_h, w_h, act_h, gi_h, n2_h, cot_h, att_h, gb_h, gs_ref, stat_two, gtok_h, *refs):
    outs, (pool, gw, w, ghid, stat, insem, tsem, osem), refs = refs[:5], refs[5:13], refs[13:]
    stat_ref = outs[4]
    n, width = pool.shape[1:]
    fresh = w.shape[1] - 2 * width
    n_t = n // TILE
    gain, shift = gs_ref[0:1, :], gs_ref[2:3, :]

    def load(src, i):
        return pltpu.make_async_copy(src, pool.at[i], insem.at[i])

    def loaded(i):
        load(pool.at[i], i).wait()
    wload = pltpu.make_async_copy(w_h, w, insem.at[6])
    for i, src in enumerate((n2_h, gi_h.at[0], gi_h.at[1], att_h, gb_h, tok_h)):
        load(src, i).start()
    wload.start()
    if remote:
        plan, late = reduce_plan(gw, outs, refs)
    else:
        plan, late = collect_plan(gw, outs, refs)
    loaded(0)

    def normalised():
        loaded(5)

        def tile(t, carry):
            r = tile_at(t)
            xhat, _ = normalise(pool[5, r, :].astype(F32))
            pool[3, r, :] = (xhat * gain + shift).astype(BF16)
            return carry
        lax.fori_loop(0, n_t, tile, 0)

    after = {0: [load(gi_h.at[2], 1).start], 1: [load(gi_h.at[3], 2).start], 2: [load(act_h.at[0], 1).start],
             3: [load(act_h.at[1], 2).start, load(cot_h, 0).start], U_OUT: [load(gq_h, 4).start, normalised],
             5: [load(act_h.at[2], 1).start], 6: [load(act_h.at[3], 2).start],
             8: [load(gk_h, 0).start, load(gv_h, 2).start]}

    def unit(u, carry):
        slot = u % 2
        ring = 1 + jnp.where(u < U_OUT, u, u - U_PROJ) % 2
        proj = (u >= U_PROJ) & (u < U_Q)
        lhs = jnp.where(u < U_OUT, 0, jnp.where(proj, ring, 3))
        rhs = jnp.where(u < U_OUT, ring, jnp.where((u == U_OUT) | (u == U_Q), 4, jnp.where(proj | (u == U_Q + 1), 0, 2)))

        @pl.when((u < U_OUT) | proj)
        def _():
            loaded(ring)

        for when, bufs in {U_OUT: (3, 4), U_PROJ: (0,), U_Q: (4,), U_Q + 1: (0,), U_Q + 2: (2,)}.items():
            @pl.when(u == when)
            def _():
                for b in bufs:
                    loaded(b)

        def rows(m, carry):
            c = pl.ds(pl.multiple_of(m * 384, 128), 384)
            g = dot_tn(pool[lhs, :, c], pool[rhs])
            gw[slot, pl.ds(m * 8, 8)] = pack(g.reshape(8, 2, 24, width)).astype(BF16)
            return carry
        lax.fori_loop(0, 2, rows, 0)
        for when in range(U_END):
            steps = after.get(when, []) + plan.get(when, [])
            if steps:
                @pl.when(u == when)
                def _():
                    for s in steps:
                        s()
        return carry
    lax.fori_loop(0, U_END, unit, 0)
    wload.wait()
    stat[...] = jnp.zeros_like(stat)

    def gin(t):
        return pltpu.make_async_copy(ghid_h.at[tile_at(t), :], ghid.at[t % 2], tsem.at[t % 2])

    def gout(t):
        return pltpu.make_async_copy(ghid.at[t % 2], gtok_h.at[tile_at(t), :], osem.at[t % 2])

    gin(0).start()

    def tile(t, carry):
        r, slot = tile_at(t), t % 2
        g = (dot_nt(pool[4, r, :], w[:, :width]) + dot_nt(pool[0, r, :], w[:, width:2 * width])
             + dot_nt(pool[2, r, :fresh], w[:, 2 * width:]))
        gin(t).wait()

        @pl.when(t > 0)
        def _():
            gout(t - 1).wait()

        @pl.when(t + 1 < n_t)
        def _():
            gin(t + 1).start()
        xhat, rstd = normalise(pool[5, r, :].astype(F32))
        stat[0:1, :] += jnp.sum(g * xhat, axis=0, keepdims=True)
        stat[2:3, :] += jnp.sum(g, axis=0, keepdims=True)
        ghid[slot] += norm_back(g, xhat, rstd, gain)
        gout(t).start()
        for when in range(n_t):
            steps = plan.get(U_END + when, [])
            if steps:
                @pl.when(t == when)
                def _():
                    for s in steps:
                        s()
        return carry
    lax.fori_loop(0, n_t, tile, 0)
    stat[...] = stat[...] + stat_two[...]
    late(stat)
    gout(n_t - 1).wait()


def collect_plan(gw, outs, refs):
    parts, stat_ref = outs[0], outs[4]
    sem = refs[0]

    def emit(u):
        def go():
            c = pltpu.make_async_copy(gw.at[u % 2], parts.at[u], sem)
            c.start()
            c.wait()
        return go

    def late(stat):
        stat_ref[...] = stat[...]
    return {u: [emit(u)] for u in range(U_END)}, late


def reduce_plan(gw, outs, refs):
    fc_t, proj_t, out_t, qkv_t, stat_ref = outs
    recv, local, (fcp, stage, came, sems, ssem) = refs[:4], refs[4:9], refs[9:]
    small, width = out_t.shape
    last = qkv_t.shape[1] - 2 * width
    place = ReducePlace()
    enter(place)
    dest = [fcp.at[u] for u in range(N_FF)] + [out_t] + [proj_t.at[pl.ds(u * small, small), :] for u in range(N_FF)] + [
        qkv_t.at[:, pl.ds(0, width)], qkv_t.at[:, pl.ds(width, width)], qkv_t.at[:, pl.ds(2 * width, last)]]
    pieces = []
    for u in range(U_END):
        whole = dest[u].shape[1] == width
        pick = lambda ref, *at: ref.at[at] if whole else ref.at[at + (slice(None),) * (len(ref.shape) - len(at) - 2) + (pl.ds(0, LAST_ROWS),)]
        bufs = [pick(b, u) for b in recv], [pick(b, u % (RING_1 if i < 2 else RING_2)) for i, b in enumerate(local)]
        pieces.append(Piece(place, pick(gw, u % 2), dest[u], *bufs, sems.at[u]))
    todo = [(u + d, -k, u) for u in range(U_END) for k, d in enumerate(DELAYS)]
    todo.sort(key=lambda e: (e[0], e[1] if e[1] else -9, e[2]))
    plan, rest = {}, []
    for when, neg, u in todo:
        step = getattr(pieces[u], "t%d" % -neg)
        if when < U_END + 4:
            plan.setdefault(when, []).append(step)
        else:
            rest.append(step)
    sums = Sum(place, stage, came, ssem)

    def late(stat):
        stage[0] = stat[...]
        sums.hop(0).start()
        between = [lambda: sums.step(0), lambda: sums.step(1), lambda: sums.step(2)]
        fc_t[...] = spread_groups([fcp[j] for j in range(N_FF)], width // small, small)
        for step in rest:
            step()
            if between:
                between.pop(0)()
        for step in between:
            step()
        stat_ref[...] = sums.finish()
    return plan, late


def grads(remote, tokens, ghid, gq, gk, gv, w, act, gi, n2, cot, att, gb, gs, stat):
    n, width = tokens.shape
    fresh = w.shape[1] - 2 * width
    small = 24
    ff = act.shape[0] * width
    s, dma = jax.ShapeDtypeStruct, pltpu.SemaphoreType.DMA
    any_, vm = pl.BlockSpec(memory_space=pl.ANY), pl.BlockSpec(memory_space=pltpu.VMEM)
    block = (2 * small, width // 2)
    outs = [s((n, width), F32)]
    scratch = [pltpu.VMEM((6, n, width), BF16), pltpu.VMEM((2, 16, 2) + block, BF16), pltpu.VMEM(w.shape, BF16), pltpu.VMEM((2, TILE, width), F32),
               pltpu.VMEM((8, width), F32), dma((7,)), dma((2,)), dma((2,))]
    params = dict(vmem_limit_bytes=VMEM_BYTES)
    if remote:
        outs += [s((small, ff), F32), s((ff // 32, width), F32), s((small, width), F32), s((small, w.shape[1]), F32)]
        specs = [vm] * 4
        scratch += [pltpu.VMEM((U_END, k) + block, BF16) for k in RECV]
        scratch += [pltpu.VMEM((r, k) + block, d) for r, k, d in ((RING_1, 8, BF16), (RING_1, 8, F32), (RING_2, 4, BF16), (RING_2, 4, F32), (RING_2, 3, BF16))]
        scratch += [pltpu.VMEM((N_FF, small, width), F32), pltpu.VMEM((4, 8, width), F32), pltpu.VMEM((6, 8, width), F32), dma((U_END, 2, 6)), dma((2, 6))]
        params.update(collective_id=2, has_side_effects=True)
    else:
        outs += [s((U_END, 16, 2) + block, BF16)] + [s((8, 128), F32)] * 3
        specs = [any_] * 4
        scratch += [dma(())]
    return pl.pallas_call(
        functools.partial(grads_kernel, remote), in_specs=[any_] * 12 + [vm] * 2, out_specs=[any_] + specs + [vm],
        out_shape=outs + [s((8, width), F32)], scratch_shapes=scratch,
        compiler_params=pltpu.CompilerParams(**params), name="grads",
    )(tokens, ghid, gq, gk, gv, w, act, gi, n2, cot, att, gb, gs, stat)


def unpack_parts(parts, width, fresh):
    p = parts.astype(F32).reshape(U_END, width // 24, 2, 24, width // 2).transpose(0, 1, 3, 2, 4).reshape(U_END, width, width)
    return (jnp.concatenate([p[U_Q], p[U_Q + 1], p[U_Q + 2, :, :fresh]], axis=1), p[U_OUT], jnp.concatenate(list(p[:N_FF]), axis=1),
            p[U_PROJ:U_Q].reshape(-1, width))


def finish_kernel(tok, fc, proj, out, qkv, stat, tok_o, fc_o, proj_o, out_o, qkv_o, gain_o, shift_o):
    tok_o[...] = tok[...]

    @pl.when(pl.program_id(0) == 0)
    def _():
        fc_o[...], proj_o[...], out_o[...], qkv_o[...] = fc[...], proj[...], out[...], qkv[...]
        width, own = stat.shape[1], gain_o.shape[1]
        mine = pltpu.roll(stat[...], lax.rem(width - own * lax.axis_index(AXES), width), 1)
        gain_o[...] = mine[0:2, :own]
        shift_o[...] = mine[2:4, :own]


def finish(tok, fc, proj, out, qkv, stat, own):
    small = jax.ShapeDtypeStruct((2, own), F32)
    args = (fc, proj, out, qkv, stat)
    outs = [jax.ShapeDtypeStruct(a.shape, F32) for a in args[:4]] + [small, small]
    tile = pl.BlockSpec((TILE // 2, tok.shape[1]), lambda t: (t, 0))
    whole = lambda a: pl.BlockSpec(a.shape, lambda t: (0, 0))
    return pl.pallas_call(
        finish_kernel, grid=(tok.shape[0] * 2 // TILE,), in_specs=[tile] + [whole(a) for a in args], out_specs=[tile] + [whole(a) for a in outs],
        out_shape=[jax.ShapeDtypeStruct(tok.shape, F32)] + outs, name="finish",
    )(tok, *args)


def body(direct, tokens, skip_values, w_qkv, w_out, w_fc, w_proj, norm_gains, norm_shifts, segment_ids, pad_mask, cotangent):
    micro, rows, length, width = tokens.shape
    half, ff = skip_values.shape[3], w_fc.shape[1]
    seqs = micro * rows
    n = seqs * length
    own = norm_gains.shape[1]
    flat = lambda a: a.reshape(n, a.shape[-1])
    seq = lambda a: a.reshape(seqs, length, a.shape[-1])
    tok, skip, cot = flat(tokens), flat(skip_values), flat(cotangent)
    seg, pad = segment_ids.reshape(seqs, 1, length), pad_mask.reshape(seqs, 1, length)
    if direct:
        q, k, v, gs, fcp, _, qkv, out, fc0, proj0 = start(tok, skip, norm_gains, norm_shifts, w_qkv, w_out, w_fc, w_proj)
        weights = (fc0, proj0, fcp, w_proj)
    else:
        qkv, out, *weights = [lax.all_gather(w, AXES, axis=0, tiled=True) for w in (w_qkv, w_out, w_fc, w_proj)]
        rows8 = jnp.concatenate([norm_gains, norm_shifts, jnp.zeros((4, own), BF16)], axis=0)
        gs = lax.all_gather(rows8, AXES, axis=1, tiled=True).astype(F32)
        q, k, v = project(tok, skip, qkv, gs)
    att, lse = attend(seq(q), seq(k), seq(v), seg, pad)
    att = flat(att)
    lout, ghid, gatt, n2, gb, act, gi, stat = mlp(direct, tok, att, cot, out, weights, gs)
    gq, gk, gv, gskip, lout = attend_back(seq(q), seq(k), seq(v), seq(gatt), lse, seg, pad, seq(lout), half)
    gtok, gfc, gproj, gout, gqkv, stat = grads(
        direct, tok, ghid, flat(gq), flat(gk), flat(gv), qkv, act, gi, n2, cot, att, gb, gs, stat)
    if direct:
        gtok, total_fc, total_proj, total_out, total_qkv, gains, shifts = finish(gtok, gfc, gproj, gout, gqkv, stat, own)
    else:
        total_qkv, total_out, total_fc, total_proj = [
            lax.psum_scatter(g, AXES, scatter_dimension=0, tiled=True) for g in unpack_parts(gfc, width, width - half)]
        gains = lax.psum_scatter(stat[0:2], AXES, scatter_dimension=1, tiled=True)
        shifts = lax.psum_scatter(stat[2:4], AXES, scatter_dimension=1, tiled=True)
    shape4 = lambda a: a.reshape(micro, rows, length, a.shape[-1])
    return (shape4(lout), shape4(gtok), shape4(gskip), total_qkv, total_out, total_fc, total_proj, gains, shifts)


def solution(mesh):
    tok, mat, row, ids = P(None, AXES, None, None), P(AXES, None), P(None, AXES), P(None, AXES, None)
    direct = dict(mesh.shape) == {"dp": 2, "fsdp": 16}
    return jax.shard_map(
        functools.partial(body, direct), mesh=mesh,
        in_specs=(tok, tok, mat, mat, mat, mat, row, row, ids, ids, tok),
        out_specs=(tok, tok, tok, mat, mat, mat, mat, row, row), check_vma=False)
```

```python
import functools
import jax
import jax.numpy as jnp
from jax import lax
from jax.experimental import pallas as pl
from jax.experimental.pallas import tpu as pltpu
from jax.sharding import PartitionSpec as P

F32, BF16 = jnp.float32, jnp.bfloat16

HEAD = 64
BLK = 128
WIN = 5
MASKED = -1e9
PAIRS_FWD, PAIRS_BWD = 6, 3


def build_bias(seg_row, pad_row, bias_ref, n_blk):
    code = jnp.where(pad_row == 1, seg_row, -1)
    key = lax.broadcasted_iota(jnp.int32, (BLK, BLK), 0)
    row = lax.broadcasted_iota(jnp.int32, (BLK, BLK), 1)
    for kb in range(n_blk):
        code_k = jnp.broadcast_to(code[:, kb * BLK:(kb + 1) * BLK], (BLK, BLK)).T
        for qb in range(kb, min(kb + WIN, n_blk)):
            vis = code_k == seg_row[:, qb * BLK:(qb + 1) * BLK]
            if kb == qb:
                vis = (vis & (key < row)) | (key == row)
            t = kb - qb + WIN - 1
            bias_ref[qb, t * BLK:(t + 1) * BLK, :] = jnp.where(vis, 0.0, MASKED)


def stack_heads(x):
    low = lax.broadcasted_iota(jnp.int32, x.shape, 1) < HEAD
    zero = jnp.zeros_like(x)
    return jnp.concatenate([jnp.where(low, x, zero), jnp.where(low, zero, x)], axis=0)


def join_heads(x2):
    return jnp.concatenate([x2[:HEAD, :BLK], x2[HEAD:, BLK:]], axis=0)


def twice(x):
    return jnp.concatenate([x, x], axis=1)


def visible_blocks(seg_s, row, qb):
    first = seg_s[row, 0, qb * BLK]
    n = jnp.int32(1)
    for back in range(1, WIN):
        kb = jnp.maximum(qb - back, 0)
        seen = (qb >= back) & (seg_s[row, 0, kb * BLK + BLK - 1] == first)
        n = n + seen.astype(jnp.int32)
    return n


def over_queries(seg_s, row, n_blk, one):
    def step(qb, carry):
        n_vis = visible_blocks(seg_s, row, qb)
        for n in range(1, WIN + 1):
            @pl.when(n_vis == n)
            def _():
                one(n, qb)
        return carry
    lax.fori_loop(0, n_blk, step, 0)


def block(i, n=1):
    return pl.ds(pl.multiple_of(i * BLK, BLK), n * BLK)


def attend_nt(a, b):
    return lax.dot_general(a, b, (((1,), (1,)), ((), ())), preferred_element_type=F32)


def fwd_kernel(n_blk, pairs, seg_s, seg_ref, pad_ref, q_ref, k_ref, v_ref, o_ref, lse_ref, bias_ref, vt_ref):
    row = pl.program_id(0)

    @pl.when(pl.program_id(1) == 0)
    def _():
        build_bias(seg_ref[...], pad_ref[...], bias_ref, n_blk)

    lanes = [slice(i * BLK, (i + 1) * BLK) for i in range(pairs)]
    for kb in range(n_blk):
        for h in lanes:
            vt_ref[h, kb * BLK:(kb + 1) * BLK] = v_ref[kb * BLK:(kb + 1) * BLK, h].T

    def one(n, qb):
        keys, here = block(qb - n + 1, n), block(qb)
        b = twice(bias_ref[qb, (WIN - n) * BLK:, :])
        s = [attend_nt(k_ref[keys, h], stack_heads(q_ref[here, h])) + b for h in lanes]
        for i, h in enumerate(lanes):
            m = jnp.max(s[i], axis=0, keepdims=True)
            p = jnp.exp(s[i] - m)
            total = jnp.sum(p, axis=0, keepdims=True)
            o2 = jnp.dot(vt_ref[h, keys], p.astype(BF16), preferred_element_type=F32) * (1.0 / total)
            o_ref[here, h] = join_heads(o2).astype(BF16).T
            lse_ref[i, qb] = m + jnp.log(total)
    over_queries(seg_s, row, n_blk, one)


def attend(q, k, v, seg, pad):
    rows, length, width = q.shape
    n_blk, pairs = length // BLK, PAIRS_FWD
    groups = width // 128 // pairs
    tok = pl.BlockSpec((None, length, pairs * 128), lambda r, h, s: (r, 0, h))
    ids = pl.BlockSpec((None, 1, length), lambda r, h, s: (r, 0, 0))
    return pl.pallas_call(
        functools.partial(fwd_kernel, n_blk, pairs),
        grid_spec=pltpu.PrefetchScalarGridSpec(
            num_scalar_prefetch=1, grid=(rows, groups),
            in_specs=[ids, ids, tok, tok, tok],
            out_specs=[tok, pl.BlockSpec((None, pairs, n_blk, 1, 2 * BLK), lambda r, h, s: (r, h, 0, 0, 0))],
            scratch_shapes=[pltpu.VMEM((n_blk, WIN * BLK, BLK), F32), pltpu.VMEM((pairs * BLK, length), BF16)]),
        out_shape=[jax.ShapeDtypeStruct((rows, length, width), BF16), jax.ShapeDtypeStruct((rows, width // 128, n_blk, 1, 2 * BLK), F32)],
        compiler_params=pltpu.CompilerParams(dimension_semantics=("arbitrary", "arbitrary"), vmem_limit_bytes=64000 << 10),
        name="attend",
    )(seg, seg, pad, q, k, v)


def bwd_kernel(n_blk, pairs, seg_s, seg_ref, pad_ref, q_ref, k_ref, v_ref, g_ref, lse_ref, result_ref, dq_ref, dk_ref, dv_ref, dskip_ref, result_out,
               bias_ref, kt_ref, dk_acc, dv_acc):
    row = pl.program_id(0)
    result_out[...] = result_ref[...]

    @pl.when(pl.program_id(1) == 0)
    def _():
        build_bias(seg_ref[...], pad_ref[...], bias_ref, n_blk)

    lanes = [slice(i * BLK, (i + 1) * BLK) for i in range(pairs)]
    for kb in range(n_blk):
        for h in lanes:
            kt_ref[h, kb * BLK:(kb + 1) * BLK] = k_ref[kb * BLK:(kb + 1) * BLK, h].T
    dk_acc[...] = jnp.zeros_like(dk_acc)
    dv_acc[...] = jnp.zeros_like(dv_acc)

    def one(n, qb):
        keys, here = block(qb - n + 1, n), block(qb)
        b = twice(bias_ref[qb, (WIN - n) * BLK:, :])
        for i, h in enumerate(lanes):
            q2, g2 = stack_heads(q_ref[here, h]), stack_heads(g_ref[here, h])
            p = jnp.exp(attend_nt(k_ref[keys, h], q2) + b - lse_ref[i, qb])
            dp = attend_nt(v_ref[keys, h], g2)
            inner = jnp.sum(p * dp, axis=0, keepdims=True)
            ds = (p * (dp - inner)).astype(BF16)
            dv_acc[keys, h] += jnp.dot(p.astype(BF16), g2, preferred_element_type=F32)
            dk_acc[keys, h] += jnp.dot(ds, q2, preferred_element_type=F32)
            dq2 = jnp.dot(kt_ref[h, keys], ds, preferred_element_type=F32)
            dq_ref[here, h] = (join_heads(dq2) * 0.125).astype(BF16).T
    over_queries(seg_s, row, n_blk, one)
    dk_ref[...] = dk_acc[...].astype(BF16)
    dv_ref[...] = dv_acc[...].astype(BF16)

    @pl.when(pl.program_id(1) == pl.num_programs(1) - 1)
    def _():
        dskip_ref[...] = dv_ref[:, dv_ref.shape[1] - dskip_ref.shape[1]:].astype(F32)


def attend_back(q, k, v, g, lse, seg, pad, result, half):
    rows, length, width = q.shape
    n_blk, pairs = length // BLK, PAIRS_BWD
    groups = width // 128 // pairs
    tok = pl.BlockSpec((None, length, pairs * 128), lambda r, h, s: (r, 0, h))
    ids = pl.BlockSpec((None, 1, length), lambda r, h, s: (r, 0, 0))
    out = jax.ShapeDtypeStruct((rows, length, width), BF16)
    return pl.pallas_call(
        functools.partial(bwd_kernel, n_blk, pairs),
        grid_spec=pltpu.PrefetchScalarGridSpec(
            num_scalar_prefetch=1, grid=(rows, groups),
            in_specs=[ids, ids, tok, tok, tok, tok, pl.BlockSpec((None, pairs, n_blk, 1, 2 * BLK), lambda r, h, s: (r, h, 0, 0, 0)), tok],
            out_specs=[tok, tok, tok, pl.BlockSpec((None, length, half), lambda r, h, s: (r, 0, 0)), tok],
            scratch_shapes=[pltpu.VMEM((n_blk, WIN * BLK, BLK), F32), pltpu.VMEM((pairs * BLK, length), BF16),
                            pltpu.VMEM((length, pairs * BLK), F32), pltpu.VMEM((length, pairs * BLK), F32)]),
        out_shape=[out, out, out, jax.ShapeDtypeStruct((rows, length, half), F32), out],
        compiler_params=pltpu.CompilerParams(dimension_semantics=("arbitrary", "arbitrary"), vmem_limit_bytes=64000 << 10),
        name="attend_back",
    )(seg, seg, pad, q, k, v, g, lse, result)


MESH = pl.DeviceIdType.MESH
NZ = 4


class Place:
    def __init__(self):
        dp, fs = lax.axis_index("dp"), lax.axis_index("fsdp")
        self.x, self.z, self.y, self.c = dp, fs // 4, (fs // 2) % 2, fs % 2
        self.slot = self.x * 16 + fs
        self.first = self.id(x=jnp.where(self.c == 0, 1 - self.x, self.x), y=jnp.where(self.c == 0, self.y, 1 - self.y))
        self.second = self.id(x=jnp.where(self.c == 0, self.x, 1 - self.x), y=jnp.where(self.c == 0, 1 - self.y, self.y))
        self.partner = self.id(c=1 - self.c)

    def id(self, x=None, y=None, z=None, c=None):
        x = self.x if x is None else x
        y = self.y if y is None else y
        z = self.z if z is None else z
        c = self.c if c is None else c
        return (x, z * 4 + y * 2 + c)

    def z_at(self, k):
        return (self.z + k) % NZ

    def peers(self):
        return [self.partner, self.first, self.second] + [self.id(z=self.z_at(k)) for k in (1, 2, 3)]

    def slot_of(self, df, ds, z):
        dx = jnp.where(self.c == 0, df, ds)
        dy = jnp.where(self.c == 0, ds, df)
        x = jnp.where(dx == 1, 1 - self.x, self.x)
        y = jnp.where(dy == 1, 1 - self.y, self.y)
        return x * 16 + z * 4 + y * 2 + self.c


def enter(place):
    bar = pltpu.get_barrier_semaphore()
    for peer in place.peers():
        pl.semaphore_signal(bar, inc=1, device_id=peer, device_id_type=MESH)
    pl.semaphore_wait(bar, 6)


class Gather:
    SENDS = 31

    def __init__(self, place, shard, out, send, recv, own):
        self.p, self.shard, self.out, self.send, self.recv, self.own = place, shard, out, send, recv, own
        self.size = shard.shape[0]

    def at(self, slot, n=1):
        return self.out.at[pl.ds(pl.multiple_of(slot * self.size, 8), n * self.size), :]

    def push(self, src, slot, to):
        pltpu.make_async_remote_copy(src_ref=src, dst_ref=self.at(slot), send_sem=self.send, recv_sem=self.recv.at[slot],
                                     device_id=to, device_id_type=MESH).start()

    def arrived(self, slot):
        pltpu.make_async_copy(self.at(slot), self.at(slot), self.recv.at[slot]).wait()

    def keep(self, slot):
        return pltpu.make_async_copy(self.shard, self.at(slot), self.own)

    def s1(self):
        p = self.p
        self.keep(p.slot).start()
        for k in (1, 3, 2):
            self.push(self.shard, p.slot, p.id(z=p.z_at(k)))
        for to in (p.first, p.partner, p.second):
            self.push(self.shard, p.slot, to)

    def s2(self):
        p = self.p
        for k in (1, 3, 2):
            slot = p.slot_of(0, 0, p.z_at(k))
            self.arrived(slot)
            for to in (p.first, p.second, p.partner):
                self.push(self.at(slot), slot, to)

    def s3(self):
        p = self.p
        for k in (0, 1, 3, 2):
            slot = p.slot_of(1, 0, p.z_at(k))
            self.arrived(slot)
            for to in (p.second, p.partner):
                self.push(self.at(slot), slot, to)

    def s4(self):
        p = self.p
        for df in (0, 1):
            for k in (0, 1, 3, 2):
                slot = p.slot_of(df, 1, p.z_at(k))
                self.arrived(slot)
                self.push(self.at(slot), slot, p.partner)

    def s5(self):
        for k in range(16):
            self.arrived(2 * k + 1 - self.p.c)
        self.keep(self.p.slot).wait()

    def drain(self):
        done = self.at(0, self.SENDS)
        pltpu.make_async_copy(done, done, self.send).wait()


VMEM_BYTES = 64000 << 10
TILE = 512
EPS = 1e-5
GELU_C = 0.7978845608028654
GELU_A = 0.044715


def dot(a, b):
    return jnp.dot(a, b, preferred_element_type=F32)


def dot_nt(a, b):
    return lax.dot_general(a, b, (((1,), (1,)), ((), ())), preferred_element_type=F32)


def dot_tn(a, b):
    return lax.dot_general(a, b, (((0,), (0,)), ((), ())), preferred_element_type=F32)


def normalise(v):
    centred = v - jnp.mean(v, axis=-1, keepdims=True)
    rstd = lax.rsqrt(jnp.mean(centred * centred, axis=-1, keepdims=True) + EPS)
    return centred * rstd, rstd


def norm_back(g, xhat, rstd, gain):
    gh = g * gain
    return rstd * (gh - jnp.mean(gh, axis=-1, keepdims=True) - xhat * jnp.mean(gh * xhat, axis=-1, keepdims=True))


def gelu_both(u, grad):
    sq = u * u
    t = jnp.tanh(u * (GELU_C + (GELU_C * GELU_A) * sq))
    half = 0.5 + 0.5 * t
    act = u * half
    slope = half + act * (1.0 - half) * (2.0 * GELU_C + (6.0 * GELU_C * GELU_A) * sq)
    return act, grad * slope


def tile_at(t):
    return pl.ds(pl.multiple_of(t * TILE, TILE), TILE)


def qkv_kernel(tok_ref, skip_ref, w_ref, gs_ref, q_ref, k_ref, v_ref):
    width, half = tok_ref.shape[1], skip_ref.shape[1]
    xhat, _ = normalise(tok_ref[...].astype(F32))
    normed = (xhat * gs_ref[0:1, :] + gs_ref[2:3, :]).astype(BF16)
    q_ref[...] = (dot(normed, w_ref[:, :width]) * 0.125).astype(BF16)
    k_ref[...] = dot(normed, w_ref[:, width:2 * width]).astype(BF16)
    v_ref[:, :half] = dot(normed, w_ref[:, 2 * width:]).astype(BF16)
    v_ref[:, half:] = skip_ref[...]


def project(tokens, skip, w, gs):
    n, width = tokens.shape
    row = lambda c: pl.BlockSpec((TILE, c), lambda t: (t, 0))
    whole = lambda a: pl.BlockSpec(a.shape, lambda t: (0, 0))
    out = jax.ShapeDtypeStruct((n, width), BF16)
    return pl.pallas_call(
        qkv_kernel, grid=(n // TILE,), in_specs=[row(width), row(skip.shape[1]), whole(w), whole(gs)],
        out_specs=[row(width)] * 3, out_shape=[out] * 3,
        compiler_params=pltpu.CompilerParams(vmem_limit_bytes=VMEM_BYTES), name="project",
    )(tokens, skip, w, gs)


def lane_mod(x, period):
    return jnp.broadcast_to(lax.rem(lax.broadcasted_iota(jnp.int32, (1, x.shape[1]), 1), jnp.int32(period)), x.shape)


def gather_groups(x, groups, size, parts):
    out = []
    total = x.shape[1]
    for j in range(parts):
        y = pltpu.roll(x, total - j * size, 1) if j else x
        span = size
        while span < groups * size:
            m = lane_mod(y, 2 * parts * span)
            y = jnp.where((m >= span) & (m < 2 * span), pltpu.roll(y, total - (parts - 1) * span, 1), y)
            span *= 2
        out.append(y[:, :groups * size])
    return out


def spread_groups(pieces, groups, size):
    parts = len(pieces)
    out = None
    for j, piece in enumerate(pieces):
        y = jnp.concatenate([piece] + [jnp.zeros_like(piece)] * (parts - 1), axis=1)
        span = groups * size
        while span > size:
            span //= 2
            m = lane_mod(y, 2 * parts * span)
            y = jnp.where((m >= parts * span) & (m < (parts + 1) * span), pltpu.roll(y, (parts - 1) * span, 1), y)
        y = pltpu.roll(y, j * size, 1) if j else y
        m = lane_mod(y, parts * size)
        y = jnp.where((m >= j * size) & (m < (j + 1) * size), y, 0.0)
        out = y if out is None else out + y
    return out


N_FF = 4


def start_kernel(tok_h, skip_h, gain_ref, shift_ref, qkv_ref, out_ref, fc_ref, proj_h,
                 q_h, k_h, v_h, gs_ref, fcp_ref, gs_all, qkv_all, out_all, fc_all, proj_all,
                 tok, skip, xhat, w, gsb, q, k, v, normed, rows_ref, insem, osem, send, recv, own):
    n, width = tok.shape
    half = skip.shape[1]
    n_t = n // TILE
    n_dev = qkv_all.shape[0] // qkv_ref.shape[0]
    size = proj_h.shape[0] // N_FF
    place = Place()
    loads = [pltpu.make_async_copy(tok_h, tok, insem.at[0]), pltpu.make_async_copy(skip_h, skip, insem.at[1])]
    for c in loads:
        c.start()
    enter(place)
    cols = [pl.ds(0, width), pl.ds(width, width), pl.ds(2 * width, half)]
    shards = (rows_ref, *[qkv_ref.at[:, c] for c in cols], out_ref, fcp_ref.at[0], proj_h.at[pl.ds(0, size), :])
    outs = (gs_all, *[qkv_all.at[:, c] for c in cols], out_all, fc_all, proj_all)
    jobs = [Gather(place, s, o, send.at[i], recv.at[i], own.at[i]) for i, (s, o) in enumerate(zip(shards, outs))]
    rows, wq, wk, wv, out, fc, proj = jobs
    wq.s1()
    mine = jnp.concatenate([gain_ref[...], shift_ref[...]], axis=0)
    lane = lax.broadcasted_iota(jnp.int32, (mine.shape[1], width), 1) - mine.shape[1] * place.slot
    spot = (lane == lax.broadcasted_iota(jnp.int32, lane.shape, 0)).astype(BF16)
    rows_ref[0:4, :] = dot(mine, spot).astype(BF16)
    rows_ref[4:8, :] = jnp.zeros((4, width), BF16)
    wk.s1(), wv.s1()
    for j, piece in enumerate(gather_groups(fc_ref[...].astype(F32), n_dev, size, N_FF)):
        fcp_ref[j] = piece.astype(BF16)
    rows.s1()
    for c in loads:
        c.wait()

    def centre(t, carry):
        r = tile_at(t)
        xhat[r, :], _ = normalise(tok[r, :].astype(F32))
        return carry
    lax.fori_loop(0, n_t // 2, centre, 0)
    wq.s2(), wk.s2(), wv.s2(), rows.s2(), out.s1()
    wq.s3(), wk.s3(), rows.s3(), wv.s3()
    lax.fori_loop(n_t // 2, n_t, centre, 0)
    fc.s1(), proj.s1()
    wq.s4(), rows.s4(), wk.s4(), out.s2(), wq.s5(), rows.s5()
    wloads = [pltpu.make_async_copy(qkv_all.at[:, c], w.at[:, c], insem.at[4 + i]) for i, c in enumerate(cols)]
    gload = pltpu.make_async_copy(gs_all, gsb, insem.at[3])
    wloads[0].start(), gload.start()
    wv.s4(), fc.s2(), proj.s2()
    gload.wait()
    gs_ref[...] = jnp.sum(gsb[...].astype(F32).reshape(n_dev, 8, width), axis=0)
    wloads[0].wait()

    def copies(r):
        return [pltpu.make_async_copy(s.at[r, :], h.at[r, :], osem.at[i]) for i, (s, h) in enumerate([(q, q_h), (k, k_h), (v, v_h)])]

    def third(i, put):
        def tile(t, carry):
            r = tile_at(t)
            put(r)
            copies(r)[i].start()
            return carry
        lax.fori_loop(0, n_t, tile, 0)

    def put_q(r):
        normed[r, :] = (xhat[r, :] * gs_ref[0:1, :] + gs_ref[2:3, :]).astype(BF16)
        q[r, :] = (dot(normed[r, :], w[:, :width]) * 0.125).astype(BF16)

    def put_k(r):
        k[r, :] = dot(normed[r, :], w[:, width:2 * width]).astype(BF16)

    def put_v(r):
        v[r, :half] = dot(normed[r, :], w[:, 2 * width:]).astype(BF16)
        v[r, half:] = skip[r, :]
    third(0, put_q)
    out.s3(), wk.s5()
    wloads[1].start()
    wv.s5()
    wloads[2].start()
    fc.s3()
    wloads[1].wait()
    third(1, put_k)
    proj.s3(), out.s4()
    wloads[2].wait()
    third(2, put_v)
    fc.s4(), out.s5(), proj.s4(), fc.s5(), proj.s5()
    for job in jobs:
        job.drain()
    for c in copies(pl.ds(0, n)):
        c.wait()


def start(tokens, skip, gains, shifts, qkv, out, fc, proj):
    n, width = tokens.shape
    n_dev = width // out.shape[0]
    s, dma = jax.ShapeDtypeStruct, pltpu.SemaphoreType.DMA
    any_, vm = pl.BlockSpec(memory_space=pl.ANY), pl.BlockSpec(memory_space=pltpu.VMEM)
    big = lambda d: pltpu.VMEM((n, width), d)
    act = s((n, width), BF16)
    gathered = [(8 * n_dev, width), (width, qkv.shape[1]), (width, width), (width, width), (width, width)]
    return pl.pallas_call(
        start_kernel, in_specs=[any_, any_] + [vm] * 5 + [any_], out_specs=[any_] * 3 + [vm] * 2 + [any_] * 5,
        out_shape=[act] * 3 + [s((8, width), F32), s((N_FF, fc.shape[0], width), BF16)] + [s(g, BF16) for g in gathered],
        scratch_shapes=[big(BF16), pltpu.VMEM(skip.shape, BF16), big(F32), pltpu.VMEM((width, qkv.shape[1]), BF16), pltpu.VMEM((8 * n_dev, width), BF16),
                        big(BF16), big(BF16), big(BF16), big(BF16), pltpu.VMEM((8, width), BF16), dma((7,)), dma((3,)), dma((7,)), dma((7, n_dev)), dma((7,))],
        compiler_params=pltpu.CompilerParams(vmem_limit_bytes=VMEM_BYTES, collective_id=0, has_side_effects=True), name="start",
    )(tokens, skip, gains, shifts, qkv, out, fc, proj)


MLP_STEPS = {1: (-1, 0, 1, 2), 2: (0, 2, 4, 6), 3: (2, 4, 6, 8)}


def mlp_kernel(remote, tok_h, att_h, cot_h, wout_h, *refs):
    if remote:
        fc0_h, proj0_h, fcp_ref, proj_ref, *refs = refs
    else:
        wfc_h, wproj_h, *refs = refs
    (gs_ref, lout_h, ghid_h, gatt_h, n2_h, gb_h, act_h, gi_h, stat_ref), refs = refs[:9], refs[9:]
    if remote:
        (fc_all, proj_all), refs = refs[:2], refs[2:]
    (tok, att, cot, hidden, oacc, gacc, n2, gb, wout, wfc, wproj, act, gi, insem, wsem, asem, osem), sems = refs[:17], refs[17:]
    n, width = tok.shape
    n_ff = N_FF
    n_t = n // TILE
    gain, shift = gs_ref[1:2, :], gs_ref[3:4, :]

    def load(src_fc, src_proj, slot):
        return (pltpu.make_async_copy(src_fc, wfc.at[slot], wsem.at[0, slot]), pltpu.make_async_copy(src_proj, wproj.at[slot], wsem.at[1, slot]))

    loads = [pltpu.make_async_copy(h, v, insem.at[i]) for i, (h, v) in enumerate([(wout_h, wout), (att_h, att), (tok_h, tok), (cot_h, cot)])]
    for c in loads:
        c.start()
    plan = {}
    if remote:
        send, recv, own = sems
        place = Place()
        enter(place)
        size = proj_ref.shape[0] // n_ff
        sets = []
        for i in range(1, n_ff):
            srcs = (fcp_ref.at[i], proj_ref.at[pl.ds(i * size, size), :])
            sets.append([Gather(place, srcs[k], (fc_all, proj_all)[k].at[i - 1], send.at[i - 1, k], recv.at[i - 1, k], own.at[i - 1, k]) for k in range(2)])

        def run(i, step):
            return lambda: [getattr(job, step)() for job in sets[i - 1]]

        def fetch(i):
            def go():
                for c in load(fc_all.at[i - 1], proj_all.at[i - 1], i % 2):
                    c.start()
            return go
        for i in range(1, n_ff):
            run(i, "s1")()
        early = []
        for i, steps in MLP_STEPS.items():
            for when, name in zip(steps, ("s2", "s3", "s4", "s5")):
                (early if when < 0 else plan.setdefault(when, [])).append(run(i, name))
            plan[steps[3]].append(fetch(i))
        for c in load(fc0_h, proj0_h, 0):
            c.start()
    else:
        early = []
        cols = lambda j: pl.ds(j * width, width)
        for i in range(1, n_ff):
            def fetch(i=i):
                for c in load(wfc_h.at[:, cols(i)], wproj_h.at[cols(i), :], i % 2):
                    c.start()
            plan[(i - 1) * n_t + 3] = [fetch]
        for c in load(wfc_h.at[:, cols(0)], wproj_h.at[cols(0), :], 0):
            c.start()
    for c in loads[:3]:
        c.wait()

    def out_copy(v, h, r, i):
        return pltpu.make_async_copy(v.at[r, :], h.at[r, :], osem.at[i])

    def forward(t, carry):
        r = tile_at(t)
        h = tok[r, :].astype(F32) + dot(att[r, :], wout[...])
        hidden[r, :] = h
        oacc[r, :] = h
        gacc[r, :] = jnp.zeros_like(h)
        xhat, _ = normalise(h)
        n2[r, :] = (xhat * gain + shift).astype(BF16)
        out_copy(n2, n2_h, r, 3).start()
        return carry
    lax.fori_loop(0, n_t, forward, 0)
    for step in early:
        step()
    loads[3].wait()

    def saves(i, t, slot):
        return (pltpu.make_async_copy(act.at[slot], act_h.at[i, tile_at(t), :], asem.at[0, slot]),
                pltpu.make_async_copy(gi.at[slot], gi_h.at[i, tile_at(t), :], asem.at[1, slot]))

    def tile(step, carry):
        i, t, slot = step // n_t, step % n_t, step % 2
        ws = i % 2
        r = tile_at(t)

        @pl.when(t == 0)
        def _():
            for c in load(wfc.at[ws], wproj.at[ws], ws):
                c.wait()

        @pl.when(step >= 2)
        def _():
            for c in saves(i, t, slot):
                c.wait()
        a, g = gelu_both(dot(n2[r, :], wfc[ws]), dot_nt(cot[r, :], wproj[ws]))
        a, g = a.astype(BF16), g.astype(BF16)
        act[slot] = a
        gi[slot] = g
        oacc[r, :] += dot(a, wproj[ws])
        gacc[r, :] += dot_nt(g, wfc[ws])
        for c in saves(i, t, slot):
            c.start()
        for when, steps in plan.items():
            @pl.when(step == when)
            def _():
                for s in steps:
                    s()
        return carry
    lax.fori_loop(0, n_ff * n_t, tile, 0)
    stat_ref[...] = jnp.zeros_like(stat_ref)

    def backward(t, carry):
        r = tile_at(t)
        tok[r, :] = oacc[r, :].astype(BF16)
        xhat, rstd = normalise(hidden[r, :])
        g = gacc[r, :]
        stat_ref[1:2, :] += jnp.sum(g * xhat, axis=0, keepdims=True)
        stat_ref[3:4, :] += jnp.sum(g, axis=0, keepdims=True)
        gh = cot[r, :].astype(F32) + norm_back(g, xhat, rstd, gain)
        hidden[r, :] = gh
        b = gh.astype(BF16)
        gb[r, :] = b
        att[r, :] = dot_nt(b, wout[...]).astype(BF16)
        for i, (v, h) in enumerate([(tok, lout_h), (hidden, ghid_h), (att, gatt_h)]):
            out_copy(v, h, r, i).start()
        out_copy(gb, gb_h, r, 4).start()
        return carry
    lax.fori_loop(0, n_t, backward, 0)
    if remote:
        for job in sets[0] + sets[1] + sets[2]:
            job.drain()
    for slot in range(2):
        for c in saves(0, 0, slot):
            c.wait()
    for i, (v, h) in enumerate([(tok, lout_h), (hidden, ghid_h), (att, gatt_h), (n2, n2_h), (gb, gb_h)]):
        out_copy(v, h, pl.ds(0, n), i).wait()


def mlp(remote, tokens, att, cot, wout, weights, gs):
    n, width = tokens.shape
    s, dma = jax.ShapeDtypeStruct, pltpu.SemaphoreType.DMA
    any_, vm = pl.BlockSpec(memory_space=pl.ANY), pl.BlockSpec(memory_space=pltpu.VMEM)
    big = lambda d: pltpu.VMEM((n, width), d)
    sq = pltpu.VMEM((2, width, width), BF16)
    part = pltpu.VMEM((2, TILE, width), BF16)
    rows = lambda d: s((n, width), d)
    outs = [rows(BF16), rows(F32), rows(BF16), rows(BF16), rows(BF16), s((4, n, width), BF16), s((4, n, width), BF16), s((8, width), F32)]
    out_specs = [any_] * 7 + [vm]
    scratch = [big(BF16), big(BF16), big(BF16), big(F32), big(F32), big(F32), big(BF16), big(BF16), pltpu.VMEM((width, width), BF16),
               sq, sq, part, part, dma((4,)), dma((2, 2)), dma((2, 2)), dma((5,))]
    params = dict(vmem_limit_bytes=VMEM_BYTES)
    if remote:
        n_dev = width // weights[2].shape[1]
        outs += [s((3, width, width), BF16), s((3, width, width), BF16)]
        out_specs += [any_] * 2
        scratch += [dma((3, 2)), dma((3, 2, n_dev)), dma((3, 2))]
        params.update(collective_id=1, has_side_effects=True)
    return pl.pallas_call(
        functools.partial(mlp_kernel, remote), in_specs=[any_] * 6 + ([vm, any_] if remote else []) + [vm], out_specs=out_specs, out_shape=outs,
        scratch_shapes=scratch, compiler_params=pltpu.CompilerParams(**params), name="mlp",
    )(tokens, att, cot, wout, *weights, gs)[:8]


class Piece:
    def __init__(self, place, parts, total, recv, local, sems):
        self.p, self.parts, self.total, self.sems = place, parts, total, sems
        self.from_core, self.in1, self.in2, self.in3 = recv
        self.out1, self.keep1, self.out2, self.keep2, self.out3 = local

    def hop(self, i, src, dst, to):
        return pltpu.make_async_remote_copy(src_ref=src, dst_ref=dst, send_sem=self.sems.at[0, i], recv_sem=self.sems.at[1, i],
                                            device_id=to, device_id_type=MESH)

    def core(self):
        return self.hop(0, self.parts.at[:, 1 - self.p.c], self.from_core, self.p.partner)

    def h1(self):
        return self.hop(1, self.out1, self.in1, self.p.first2)

    def h2(self):
        return self.hop(2, self.out2, self.in2, self.p.second2)

    def h3(self, k):
        return self.hop(2 + k, self.out3.at[k - 1], self.in3.at[k - 1], self.p.id(z=self.p.z_at(k)))

    def t0(self):
        self.core().start()

    def t1(self):
        p = self.p
        self.core().wait_recv()

        def both(k):
            return self.parts[k, p.c].astype(F32) + self.from_core[k].astype(F32)

        def away(b, carry):
            self.out1[b] = both(p.block(1, b // 4, b % 4)).astype(BF16)
            return carry
        lax.fori_loop(0, 8, away, 0)
        self.h1().start()

        def here(b, carry):
            self.keep1[b] = both(p.block(0, b // 4, b % 4))
            return carry
        lax.fori_loop(0, 8, here, 0)
        self.core().wait_send()

    def t2(self):
        self.h1().wait_recv()

        def away(z, carry):
            self.out2[z] = (self.keep1[4 + z] + self.in1[4 + z].astype(F32)).astype(BF16)
            return carry
        lax.fori_loop(0, 4, away, 0)
        self.h2().start()

        def here(z, carry):
            self.keep2[z] = self.keep1[z] + self.in1[z].astype(F32)
            return carry
        lax.fori_loop(0, 4, here, 0)
        self.h1().wait_send()

    def t3(self):
        p = self.p
        self.h2().wait_recv()
        for k in (2, 1, 3):
            z = p.z_at(k)
            self.out3[k - 1] = (self.keep2[z] + self.in2[z].astype(F32)).astype(BF16)
            self.h3(k).start()
        self.keep2[p.z] = self.keep2[p.z] + self.in2[p.z].astype(F32)
        self.h2().wait_send()

    def t4(self):
        total = self.keep2[self.p.z]
        for k in (1, 3, 2):
            self.h3(k).wait_recv()
            total = total + self.in3[k - 1].astype(F32)
        rows, half = self.total.shape[0], total.shape[1]
        for i in range(self.total.shape[1] // half):
            self.total[:, i * half:(i + 1) * half] = total[i * rows:(i + 1) * rows]
        for k in (1, 2, 3):
            self.h3(k).wait_send()


class Sum:
    def __init__(self, place, stage, came, sems):
        self.p, self.stage, self.came, self.sems = place, stage, came, sems

    def hop(self, i):
        p = self.p
        to = [p.partner, p.first2, p.second2] + [p.id(z=p.z_at(k)) for k in (1, 2, 3)]
        return pltpu.make_async_remote_copy(src_ref=self.stage.at[min(i, 3)], dst_ref=self.came.at[i], send_sem=self.sems.at[0, i],
                                            recv_sem=self.sems.at[1, i], device_id=to[i], device_id_type=MESH)

    def step(self, i):
        self.hop(i).wait_recv()
        self.stage[i + 1] = self.stage[i] + self.came[i]
        for k in (i + 1,) if i < 2 else (3, 4, 5):
            self.hop(k).start()

    def finish(self):
        for i in (3, 4, 5):
            self.hop(i).wait_recv()
        for i in range(6):
            self.hop(i).wait_send()
        return self.stage[3] + self.came[3] + self.came[4] + self.came[5]


class ReducePlace(Place):
    def __init__(self):
        super().__init__()
        self.first2, self.second2 = self.second, self.first

    def block(self, df, ds, z):
        return self.slot_of(ds, df, z) // 2


AXES = ("dp", "fsdp")
U_OUT, U_PROJ, U_Q, U_END = 4, 5, 9, 12
LAST_ROWS = 32
DELAYS = (0, 1, 4, 6, 8)
RING_1, RING_2 = 4, 6
RECV = (16, 8, 4, 3)


def pack(g):
    half = g.shape[-1] // 2
    return jnp.concatenate([g[..., :half], g[..., half:]], axis=-2)


def grads_kernel(remote, tok_h, ghid_h, gq_h, gk_h, gv_h, w_h, act_h, gi_h, n2_h, cot_h, att_h, gb_h, gs_ref, stat_two, gtok_h, *refs):
    outs, (pool, gw, w, ghid, stat, insem, tsem, osem), refs = refs[:5], refs[5:13], refs[13:]
    stat_ref = outs[4]
    n, width = pool.shape[1:]
    fresh = w.shape[1] - 2 * width
    n_t = n // TILE
    gain, shift = gs_ref[0:1, :], gs_ref[2:3, :]

    def load(src, i):
        return pltpu.make_async_copy(src, pool.at[i], insem.at[i])

    def loaded(i):
        load(pool.at[i], i).wait()
    wload = pltpu.make_async_copy(w_h, w, insem.at[6])
    for i, src in enumerate((n2_h, gi_h.at[0], gi_h.at[1], att_h, gb_h, tok_h)):
        load(src, i).start()
    wload.start()
    if remote:
        plan, late = reduce_plan(gw, outs, refs)
    else:
        plan, late = collect_plan(gw, outs, refs)
    loaded(0)

    def normalised():
        loaded(5)

        def tile(t, carry):
            r = tile_at(t)
            xhat, _ = normalise(pool[5, r, :].astype(F32))
            pool[3, r, :] = (xhat * gain + shift).astype(BF16)
            return carry
        lax.fori_loop(0, n_t, tile, 0)

    after = {0: [load(gi_h.at[2], 1).start], 1: [load(gi_h.at[3], 2).start], 2: [load(act_h.at[0], 1).start],
             3: [load(act_h.at[1], 2).start, load(cot_h, 0).start], U_OUT: [load(gq_h, 4).start, normalised],
             5: [load(act_h.at[2], 1).start], 6: [load(act_h.at[3], 2).start],
             8: [load(gk_h, 0).start, load(gv_h, 2).start]}

    def unit(u, carry):
        slot = u % 2
        ring = 1 + jnp.where(u < U_OUT, u, u - U_PROJ) % 2
        proj = (u >= U_PROJ) & (u < U_Q)
        lhs = jnp.where(u < U_OUT, 0, jnp.where(proj, ring, 3))
        rhs = jnp.where(u < U_OUT, ring, jnp.where((u == U_OUT) | (u == U_Q), 4, jnp.where(proj | (u == U_Q + 1), 0, 2)))

        @pl.when((u < U_OUT) | proj)
        def _():
            loaded(ring)

        for when, bufs in {U_OUT: (3, 4), U_PROJ: (0,), U_Q: (4,), U_Q + 1: (0,), U_Q + 2: (2,)}.items():
            @pl.when(u == when)
            def _():
                for b in bufs:
                    loaded(b)

        def rows(m, carry):
            c = pl.ds(pl.multiple_of(m * 384, 128), 384)
            g = dot_tn(pool[lhs, :, c], pool[rhs])
            gw[slot, pl.ds(m * 8, 8)] = pack(g.reshape(8, 2, 24, width)).astype(BF16)
            return carry
        lax.fori_loop(0, 2, rows, 0)
        for when in range(U_END):
            steps = after.get(when, []) + plan.get(when, [])
            if steps:
                @pl.when(u == when)
                def _():
                    for s in steps:
                        s()
        return carry
    lax.fori_loop(0, U_END, unit, 0)
    wload.wait()
    stat[...] = jnp.zeros_like(stat)

    def gin(t):
        return pltpu.make_async_copy(ghid_h.at[tile_at(t), :], ghid.at[t % 2], tsem.at[t % 2])

    def gout(t):
        return pltpu.make_async_copy(ghid.at[t % 2], gtok_h.at[tile_at(t), :], osem.at[t % 2])

    gin(0).start()

    def tile(t, carry):
        r, slot = tile_at(t), t % 2
        g = (dot_nt(pool[4, r, :], w[:, :width]) + dot_nt(pool[0, r, :], w[:, width:2 * width])
             + dot_nt(pool[2, r, :fresh], w[:, 2 * width:]))
        gin(t).wait()

        @pl.when(t > 0)
        def _():
            gout(t - 1).wait()

        @pl.when(t + 1 < n_t)
        def _():
            gin(t + 1).start()
        xhat, rstd = normalise(pool[5, r, :].astype(F32))
        stat[0:1, :] += jnp.sum(g * xhat, axis=0, keepdims=True)
        stat[2:3, :] += jnp.sum(g, axis=0, keepdims=True)
        ghid[slot] += norm_back(g, xhat, rstd, gain)
        gout(t).start()
        for when in range(n_t):
            steps = plan.get(U_END + when, [])
            if steps:
                @pl.when(t == when)
                def _():
                    for s in steps:
                        s()
        return carry
    lax.fori_loop(0, n_t, tile, 0)
    stat[...] = stat[...] + stat_two[...]
    late(stat)
    gout(n_t - 1).wait()


def collect_plan(gw, outs, refs):
    parts, stat_ref = outs[0], outs[4]
    sem = refs[0]

    def emit(u):
        def go():
            c = pltpu.make_async_copy(gw.at[u % 2], parts.at[u], sem)
            c.start()
            c.wait()
        return go

    def late(stat):
        stat_ref[...] = stat[...]
    return {u: [emit(u)] for u in range(U_END)}, late


def reduce_plan(gw, outs, refs):
    fc_t, proj_t, out_t, qkv_t, stat_ref = outs
    recv, local, (fcp, stage, came, sems, ssem) = refs[:4], refs[4:9], refs[9:]
    small, width = out_t.shape
    last = qkv_t.shape[1] - 2 * width
    place = ReducePlace()
    enter(place)
    dest = [fcp.at[u] for u in range(N_FF)] + [out_t] + [proj_t.at[pl.ds(u * small, small), :] for u in range(N_FF)] + [
        qkv_t.at[:, pl.ds(0, width)], qkv_t.at[:, pl.ds(width, width)], qkv_t.at[:, pl.ds(2 * width, last)]]
    pieces = []
    for u in range(U_END):
        whole = dest[u].shape[1] == width
        pick = lambda ref, *at: ref.at[at] if whole else ref.at[at + (slice(None),) * (len(ref.shape) - len(at) - 2) + (pl.ds(0, LAST_ROWS),)]
        bufs = [pick(b, u) for b in recv], [pick(b, u % (RING_1 if i < 2 else RING_2)) for i, b in enumerate(local)]
        pieces.append(Piece(place, pick(gw, u % 2), dest[u], *bufs, sems.at[u]))
    todo = [(u + d, -k, u) for u in range(U_END) for k, d in enumerate(DELAYS)]
    todo.sort(key=lambda e: (e[0], e[1] if e[1] else -9, e[2]))
    plan, rest = {}, []
    for when, neg, u in todo:
        step = getattr(pieces[u], "t%d" % -neg)
        if when < U_END + 4:
            plan.setdefault(when, []).append(step)
        else:
            rest.append(step)
    sums = Sum(place, stage, came, ssem)

    def late(stat):
        stage[0] = stat[...]
        sums.hop(0).start()
        between = [lambda: sums.step(0), lambda: sums.step(1), lambda: sums.step(2)]
        fc_t[...] = spread_groups([fcp[j] for j in range(N_FF)], width // small, small)
        for step in rest:
            step()
            if between:
                between.pop(0)()
        for step in between:
            step()
        stat_ref[...] = sums.finish()
    return plan, late


def grads(remote, tokens, ghid, gq, gk, gv, w, act, gi, n2, cot, att, gb, gs, stat):
    n, width = tokens.shape
    fresh = w.shape[1] - 2 * width
    small = 24
    ff = act.shape[0] * width
    s, dma = jax.ShapeDtypeStruct, pltpu.SemaphoreType.DMA
    any_, vm = pl.BlockSpec(memory_space=pl.ANY), pl.BlockSpec(memory_space=pltpu.VMEM)
    block = (2 * small, width // 2)
    outs = [s((n, width), F32)]
    scratch = [pltpu.VMEM((6, n, width), BF16), pltpu.VMEM((2, 16, 2) + block, BF16), pltpu.VMEM(w.shape, BF16), pltpu.VMEM((2, TILE, width), F32),
               pltpu.VMEM((8, width), F32), dma((7,)), dma((2,)), dma((2,))]
    params = dict(vmem_limit_bytes=VMEM_BYTES)
    if remote:
        outs += [s((small, ff), F32), s((ff // 32, width), F32), s((small, width), F32), s((small, w.shape[1]), F32)]
        specs = [vm] * 4
        scratch += [pltpu.VMEM((U_END, k) + block, BF16) for k in RECV]
        scratch += [pltpu.VMEM((r, k) + block, d) for r, k, d in ((RING_1, 8, BF16), (RING_1, 8, F32), (RING_2, 4, BF16), (RING_2, 4, F32), (RING_2, 3, BF16))]
        scratch += [pltpu.VMEM((N_FF, small, width), F32), pltpu.VMEM((4, 8, width), F32), pltpu.VMEM((6, 8, width), F32), dma((U_END, 2, 6)), dma((2, 6))]
        params.update(collective_id=2, has_side_effects=True)
    else:
        outs += [s((U_END, 16, 2) + block, BF16)] + [s((8, 128), F32)] * 3
        specs = [any_] * 4
        scratch += [dma(())]
    return pl.pallas_call(
        functools.partial(grads_kernel, remote), in_specs=[any_] * 12 + [vm] * 2, out_specs=[any_] + specs + [vm],
        out_shape=outs + [s((8, width), F32)], scratch_shapes=scratch,
        compiler_params=pltpu.CompilerParams(**params), name="grads",
    )(tokens, ghid, gq, gk, gv, w, act, gi, n2, cot, att, gb, gs, stat)


def unpack_parts(parts, width, fresh):
    p = parts.astype(F32).reshape(U_END, width // 24, 2, 24, width // 2).transpose(0, 1, 3, 2, 4).reshape(U_END, width, width)
    return (jnp.concatenate([p[U_Q], p[U_Q + 1], p[U_Q + 2, :, :fresh]], axis=1), p[U_OUT], jnp.concatenate(list(p[:N_FF]), axis=1),
            p[U_PROJ:U_Q].reshape(-1, width))


N_COPY = 8


def finish_kernel(tok, fc, proj, out, qkv, stat, tok_o, fc_o, proj_o, out_o, qkv_o, gain_o, shift_o, buf, isem, osem):
    n = tok.shape[0] // N_COPY
    rows = [pl.ds(i * n, n) for i in range(N_COPY)]
    loads = [pltpu.make_async_copy(tok.at[r, :], buf.at[r, :], isem.at[i]) for i, r in enumerate(rows)]
    stores = [pltpu.make_async_copy(buf.at[r, :], tok_o.at[r, :], osem.at[i]) for i, r in enumerate(rows)]
    for c in loads:
        c.start()
    fc_o[...], proj_o[...], out_o[...], qkv_o[...] = fc[...], proj[...], out[...], qkv[...]
    width, own = stat.shape[1], gain_o.shape[1]
    mine = pltpu.roll(stat[...], lax.rem(width - own * lax.axis_index(AXES), width), 1)
    gain_o[...] = mine[0:2, :own]
    shift_o[...] = mine[2:4, :own]
    for load, store in zip(loads, stores):
        load.wait()
        store.start()
    for c in stores:
        c.wait()


def finish(tok, fc, proj, out, qkv, stat, own):
    small = jax.ShapeDtypeStruct((2, own), F32)
    outs = [jax.ShapeDtypeStruct(a.shape, F32) for a in (tok, fc, proj, out, qkv)] + [small, small]
    any_, vm = pl.BlockSpec(memory_space=pl.ANY), pl.BlockSpec(memory_space=pltpu.VMEM)
    return pl.pallas_call(
        finish_kernel, in_specs=[any_] + [vm] * 5, out_specs=[any_] + [vm] * 6, out_shape=outs,
        scratch_shapes=[pltpu.VMEM(tok.shape, F32), pltpu.SemaphoreType.DMA((N_COPY,)), pltpu.SemaphoreType.DMA((N_COPY,))],
        compiler_params=pltpu.CompilerParams(vmem_limit_bytes=VMEM_BYTES), name="finish",
    )(tok, fc, proj, out, qkv, stat)


def body(direct, tokens, skip_values, w_qkv, w_out, w_fc, w_proj, norm_gains, norm_shifts, segment_ids, pad_mask, cotangent):
    micro, rows, length, width = tokens.shape
    half, ff = skip_values.shape[3], w_fc.shape[1]
    seqs = micro * rows
    n = seqs * length
    own = norm_gains.shape[1]
    flat = lambda a: a.reshape(n, a.shape[-1])
    seq = lambda a: a.reshape(seqs, length, a.shape[-1])
    tok, skip, cot = flat(tokens), flat(skip_values), flat(cotangent)
    seg, pad = segment_ids.reshape(seqs, 1, length), pad_mask.reshape(seqs, 1, length)
    if direct:
        q, k, v, gs, fcp, _, qkv, out, fc0, proj0 = start(tok, skip, norm_gains, norm_shifts, w_qkv, w_out, w_fc, w_proj)
        weights = (fc0, proj0, fcp, w_proj)
    else:
        qkv, out, *weights = [lax.all_gather(w, AXES, axis=0, tiled=True) for w in (w_qkv, w_out, w_fc, w_proj)]
        rows8 = jnp.concatenate([norm_gains, norm_shifts, jnp.zeros((4, own), BF16)], axis=0)
        gs = lax.all_gather(rows8, AXES, axis=1, tiled=True).astype(F32)
        q, k, v = project(tok, skip, qkv, gs)
    att, lse = attend(seq(q), seq(k), seq(v), seg, pad)
    att = flat(att)
    lout, ghid, gatt, n2, gb, act, gi, stat = mlp(direct, tok, att, cot, out, weights, gs)
    gq, gk, gv, gskip, lout = attend_back(seq(q), seq(k), seq(v), seq(gatt), lse, seg, pad, seq(lout), half)
    gtok, gfc, gproj, gout, gqkv, stat = grads(
        direct, tok, ghid, flat(gq), flat(gk), flat(gv), qkv, act, gi, n2, cot, att, gb, gs, stat)
    if direct:
        gtok, total_fc, total_proj, total_out, total_qkv, gains, shifts = finish(gtok, gfc, gproj, gout, gqkv, stat, own)
    else:
        total_qkv, total_out, total_fc, total_proj = [
            lax.psum_scatter(g, AXES, scatter_dimension=0, tiled=True) for g in unpack_parts(gfc, width, width - half)]
        gains = lax.psum_scatter(stat[0:2], AXES, scatter_dimension=1, tiled=True)
        shifts = lax.psum_scatter(stat[2:4], AXES, scatter_dimension=1, tiled=True)
    shape4 = lambda a: a.reshape(micro, rows, length, a.shape[-1])
    return (shape4(lout), shape4(gtok), shape4(gskip), total_qkv, total_out, total_fc, total_proj, gains, shifts)


def solution(mesh):
    tok, mat, row, ids = P(None, AXES, None, None), P(AXES, None), P(None, AXES), P(None, AXES, None)
    direct = dict(mesh.shape) == {"dp": 2, "fsdp": 16}
    return jax.shard_map(
        functools.partial(body, direct), mesh=mesh,
        in_specs=(tok, tok, mat, mat, mat, mat, row, row, ids, ids, tok),
        out_specs=(tok, tok, tok, mat, mat, mat, mat, row, row), check_vma=False)
```

```python
import functools
import jax
import jax.numpy as jnp
from jax import lax
from jax.experimental import pallas as pl
from jax.experimental.pallas import tpu as pltpu
from jax.sharding import PartitionSpec as P

F32, BF16 = jnp.float32, jnp.bfloat16

HEAD = 64
BLK = 128
WIN = 5
MASKED = -1e9
PAIRS_FWD, PAIRS_BWD = 6, 6


def build_bias(seg_row, pad_row, bias_ref, n_blk):
    code = jnp.where(pad_row == 1, seg_row, -1)
    key = lax.broadcasted_iota(jnp.int32, (BLK, BLK), 0)
    row = lax.broadcasted_iota(jnp.int32, (BLK, BLK), 1)
    for kb in range(n_blk):
        code_k = jnp.broadcast_to(code[:, kb * BLK:(kb + 1) * BLK], (BLK, BLK)).T
        for qb in range(kb, min(kb + WIN, n_blk)):
            vis = code_k == seg_row[:, qb * BLK:(qb + 1) * BLK]
            if kb == qb:
                vis = (vis & (key < row)) | (key == row)
            t = kb - qb + WIN - 1
            bias_ref[qb, t * BLK:(t + 1) * BLK, :] = jnp.where(vis, 0.0, MASKED)


def stack_heads(x):
    low = lax.broadcasted_iota(jnp.int32, x.shape, 1) < HEAD
    zero = jnp.zeros_like(x)
    return jnp.concatenate([jnp.where(low, x, zero), jnp.where(low, zero, x)], axis=0)


def join_heads(x2):
    return jnp.concatenate([x2[:HEAD, :BLK], x2[HEAD:, BLK:]], axis=0)


def twice(x):
    return jnp.concatenate([x, x], axis=1)


def visible_blocks(seg_s, row, qb):
    first = seg_s[row, 0, qb * BLK]
    n = jnp.int32(1)
    for back in range(1, WIN):
        kb = jnp.maximum(qb - back, 0)
        seen = (qb >= back) & (seg_s[row, 0, kb * BLK + BLK - 1] == first)
        n = n + seen.astype(jnp.int32)
    return n


def over_queries(seg_s, row, n_blk, one):
    def step(qb, carry):
        n_vis = visible_blocks(seg_s, row, qb)
        for n in range(1, WIN + 1):
            @pl.when(n_vis == n)
            def _():
                one(n, qb)
        return carry
    lax.fori_loop(0, n_blk, step, 0)


def block(i, n=1):
    return pl.ds(pl.multiple_of(i * BLK, BLK), n * BLK)


def attend_nt(a, b):
    return lax.dot_general(a, b, (((1,), (1,)), ((), ())), preferred_element_type=F32)


def fwd_kernel(n_blk, pairs, seg_s, seg_ref, pad_ref, q_ref, k_ref, v_ref, o_ref, lse_ref, bias_ref, vt_ref):
    row = pl.program_id(0)

    @pl.when(pl.program_id(1) == 0)
    def _():
        build_bias(seg_ref[...], pad_ref[...], bias_ref, n_blk)

    lanes = [slice(i * BLK, (i + 1) * BLK) for i in range(pairs)]
    for kb in range(n_blk):
        for h in lanes:
            vt_ref[h, kb * BLK:(kb + 1) * BLK] = v_ref[kb * BLK:(kb + 1) * BLK, h].T

    def one(n, qb):
        keys, here = block(qb - n + 1, n), block(qb)
        b = twice(bias_ref[qb, (WIN - n) * BLK:, :])
        s = [attend_nt(k_ref[keys, h], stack_heads(q_ref[here, h])) + b for h in lanes]
        for i, h in enumerate(lanes):
            m = jnp.max(s[i], axis=0, keepdims=True)
            p = jnp.exp(s[i] - m)
            total = jnp.sum(p, axis=0, keepdims=True)
            o2 = jnp.dot(vt_ref[h, keys], p.astype(BF16), preferred_element_type=F32) * (1.0 / total)
            o_ref[here, h] = join_heads(o2).astype(BF16).T
            lse_ref[i, qb] = m + jnp.log(total)
    over_queries(seg_s, row, n_blk, one)


def attend(q, k, v, seg, pad):
    rows, length, width = q.shape
    n_blk, pairs = length // BLK, PAIRS_FWD
    groups = width // 128 // pairs
    tok = pl.BlockSpec((None, length, pairs * 128), lambda r, h, s: (r, 0, h))
    ids = pl.BlockSpec((None, 1, length), lambda r, h, s: (r, 0, 0))
    return pl.pallas_call(
        functools.partial(fwd_kernel, n_blk, pairs),
        grid_spec=pltpu.PrefetchScalarGridSpec(
            num_scalar_prefetch=1, grid=(rows, groups),
            in_specs=[ids, ids, tok, tok, tok],
            out_specs=[tok, pl.BlockSpec((None, pairs, n_blk, 1, 2 * BLK), lambda r, h, s: (r, h, 0, 0, 0))],
            scratch_shapes=[pltpu.VMEM((n_blk, WIN * BLK, BLK), F32), pltpu.VMEM((pairs * BLK, length), BF16)]),
        out_shape=[jax.ShapeDtypeStruct((rows, length, width), BF16), jax.ShapeDtypeStruct((rows, width // 128, n_blk, 1, 2 * BLK), F32)],
        compiler_params=pltpu.CompilerParams(dimension_semantics=("arbitrary", "arbitrary"), vmem_limit_bytes=64000 << 10),
        name="attend",
    )(seg, seg, pad, q, k, v)


def bwd_kernel(n_blk, pairs, seg_s, seg_ref, pad_ref, q_ref, k_ref, v_ref, g_ref, lse_ref, result_ref, dq_ref, dk_ref, dv_ref, dskip_ref, result_out,
               bias_ref, kt_ref, dk_acc, dv_acc):
    row = pl.program_id(0)
    result_out[...] = result_ref[...]

    @pl.when(pl.program_id(1) == 0)
    def _():
        build_bias(seg_ref[...], pad_ref[...], bias_ref, n_blk)

    lanes = [slice(i * BLK, (i + 1) * BLK) for i in range(pairs)]
    for kb in range(n_blk):
        for h in lanes:
            kt_ref[h, kb * BLK:(kb + 1) * BLK] = k_ref[kb * BLK:(kb + 1) * BLK, h].T
    dk_acc[...] = jnp.zeros_like(dk_acc)
    dv_acc[...] = jnp.zeros_like(dv_acc)

    def one(n, qb):
        keys, here = block(qb - n + 1, n), block(qb)
        b = twice(bias_ref[qb, (WIN - n) * BLK:, :])
        for i, h in enumerate(lanes):
            q2, g2 = stack_heads(q_ref[here, h]), stack_heads(g_ref[here, h])
            p = jnp.exp(attend_nt(k_ref[keys, h], q2) + b - lse_ref[i, qb])
            dp = attend_nt(v_ref[keys, h], g2)
            inner = jnp.sum(p * dp, axis=0, keepdims=True)
            ds = (p * (dp - inner)).astype(BF16)
            dv_acc[keys, h] += jnp.dot(p.astype(BF16), g2, preferred_element_type=F32)
            dk_acc[keys, h] += jnp.dot(ds, q2, preferred_element_type=F32)
            dq2 = jnp.dot(kt_ref[h, keys], ds, preferred_element_type=F32)
            dq_ref[here, h] = (join_heads(dq2) * 0.125).astype(BF16).T
    over_queries(seg_s, row, n_blk, one)
    dk_ref[...] = dk_acc[...].astype(BF16)
    dv_ref[...] = dv_acc[...].astype(BF16)

    @pl.when(pl.program_id(1) == pl.num_programs(1) - 1)
    def _():
        dskip_ref[...] = dv_ref[:, dv_ref.shape[1] - dskip_ref.shape[1]:].astype(F32)


def attend_back(q, k, v, g, lse, seg, pad, result, half):
    rows, length, width = q.shape
    n_blk, pairs = length // BLK, PAIRS_BWD
    groups = width // 128 // pairs
    tok = pl.BlockSpec((None, length, pairs * 128), lambda r, h, s: (r, 0, h))
    ids = pl.BlockSpec((None, 1, length), lambda r, h, s: (r, 0, 0))
    out = jax.ShapeDtypeStruct((rows, length, width), BF16)
    return pl.pallas_call(
        functools.partial(bwd_kernel, n_blk, pairs),
        grid_spec=pltpu.PrefetchScalarGridSpec(
            num_scalar_prefetch=1, grid=(rows, groups),
            in_specs=[ids, ids, tok, tok, tok, tok, pl.BlockSpec((None, pairs, n_blk, 1, 2 * BLK), lambda r, h, s: (r, h, 0, 0, 0)), tok],
            out_specs=[tok, tok, tok, pl.BlockSpec((None, length, half), lambda r, h, s: (r, 0, 0)), tok],
            scratch_shapes=[pltpu.VMEM((n_blk, WIN * BLK, BLK), F32), pltpu.VMEM((pairs * BLK, length), BF16),
                            pltpu.VMEM((length, pairs * BLK), F32), pltpu.VMEM((length, pairs * BLK), F32)]),
        out_shape=[out, out, out, jax.ShapeDtypeStruct((rows, length, half), F32), out],
        compiler_params=pltpu.CompilerParams(dimension_semantics=("arbitrary", "arbitrary"), vmem_limit_bytes=64000 << 10),
        name="attend_back",
    )(seg, seg, pad, q, k, v, g, lse, result)


MESH = pl.DeviceIdType.MESH
NZ = 4


class Place:
    def __init__(self):
        dp, fs = lax.axis_index("dp"), lax.axis_index("fsdp")
        self.x, self.z, self.y, self.c = dp, fs // 4, (fs // 2) % 2, fs % 2
        self.slot = self.x * 16 + fs
        self.first = self.id(x=jnp.where(self.c == 0, 1 - self.x, self.x), y=jnp.where(self.c == 0, self.y, 1 - self.y))
        self.second = self.id(x=jnp.where(self.c == 0, self.x, 1 - self.x), y=jnp.where(self.c == 0, 1 - self.y, self.y))
        self.partner = self.id(c=1 - self.c)

    def id(self, x=None, y=None, z=None, c=None):
        x = self.x if x is None else x
        y = self.y if y is None else y
        z = self.z if z is None else z
        c = self.c if c is None else c
        return (x, z * 4 + y * 2 + c)

    def z_at(self, k):
        return (self.z + k) % NZ

    def peers(self):
        return [self.partner, self.first, self.second] + [self.id(z=self.z_at(k)) for k in (1, 2, 3)]

    def slot_of(self, df, ds, z):
        dx = jnp.where(self.c == 0, df, ds)
        dy = jnp.where(self.c == 0, ds, df)
        x = jnp.where(dx == 1, 1 - self.x, self.x)
        y = jnp.where(dy == 1, 1 - self.y, self.y)
        return x * 16 + z * 4 + y * 2 + self.c


def enter(place):
    bar = pltpu.get_barrier_semaphore()
    for peer in place.peers():
        pl.semaphore_signal(bar, inc=1, device_id=peer, device_id_type=MESH)
    pl.semaphore_wait(bar, 6)


class Gather:
    SENDS = 31

    def __init__(self, place, shard, out, send, recv, own):
        self.p, self.shard, self.out, self.send, self.recv, self.own = place, shard, out, send, recv, own
        self.size = shard.shape[0]

    def at(self, slot, n=1):
        return self.out.at[pl.ds(pl.multiple_of(slot * self.size, 8), n * self.size), :]

    def push(self, src, slot, to):
        pltpu.make_async_remote_copy(src_ref=src, dst_ref=self.at(slot), send_sem=self.send, recv_sem=self.recv.at[slot],
                                     device_id=to, device_id_type=MESH).start()

    def arrived(self, slot):
        pltpu.make_async_copy(self.at(slot), self.at(slot), self.recv.at[slot]).wait()

    def keep(self, slot):
        return pltpu.make_async_copy(self.shard, self.at(slot), self.own)

    def s1(self):
        p = self.p
        self.keep(p.slot).start()
        for k in (1, 3, 2):
            self.push(self.shard, p.slot, p.id(z=p.z_at(k)))
        for to in (p.first, p.partner, p.second):
            self.push(self.shard, p.slot, to)

    def each(self, n, slot_at, targets):
        def go(i, carry):
            slot = slot_at(i)
            self.arrived(slot)
            for to in targets:
                self.push(self.at(slot), slot, to)
            return carry
        lax.fori_loop(0, n, go, 0)

    def s2(self):
        p = self.p
        self.each(3, lambda i: p.slot_of(0, 0, p.z_at(i + 1)), (p.first, p.second, p.partner))

    def s3(self):
        p = self.p
        self.each(4, lambda i: p.slot_of(1, 0, p.z_at(i)), (p.second, p.partner))

    def s4(self):
        p = self.p
        self.each(8, lambda i: p.slot_of(i // 4, 1, p.z_at(i % 4)), (p.partner,))

    def s5(self):
        self.each(16, lambda i: 2 * i + 1 - self.p.c, ())
        self.keep(self.p.slot).wait()

    def drain(self):
        done = self.at(0, self.SENDS)
        pltpu.make_async_copy(done, done, self.send).wait()


VMEM_BYTES = 64000 << 10
TILE = 512
SMALL_TILE = 256
EPS = 1e-5
GELU_C = 0.7978845608028654
GELU_A = 0.044715


def dot(a, b):
    return jnp.dot(a, b, preferred_element_type=F32)


def dot_nt(a, b):
    return lax.dot_general(a, b, (((1,), (1,)), ((), ())), preferred_element_type=F32)


def dot_tn(a, b):
    return lax.dot_general(a, b, (((0,), (0,)), ((), ())), preferred_element_type=F32)


def normalise(v):
    centred = v - jnp.mean(v, axis=-1, keepdims=True)
    rstd = lax.rsqrt(jnp.mean(centred * centred, axis=-1, keepdims=True) + EPS)
    return centred * rstd, rstd


def norm_back(g, xhat, rstd, gain):
    gh = g * gain
    return rstd * (gh - jnp.mean(gh, axis=-1, keepdims=True) - xhat * jnp.mean(gh * xhat, axis=-1, keepdims=True))


def gelu_both(u, grad):
    sq = u * u
    t = jnp.tanh(u * (GELU_C + (GELU_C * GELU_A) * sq))
    half = 0.5 + 0.5 * t
    act = u * half
    slope = half + act * (1.0 - half) * (2.0 * GELU_C + (6.0 * GELU_C * GELU_A) * sq)
    return act, grad * slope


def tile_at(t):
    return pl.ds(pl.multiple_of(t * TILE, TILE), TILE)


def qkv_kernel(tok_ref, skip_ref, w_ref, gs_ref, q_ref, k_ref, v_ref):
    width, half = tok_ref.shape[1], skip_ref.shape[1]
    xhat, _ = normalise(tok_ref[...].astype(F32))
    normed = (xhat * gs_ref[0:1, :] + gs_ref[2:3, :]).astype(BF16)
    q_ref[...] = (dot(normed, w_ref[:, :width]) * 0.125).astype(BF16)
    k_ref[...] = dot(normed, w_ref[:, width:2 * width]).astype(BF16)
    v_ref[:, :half] = dot(normed, w_ref[:, 2 * width:]).astype(BF16)
    v_ref[:, half:] = skip_ref[...]


def project(tokens, skip, w, gs):
    n, width = tokens.shape
    row = lambda c: pl.BlockSpec((TILE, c), lambda t: (t, 0))
    whole = lambda a: pl.BlockSpec(a.shape, lambda t: (0, 0))
    out = jax.ShapeDtypeStruct((n, width), BF16)
    return pl.pallas_call(
        qkv_kernel, grid=(n // TILE,), in_specs=[row(width), row(skip.shape[1]), whole(w), whole(gs)],
        out_specs=[row(width)] * 3, out_shape=[out] * 3,
        compiler_params=pltpu.CompilerParams(vmem_limit_bytes=VMEM_BYTES), name="project",
    )(tokens, skip, w, gs)


def lane_mod(x, period):
    return jnp.broadcast_to(lax.rem(lax.broadcasted_iota(jnp.int32, (1, x.shape[1]), 1), jnp.int32(period)), x.shape)


def gather_groups(x, groups, size, parts):
    out = []
    total = x.shape[1]
    for j in range(parts):
        y = pltpu.roll(x, total - j * size, 1) if j else x
        span = size
        while span < groups * size:
            m = lane_mod(y, 2 * parts * span)
            y = jnp.where((m >= span) & (m < 2 * span), pltpu.roll(y, total - (parts - 1) * span, 1), y)
            span *= 2
        out.append(y[:, :groups * size])
    return out


def spread_groups(pieces, groups, size):
    parts = len(pieces)
    out = None
    for j, piece in enumerate(pieces):
        y = jnp.concatenate([piece] + [jnp.zeros_like(piece)] * (parts - 1), axis=1)
        span = groups * size
        while span > size:
            span //= 2
            m = lane_mod(y, 2 * parts * span)
            y = jnp.where((m >= parts * span) & (m < (parts + 1) * span), pltpu.roll(y, (parts - 1) * span, 1), y)
        y = pltpu.roll(y, j * size, 1) if j else y
        m = lane_mod(y, parts * size)
        y = jnp.where((m >= j * size) & (m < (j + 1) * size), y, 0.0)
        out = y if out is None else out + y
    return out


N_FF = 4


def start_kernel(tok_h, skip_h, gain_ref, shift_ref, qkv_ref, out_ref, fc_ref, proj_h,
                 q_h, k_h, v_h, gs_ref, fcp_ref, gs_all, qkv_all, out_all, fc_all, proj_all,
                 tok, skip, xhat, w, gsb, q, k, v, normed, rows_ref, insem, osem, send, recv, own):
    n, width = tok.shape
    half = skip.shape[1]
    n_t = n // TILE
    n_dev = qkv_all.shape[0] // qkv_ref.shape[0]
    size = proj_h.shape[0] // N_FF
    place = Place()
    loads = [pltpu.make_async_copy(tok_h, tok, insem.at[0]), pltpu.make_async_copy(skip_h, skip, insem.at[1])]
    for c in loads:
        c.start()
    enter(place)
    cols = [pl.ds(0, width), pl.ds(width, width), pl.ds(2 * width, half)]
    shards = (rows_ref, *[qkv_ref.at[:, c] for c in cols], out_ref, fcp_ref.at[0], proj_h.at[pl.ds(0, size), :])
    outs = (gs_all, *[qkv_all.at[:, c] for c in cols], out_all, fc_all, proj_all)
    jobs = [Gather(place, s, o, send.at[i], recv.at[i], own.at[i]) for i, (s, o) in enumerate(zip(shards, outs))]
    rows, wq, wk, wv, out, fc, proj = jobs
    wq.s1()
    mine = jnp.concatenate([gain_ref[...], shift_ref[...]], axis=0)
    lane = lax.broadcasted_iota(jnp.int32, (mine.shape[1], width), 1) - mine.shape[1] * place.slot
    spot = (lane == lax.broadcasted_iota(jnp.int32, lane.shape, 0)).astype(BF16)
    rows_ref[0:4, :] = dot(mine, spot).astype(BF16)
    rows_ref[4:8, :] = jnp.zeros((4, width), BF16)
    wk.s1(), wv.s1()
    for j, piece in enumerate(gather_groups(fc_ref[...].astype(F32), n_dev, size, N_FF)):
        fcp_ref[j] = piece.astype(BF16)
    rows.s1()
    for c in loads:
        c.wait()

    def centre(t, carry):
        r = tile_at(t)
        xhat[r, :], _ = normalise(tok[r, :].astype(F32))
        return carry
    lax.fori_loop(0, n_t // 2, centre, 0)
    wq.s2(), wk.s2(), wv.s2(), rows.s2(), out.s1()
    wq.s3(), wk.s3(), rows.s3(), wv.s3()
    lax.fori_loop(n_t // 2, n_t, centre, 0)
    fc.s1(), proj.s1()
    wq.s4(), rows.s4(), wk.s4(), out.s2(), wq.s5(), rows.s5()
    wloads = [pltpu.make_async_copy(qkv_all.at[:, c], w.at[:, c], insem.at[4 + i]) for i, c in enumerate(cols)]
    gload = pltpu.make_async_copy(gs_all, gsb, insem.at[3])
    wloads[0].start(), gload.start()
    wv.s4(), fc.s2(), proj.s2()
    gload.wait()
    gs_ref[...] = jnp.sum(gsb[...].astype(F32).reshape(n_dev, 8, width), axis=0)
    wloads[0].wait()

    def copies(r):
        return [pltpu.make_async_copy(s.at[r, :], h.at[r, :], osem.at[i]) for i, (s, h) in enumerate([(q, q_h), (k, k_h), (v, v_h)])]

    def third(i, put):
        def tile(t, carry):
            r = pl.ds(pl.multiple_of(t * SMALL_TILE, SMALL_TILE), SMALL_TILE)
            put(r)
            copies(r)[i].start()
            return carry
        lax.fori_loop(0, n // SMALL_TILE, tile, 0)

    def put_q(r):
        normed[r, :] = (xhat[r, :] * gs_ref[0:1, :] + gs_ref[2:3, :]).astype(BF16)
        q[r, :] = (dot(normed[r, :], w[:, :width]) * 0.125).astype(BF16)

    def put_k(r):
        k[r, :] = dot(normed[r, :], w[:, width:2 * width]).astype(BF16)

    def put_v(r):
        v[r, :half] = dot(normed[r, :], w[:, 2 * width:]).astype(BF16)
        v[r, half:] = skip[r, :]
    third(0, put_q)
    out.s3(), wk.s5()
    wloads[1].start()
    wv.s5()
    wloads[2].start()
    fc.s3()
    wloads[1].wait()
    third(1, put_k)
    proj.s3(), out.s4()
    wloads[2].wait()
    third(2, put_v)
    fc.s4(), out.s5(), proj.s4(), fc.s5(), proj.s5()
    for job in jobs:
        job.drain()
    for c in copies(pl.ds(0, n)):
        c.wait()


def start(tokens, skip, gains, shifts, qkv, out, fc, proj):
    n, width = tokens.shape
    n_dev = width // out.shape[0]
    s, dma = jax.ShapeDtypeStruct, pltpu.SemaphoreType.DMA
    any_, vm = pl.BlockSpec(memory_space=pl.ANY), pl.BlockSpec(memory_space=pltpu.VMEM)
    big = lambda d: pltpu.VMEM((n, width), d)
    act = s((n, width), BF16)
    gathered = [(8 * n_dev, width), (width, qkv.shape[1]), (width, width), (width, width), (width, width)]
    return pl.pallas_call(
        start_kernel, in_specs=[any_, any_] + [vm] * 5 + [any_], out_specs=[any_] * 3 + [vm] * 2 + [any_] * 5,
        out_shape=[act] * 3 + [s((8, width), F32), s((N_FF, fc.shape[0], width), BF16)] + [s(g, BF16) for g in gathered],
        scratch_shapes=[big(BF16), pltpu.VMEM(skip.shape, BF16), big(F32), pltpu.VMEM((width, qkv.shape[1]), BF16), pltpu.VMEM((8 * n_dev, width), BF16),
                        big(BF16), big(BF16), big(BF16), big(BF16), pltpu.VMEM((8, width), BF16), dma((7,)), dma((3,)), dma((7,)), dma((7, n_dev)), dma((7,))],
        compiler_params=pltpu.CompilerParams(vmem_limit_bytes=VMEM_BYTES, collective_id=0, has_side_effects=True), name="start",
    )(tokens, skip, gains, shifts, qkv, out, fc, proj)


MLP_STEPS = {1: (-1, 0, 1, 2), 2: (0, 2, 4, 6), 3: (2, 4, 6, 8)}


def mlp_kernel(remote, tok_h, att_h, cot_h, wout_h, *refs):
    if remote:
        fc0_h, proj0_h, fcp_ref, proj_ref, *refs = refs
    else:
        wfc_h, wproj_h, *refs = refs
    (gs_ref, lout_h, ghid_h, gatt_h, n2_h, gb_h, act_h, gi_h, stat_ref), refs = refs[:9], refs[9:]
    if remote:
        (fc_all, proj_all), refs = refs[:2], refs[2:]
    (tok, att, cot, hidden, oacc, gacc, n2, gb, wout, wfc, wproj, act, gi, insem, wsem, asem, osem), sems = refs[:17], refs[17:]
    n, width = tok.shape
    n_ff = N_FF
    n_t = n // TILE
    gain, shift = gs_ref[1:2, :], gs_ref[3:4, :]

    def load(src_fc, src_proj, slot):
        return (pltpu.make_async_copy(src_fc, wfc.at[slot], wsem.at[0, slot]), pltpu.make_async_copy(src_proj, wproj.at[slot], wsem.at[1, slot]))

    loads = [pltpu.make_async_copy(h, v, insem.at[i]) for i, (h, v) in enumerate([(wout_h, wout), (att_h, att), (tok_h, tok), (cot_h, cot)])]
    for c in loads:
        c.start()
    plan = {}
    if remote:
        send, recv, own = sems
        place = Place()
        enter(place)
        size = proj_ref.shape[0] // n_ff
        sets = []
        for i in range(1, n_ff):
            srcs = (fcp_ref.at[i], proj_ref.at[pl.ds(i * size, size), :])
            sets.append([Gather(place, srcs[k], (fc_all, proj_all)[k].at[i - 1], send.at[i - 1, k], recv.at[i - 1, k], own.at[i - 1, k]) for k in range(2)])

        def run(i, step):
            return lambda: [getattr(job, step)() for job in sets[i - 1]]

        def fetch(i):
            def go():
                for c in load(fc_all.at[i - 1], proj_all.at[i - 1], i % 2):
                    c.start()
            return go
        for i in range(1, n_ff):
            run(i, "s1")()
        early = []
        for i, steps in MLP_STEPS.items():
            for when, name in zip(steps, ("s2", "s3", "s4", "s5")):
                (early if when < 0 else plan.setdefault(when, [])).append(run(i, name))
            plan[steps[3]].append(fetch(i))
        for c in load(fc0_h, proj0_h, 0):
            c.start()
    else:
        early = []
        cols = lambda j: pl.ds(j * width, width)
        for i in range(1, n_ff):
            def fetch(i=i):
                for c in load(wfc_h.at[:, cols(i)], wproj_h.at[cols(i), :], i % 2):
                    c.start()
            plan[(i - 1) * n_t + 3] = [fetch]
        for c in load(wfc_h.at[:, cols(0)], wproj_h.at[cols(0), :], 0):
            c.start()
    for c in loads[:3]:
        c.wait()

    def out_copy(v, h, r, i):
        return pltpu.make_async_copy(v.at[r, :], h.at[r, :], osem.at[i])

    def forward(t, carry):
        r = pl.ds(pl.multiple_of(t * SMALL_TILE, SMALL_TILE), SMALL_TILE)
        h = tok[r, :].astype(F32) + dot(att[r, :], wout[...])
        hidden[r, :] = h
        oacc[r, :] = h
        gacc[r, :] = jnp.zeros_like(h)
        xhat, _ = normalise(h)
        n2[r, :] = (xhat * gain + shift).astype(BF16)
        out_copy(n2, n2_h, r, 3).start()
        return carry
    lax.fori_loop(0, n // SMALL_TILE, forward, 0)
    for step in early:
        step()
    loads[3].wait()

    def saves(i, t, slot):
        return (pltpu.make_async_copy(act.at[slot], act_h.at[i, tile_at(t), :], asem.at[0, slot]),
                pltpu.make_async_copy(gi.at[slot], gi_h.at[i, tile_at(t), :], asem.at[1, slot]))

    def tile(step, carry):
        i, t, slot = step // n_t, step % n_t, step % 2
        ws = i % 2
        r = tile_at(t)

        @pl.when(t == 0)
        def _():
            for c in load(wfc.at[ws], wproj.at[ws], ws):
                c.wait()

        @pl.when(step >= 2)
        def _():
            for c in saves(i, t, slot):
                c.wait()
        a, g = gelu_both(dot(n2[r, :], wfc[ws]), dot_nt(cot[r, :], wproj[ws]))
        a, g = a.astype(BF16), g.astype(BF16)
        act[slot] = a
        gi[slot] = g
        oacc[r, :] += dot(a, wproj[ws])
        gacc[r, :] += dot_nt(g, wfc[ws])
        for c in saves(i, t, slot):
            c.start()
        for when, steps in plan.items():
            @pl.when(step == when)
            def _():
                for s in steps:
                    s()
        return carry
    lax.fori_loop(0, n_ff * n_t, tile, 0)
    stat_ref[...] = jnp.zeros_like(stat_ref)

    def backward(t, carry):
        r = pl.ds(pl.multiple_of(t * SMALL_TILE, SMALL_TILE), SMALL_TILE)
        tok[r, :] = oacc[r, :].astype(BF16)
        xhat, rstd = normalise(hidden[r, :])
        g = gacc[r, :]
        stat_ref[1:2, :] += jnp.sum(g * xhat, axis=0, keepdims=True)
        stat_ref[3:4, :] += jnp.sum(g, axis=0, keepdims=True)
        gh = cot[r, :].astype(F32) + norm_back(g, xhat, rstd, gain)
        hidden[r, :] = gh
        b = gh.astype(BF16)
        gb[r, :] = b
        att[r, :] = dot_nt(b, wout[...]).astype(BF16)
        for i, (v, h) in enumerate([(tok, lout_h), (hidden, ghid_h), (att, gatt_h)]):
            out_copy(v, h, r, i).start()
        out_copy(gb, gb_h, r, 4).start()
        return carry
    lax.fori_loop(0, n // SMALL_TILE, backward, 0)
    if remote:
        for job in sets[0] + sets[1] + sets[2]:
            job.drain()
    for slot in range(2):
        for c in saves(0, 0, slot):
            c.wait()
    for i, (v, h) in enumerate([(tok, lout_h), (hidden, ghid_h), (att, gatt_h), (n2, n2_h), (gb, gb_h)]):
        out_copy(v, h, pl.ds(0, n), i).wait()


def mlp(remote, tokens, att, cot, wout, weights, gs):
    n, width = tokens.shape
    s, dma = jax.ShapeDtypeStruct, pltpu.SemaphoreType.DMA
    any_, vm = pl.BlockSpec(memory_space=pl.ANY), pl.BlockSpec(memory_space=pltpu.VMEM)
    big = lambda d: pltpu.VMEM((n, width), d)
    sq = pltpu.VMEM((2, width, width), BF16)
    part = pltpu.VMEM((2, TILE, width), BF16)
    rows = lambda d: s((n, width), d)
    outs = [rows(BF16), rows(F32), rows(BF16), rows(BF16), rows(BF16), s((4, n, width), BF16), s((4, n, width), BF16), s((8, width), F32)]
    out_specs = [any_] * 7 + [vm]
    scratch = [big(BF16), big(BF16), big(BF16), big(F32), big(F32), big(F32), big(BF16), big(BF16), pltpu.VMEM((width, width), BF16),
               sq, sq, part, part, dma((4,)), dma((2, 2)), dma((2, 2)), dma((5,))]
    params = dict(vmem_limit_bytes=VMEM_BYTES)
    if remote:
        n_dev = width // weights[2].shape[1]
        outs += [s((3, width, width), BF16), s((3, width, width), BF16)]
        out_specs += [any_] * 2
        scratch += [dma((3, 2)), dma((3, 2, n_dev)), dma((3, 2))]
        params.update(collective_id=1, has_side_effects=True)
    return pl.pallas_call(
        functools.partial(mlp_kernel, remote), in_specs=[any_] * 6 + ([vm, any_] if remote else []) + [vm], out_specs=out_specs, out_shape=outs,
        scratch_shapes=scratch, compiler_params=pltpu.CompilerParams(**params), name="mlp",
    )(tokens, att, cot, wout, *weights, gs)[:8]


class Piece:
    def __init__(self, place, parts, total, recv, local, sems):
        self.p, self.parts, self.total, self.sems = place, parts, total, sems
        self.from_core, self.in1, self.in2, self.in3 = recv
        self.out1, self.keep1, self.out2, self.keep2, self.out3 = local

    def hop(self, i, src, dst, to):
        return pltpu.make_async_remote_copy(src_ref=src, dst_ref=dst, send_sem=self.sems.at[0, i], recv_sem=self.sems.at[1, i],
                                            device_id=to, device_id_type=MESH)

    def core(self):
        return self.hop(0, self.parts.at[:, 1 - self.p.c], self.from_core, self.p.partner)

    def h1(self):
        return self.hop(1, self.out1, self.in1, self.p.first2)

    def h2(self):
        return self.hop(2, self.out2, self.in2, self.p.second2)

    def h3(self, k):
        return self.hop(2 + k, self.out3.at[k - 1], self.in3.at[k - 1], self.p.id(z=self.p.z_at(k)))

    def t0(self):
        self.core().start()

    def t1(self):
        p = self.p
        self.core().wait_recv()

        def both(k):
            return self.parts[k, p.c].astype(F32) + self.from_core[k].astype(F32)

        def away(b, carry):
            self.out1[b] = both(p.block(1, b // 4, b % 4)).astype(BF16)
            return carry
        lax.fori_loop(0, 8, away, 0)
        self.h1().start()

        def here(b, carry):
            self.keep1[b] = both(p.block(0, b // 4, b % 4))
            return carry
        lax.fori_loop(0, 8, here, 0)
        self.core().wait_send()

    def t2(self):
        self.h1().wait_recv()

        def away(z, carry):
            self.out2[z] = (self.keep1[4 + z] + self.in1[4 + z].astype(F32)).astype(BF16)
            return carry
        lax.fori_loop(0, 4, away, 0)
        self.h2().start()

        def here(z, carry):
            self.keep2[z] = self.keep1[z] + self.in1[z].astype(F32)
            return carry
        lax.fori_loop(0, 4, here, 0)
        self.h1().wait_send()

    def t3(self):
        p = self.p
        self.h2().wait_recv()
        for k in (2, 1, 3):
            z = p.z_at(k)
            self.out3[k - 1] = (self.keep2[z] + self.in2[z].astype(F32)).astype(BF16)
            self.h3(k).start()
        self.keep2[p.z] = self.keep2[p.z] + self.in2[p.z].astype(F32)
        self.h2().wait_send()

    def t4(self):
        total = self.keep2[self.p.z]
        for k in (1, 3, 2):
            self.h3(k).wait_recv()
            total = total + self.in3[k - 1].astype(F32)
        rows, half = self.total.shape[0], total.shape[1]
        for i in range(self.total.shape[1] // half):
            self.total[:, i * half:(i + 1) * half] = total[i * rows:(i + 1) * rows]
        for k in (1, 2, 3):
            self.h3(k).wait_send()


class Sum:
    def __init__(self, place, stage, came, sems):
        self.p, self.stage, self.came, self.sems = place, stage, came, sems

    def hop(self, i):
        p = self.p
        to = [p.partner, p.first2, p.second2] + [p.id(z=p.z_at(k)) for k in (1, 2, 3)]
        return pltpu.make_async_remote_copy(src_ref=self.stage.at[min(i, 3)], dst_ref=self.came.at[i], send_sem=self.sems.at[0, i],
                                            recv_sem=self.sems.at[1, i], device_id=to[i], device_id_type=MESH)

    def step(self, i):
        self.hop(i).wait_recv()
        self.stage[i + 1] = self.stage[i] + self.came[i]
        for k in (i + 1,) if i < 2 else (3, 4, 5):
            self.hop(k).start()

    def finish(self):
        for i in (3, 4, 5):
            self.hop(i).wait_recv()
        for i in range(6):
            self.hop(i).wait_send()
        return self.stage[3] + self.came[3] + self.came[4] + self.came[5]


class ReducePlace(Place):
    def __init__(self):
        super().__init__()
        self.first2, self.second2 = self.second, self.first

    def block(self, df, ds, z):
        return self.slot_of(ds, df, z) // 2


AXES = ("dp", "fsdp")
U_OUT, U_PROJ, U_Q, U_END = 4, 5, 9, 12
LAST_ROWS = 32
DELAYS = (0, 1, 4, 6, 8)
RING_1, RING_2 = 4, 6
RECV = (16, 8, 4, 3)


def pack(g):
    half = g.shape[-1] // 2
    return jnp.concatenate([g[..., :half], g[..., half:]], axis=-2)


def grads_kernel(remote, tok_h, ghid_h, gq_h, gk_h, gv_h, w_h, act_h, gi_h, n2_h, cot_h, att_h, gb_h, gs_ref, stat_two, gtok_h, *refs):
    outs, (pool, gw, w, ghid, stat, insem, tsem, osem), refs = refs[:5], refs[5:13], refs[13:]
    stat_ref = outs[4]
    n, width = pool.shape[1:]
    fresh = w.shape[1] - 2 * width
    n_t = n // TILE
    gain, shift = gs_ref[0:1, :], gs_ref[2:3, :]

    def load(src, i):
        return pltpu.make_async_copy(src, pool.at[i], insem.at[i])

    def loaded(i):
        load(pool.at[i], i).wait()
    wload = pltpu.make_async_copy(w_h, w, insem.at[6])
    for i, src in enumerate((n2_h, gi_h.at[0], gi_h.at[1], att_h, gb_h, tok_h)):
        load(src, i).start()
    wload.start()
    if remote:
        plan, late, moving = reduce_plan(gw, outs, refs)
    else:
        (plan, late), moving = collect_plan(gw, outs, refs), lambda u: None
    loaded(0)

    def normalised():
        loaded(5)

        def tile(t, carry):
            r = tile_at(t)
            xhat, _ = normalise(pool[5, r, :].astype(F32))
            pool[3, r, :] = (xhat * gain + shift).astype(BF16)
            return carry
        lax.fori_loop(0, n_t, tile, 0)

    after = {0: [load(gi_h.at[2], 1).start], 1: [load(gi_h.at[3], 2).start], 2: [load(act_h.at[0], 1).start],
             3: [load(act_h.at[1], 2).start, load(cot_h, 0).start], U_OUT: [load(gq_h, 4).start, normalised],
             5: [load(act_h.at[2], 1).start], 6: [load(act_h.at[3], 2).start],
             8: [load(gk_h, 0).start, load(gv_h, 2).start]}

    def unit(u, carry):
        slot = u % 2
        ring = 1 + jnp.where(u < U_OUT, u, u - U_PROJ) % 2
        proj = (u >= U_PROJ) & (u < U_Q)
        lhs = jnp.where(u < U_OUT, 0, jnp.where(proj, ring, 3))
        rhs = jnp.where(u < U_OUT, ring, jnp.where((u == U_OUT) | (u == U_Q), 4, jnp.where(proj | (u == U_Q + 1), 0, 2)))

        @pl.when((u < U_OUT) | proj)
        def _():
            loaded(ring)

        for when, bufs in {U_OUT: (3, 4), U_PROJ: (0,), U_Q: (4,), U_Q + 1: (0,), U_Q + 2: (2,)}.items():
            @pl.when(u == when)
            def _():
                for b in bufs:
                    loaded(b)

        def rows(m, carry):
            c = pl.ds(pl.multiple_of(m * 384, 128), 384)
            g = dot_tn(pool[lhs, :, c], pool[rhs])
            gw[slot, pl.ds(m * 8, 8)] = pack(g.reshape(8, 2, 24, width)).astype(BF16)
            return carry
        lax.fori_loop(0, 2, rows, 0)
        moving(u)
        for when in range(U_END):
            steps = after.get(when, []) + plan.get(when, [])
            if steps:
                @pl.when(u == when)
                def _():
                    for s in steps:
                        s()
        return carry
    lax.fori_loop(0, U_END, unit, 0)
    wload.wait()
    stat[...] = jnp.zeros_like(stat)

    def gin(t):
        return pltpu.make_async_copy(ghid_h.at[tile_at(t), :], ghid.at[t % 2], tsem.at[t % 2])

    def gout(t):
        return pltpu.make_async_copy(ghid.at[t % 2], gtok_h.at[tile_at(t), :], osem.at[t % 2])

    gin(0).start()

    def tile(t, carry):
        r, slot = tile_at(t), t % 2
        g = (dot_nt(pool[4, r, :], w[:, :width]) + dot_nt(pool[0, r, :], w[:, width:2 * width])
             + dot_nt(pool[2, r, :fresh], w[:, 2 * width:]))
        gin(t).wait()

        @pl.when(t > 0)
        def _():
            gout(t - 1).wait()

        @pl.when(t + 1 < n_t)
        def _():
            gin(t + 1).start()
        xhat, rstd = normalise(pool[5, r, :].astype(F32))
        stat[0:1, :] += jnp.sum(g * xhat, axis=0, keepdims=True)
        stat[2:3, :] += jnp.sum(g, axis=0, keepdims=True)
        ghid[slot] += norm_back(g, xhat, rstd, gain)
        gout(t).start()
        moving(U_END + t)
        for when in range(n_t):
            steps = plan.get(U_END + when, [])
            if steps:
                @pl.when(t == when)
                def _():
                    for s in steps:
                        s()
        return carry
    lax.fori_loop(0, n_t, tile, 0)
    stat[...] = stat[...] + stat_two[...]
    late(stat)
    gout(n_t - 1).wait()


def collect_plan(gw, outs, refs):
    parts, stat_ref = outs[0], outs[4]
    sem = refs[0]

    def emit(u):
        def go():
            c = pltpu.make_async_copy(gw.at[u % 2], parts.at[u], sem)
            c.start()
            c.wait()
        return go

    def late(stat):
        stat_ref[...] = stat[...]
    return {u: [emit(u)] for u in range(U_END)}, late


def reduce_plan(gw, outs, refs):
    fc_t, proj_t, out_t, qkv_t, stat_ref = outs
    recv, local, (fcp, stage, came, sems, ssem) = refs[:4], refs[4:9], refs[9:]
    small, width = out_t.shape
    last = qkv_t.shape[1] - 2 * width
    place = ReducePlace()
    enter(place)
    dest = [fcp.at[u] for u in range(N_FF)] + [out_t] + [proj_t.at[pl.ds(u * small, small), :] for u in range(N_FF)] + [
        qkv_t.at[:, pl.ds(0, width)], qkv_t.at[:, pl.ds(width, width)], qkv_t.at[:, pl.ds(2 * width, last)]]
    pieces = []
    for u in range(U_END):
        whole = dest[u].shape[1] == width
        pick = lambda ref, *at: ref.at[at] if whole else ref.at[at + (slice(None),) * (len(ref.shape) - len(at) - 2) + (pl.ds(0, LAST_ROWS),)]
        bufs = [pick(b, u) for b in recv], [pick(b, u % (RING_1 if i < 2 else RING_2)) for i, b in enumerate(local)]
        pieces.append(Piece(place, pick(gw, u % 2), dest[u], *bufs, sems.at[u]))
    todo = [(u + d, -k, u) for u in range(U_END) for k, d in enumerate(DELAYS)]
    todo.sort(key=lambda e: (e[0], e[1] if e[1] else -9, e[2]))
    plan, rest = {}, []
    for when, neg, u in todo:
        step = getattr(pieces[u], "t%d" % -neg)
        if when < U_END + 4:
            if neg == -4 or u == U_END - 1:
                plan.setdefault(when, []).append(step)
        else:
            rest.append(step)
    sums = Sum(place, stage, came, ssem)

    def moving(time):
        for k in (0, 3, 2, 1):
            p = time - DELAYS[k]

            @pl.when((p >= 0) & (p < U_END - 1))
            def _():
                local_p = [b.at[p % (RING_1 if i < 2 else RING_2)] for i, b in enumerate(local)]
                getattr(Piece(place, gw.at[p % 2], None, [b.at[p] for b in recv], local_p, sems.at[p]), "t%d" % k)()

    def late(stat):
        stage[0] = stat[...]
        sums.hop(0).start()
        between = [lambda: sums.step(0), lambda: sums.step(1), lambda: sums.step(2)]
        fc_t[...] = spread_groups([fcp[j] for j in range(N_FF)], width // small, small)
        for step in rest:
            step()
            if between:
                between.pop(0)()
        for step in between:
            step()
        stat_ref[...] = sums.finish()
    return plan, late, moving


def grads(remote, tokens, ghid, gq, gk, gv, w, act, gi, n2, cot, att, gb, gs, stat):
    n, width = tokens.shape
    fresh = w.shape[1] - 2 * width
    small = 24
    ff = act.shape[0] * width
    s, dma = jax.ShapeDtypeStruct, pltpu.SemaphoreType.DMA
    any_, vm = pl.BlockSpec(memory_space=pl.ANY), pl.BlockSpec(memory_space=pltpu.VMEM)
    block = (2 * small, width // 2)
    outs = [s((n, width), F32)]
    scratch = [pltpu.VMEM((6, n, width), BF16), pltpu.VMEM((2, 16, 2) + block, BF16), pltpu.VMEM(w.shape, BF16), pltpu.VMEM((2, TILE, width), F32),
               pltpu.VMEM((8, width), F32), dma((7,)), dma((2,)), dma((2,))]
    params = dict(vmem_limit_bytes=VMEM_BYTES)
    if remote:
        outs += [s((small, ff), F32), s((ff // 32, width), F32), s((small, width), F32), s((small, w.shape[1]), F32)]
        specs = [vm] * 4
        scratch += [pltpu.VMEM((U_END, k) + block, BF16) for k in RECV]
        scratch += [pltpu.VMEM((r, k) + block, d) for r, k, d in ((RING_1, 8, BF16), (RING_1, 8, F32), (RING_2, 4, BF16), (RING_2, 4, F32), (RING_2, 3, BF16))]
        scratch += [pltpu.VMEM((N_FF, small, width), F32), pltpu.VMEM((4, 8, width), F32), pltpu.VMEM((6, 8, width), F32), dma((U_END, 2, 6)), dma((2, 6))]
        params.update(collective_id=2, has_side_effects=True)
    else:
        outs += [s((U_END, 16, 2) + block, BF16)] + [s((8, 128), F32)] * 3
        specs = [any_] * 4
        scratch += [dma(())]
    return pl.pallas_call(
        functools.partial(grads_kernel, remote), in_specs=[any_] * 12 + [vm] * 2, out_specs=[any_] + specs + [vm],
        out_shape=outs + [s((8, width), F32)], scratch_shapes=scratch,
        compiler_params=pltpu.CompilerParams(**params), name="grads",
    )(tokens, ghid, gq, gk, gv, w, act, gi, n2, cot, att, gb, gs, stat)


def unpack_parts(parts, width, fresh):
    p = parts.astype(F32).reshape(U_END, width // 24, 2, 24, width // 2).transpose(0, 1, 3, 2, 4).reshape(U_END, width, width)
    return (jnp.concatenate([p[U_Q], p[U_Q + 1], p[U_Q + 2, :, :fresh]], axis=1), p[U_OUT], jnp.concatenate(list(p[:N_FF]), axis=1),
            p[U_PROJ:U_Q].reshape(-1, width))


N_COPY = 8


def finish_kernel(tok, fc, proj, out, qkv, stat, tok_o, fc_o, proj_o, out_o, qkv_o, gain_o, shift_o, buf, isem, osem):
    n = tok.shape[0] // N_COPY
    rows = [pl.ds(i * n, n) for i in range(N_COPY)]
    loads = [pltpu.make_async_copy(tok.at[r, :], buf.at[r, :], isem.at[i]) for i, r in enumerate(rows)]
    stores = [pltpu.make_async_copy(buf.at[r, :], tok_o.at[r, :], osem.at[i]) for i, r in enumerate(rows)]
    for c in loads:
        c.start()
    fc_o[...], proj_o[...], out_o[...], qkv_o[...] = fc[...], proj[...], out[...], qkv[...]
    width, own = stat.shape[1], gain_o.shape[1]
    mine = pltpu.roll(stat[...], lax.rem(width - own * lax.axis_index(AXES), width), 1)
    gain_o[...] = mine[0:2, :own]
    shift_o[...] = mine[2:4, :own]
    for load, store in zip(loads, stores):
        load.wait()
        store.start()
    for c in stores:
        c.wait()


def finish(tok, fc, proj, out, qkv, stat, own):
    small = jax.ShapeDtypeStruct((2, own), F32)
    outs = [jax.ShapeDtypeStruct(a.shape, F32) for a in (tok, fc, proj, out, qkv)] + [small, small]
    any_, vm = pl.BlockSpec(memory_space=pl.ANY), pl.BlockSpec(memory_space=pltpu.VMEM)
    return pl.pallas_call(
        finish_kernel, in_specs=[any_] + [vm] * 5, out_specs=[any_] + [vm] * 6, out_shape=outs,
        scratch_shapes=[pltpu.VMEM(tok.shape, F32), pltpu.SemaphoreType.DMA((N_COPY,)), pltpu.SemaphoreType.DMA((N_COPY,))],
        compiler_params=pltpu.CompilerParams(vmem_limit_bytes=VMEM_BYTES), name="finish",
    )(tok, fc, proj, out, qkv, stat)


def body(direct, tokens, skip_values, w_qkv, w_out, w_fc, w_proj, norm_gains, norm_shifts, segment_ids, pad_mask, cotangent):
    micro, rows, length, width = tokens.shape
    half, ff = skip_values.shape[3], w_fc.shape[1]
    seqs = micro * rows
    n = seqs * length
    own = norm_gains.shape[1]
    flat = lambda a: a.reshape(n, a.shape[-1])
    seq = lambda a: a.reshape(seqs, length, a.shape[-1])
    tok, skip, cot = flat(tokens), flat(skip_values), flat(cotangent)
    seg, pad = segment_ids.reshape(seqs, 1, length), pad_mask.reshape(seqs, 1, length)
    if direct:
        q, k, v, gs, fcp, _, qkv, out, fc0, proj0 = start(tok, skip, norm_gains, norm_shifts, w_qkv, w_out, w_fc, w_proj)
        weights = (fc0, proj0, fcp, w_proj)
    else:
        qkv, out, *weights = [lax.all_gather(w, AXES, axis=0, tiled=True) for w in (w_qkv, w_out, w_fc, w_proj)]
        rows8 = jnp.concatenate([norm_gains, norm_shifts, jnp.zeros((4, own), BF16)], axis=0)
        gs = lax.all_gather(rows8, AXES, axis=1, tiled=True).astype(F32)
        q, k, v = project(tok, skip, qkv, gs)
    att, lse = attend(seq(q), seq(k), seq(v), seg, pad)
    att = flat(att)
    lout, ghid, gatt, n2, gb, act, gi, stat = mlp(direct, tok, att, cot, out, weights, gs)
    gq, gk, gv, gskip, lout = attend_back(seq(q), seq(k), seq(v), seq(gatt), lse, seg, pad, seq(lout), half)
    gtok, gfc, gproj, gout, gqkv, stat = grads(
        direct, tok, ghid, flat(gq), flat(gk), flat(gv), qkv, act, gi, n2, cot, att, gb, gs, stat)
    if direct:
        gtok, total_fc, total_proj, total_out, total_qkv, gains, shifts = finish(gtok, gfc, gproj, gout, gqkv, stat, own)
    else:
        total_qkv, total_out, total_fc, total_proj = [
            lax.psum_scatter(g, AXES, scatter_dimension=0, tiled=True) for g in unpack_parts(gfc, width, width - half)]
        gains = lax.psum_scatter(stat[0:2], AXES, scatter_dimension=1, tiled=True)
        shifts = lax.psum_scatter(stat[2:4], AXES, scatter_dimension=1, tiled=True)
    shape4 = lambda a: a.reshape(micro, rows, length, a.shape[-1])
    return (shape4(lout), shape4(gtok), shape4(gskip), total_qkv, total_out, total_fc, total_proj, gains, shifts)


def solution(mesh):
    tok, mat, row, ids = P(None, AXES, None, None), P(AXES, None), P(None, AXES), P(None, AXES, None)
    direct = dict(mesh.shape) == {"dp": 2, "fsdp": 16}
    return jax.shard_map(
        functools.partial(body, direct), mesh=mesh,
        in_specs=(tok, tok, mat, mat, mat, mat, row, row, ids, ids, tok),
        out_specs=(tok, tok, tok, mat, mat, mat, mat, row, row), check_vma=False)
```

```python
import functools
import jax
import jax.numpy as jnp
from jax import lax
from jax.experimental import pallas as pl
from jax.experimental.pallas import tpu as pltpu
from jax.sharding import PartitionSpec as P

F32, BF16 = jnp.float32, jnp.bfloat16

HEAD = 64
BLK = 128
WIN = 5
MASKED = -1e9
PAIRS_FWD, PAIRS_BWD = 6, 6


def build_bias(seg_row, pad_row, bias_ref, n_blk):
    code = jnp.where(pad_row == 1, seg_row, -1)
    key = lax.broadcasted_iota(jnp.int32, (BLK, BLK), 0)
    row = lax.broadcasted_iota(jnp.int32, (BLK, BLK), 1)
    for kb in range(n_blk):
        code_k = jnp.broadcast_to(code[:, kb * BLK:(kb + 1) * BLK], (BLK, BLK)).T
        for qb in range(kb, min(kb + WIN, n_blk)):
            vis = code_k == seg_row[:, qb * BLK:(qb + 1) * BLK]
            if kb == qb:
                vis = (vis & (key < row)) | (key == row)
            t = kb - qb + WIN - 1
            bias_ref[qb, t * BLK:(t + 1) * BLK, :] = jnp.where(vis, 0.0, MASKED)


def stack_heads(x):
    low = lax.broadcasted_iota(jnp.int32, x.shape, 1) < HEAD
    zero = jnp.zeros_like(x)
    return jnp.concatenate([jnp.where(low, x, zero), jnp.where(low, zero, x)], axis=0)


def join_heads(x2):
    return jnp.concatenate([x2[:HEAD, :BLK], x2[HEAD:, BLK:]], axis=0)


def twice(x):
    return jnp.concatenate([x, x], axis=1)


def visible_blocks(seg_s, row, qb):
    first = seg_s[row, 0, qb * BLK]
    n = jnp.int32(1)
    for back in range(1, WIN):
        kb = jnp.maximum(qb - back, 0)
        seen = (qb >= back) & (seg_s[row, 0, kb * BLK + BLK - 1] == first)
        n = n + seen.astype(jnp.int32)
    return n


def over_queries(seg_s, row, n_blk, one):
    def step(qb, carry):
        n_vis = visible_blocks(seg_s, row, qb)
        for n in range(1, WIN + 1):
            @pl.when(n_vis == n)
            def _():
                one(n, qb)
        return carry
    lax.fori_loop(0, n_blk, step, 0)


def block(i, n=1):
    return pl.ds(pl.multiple_of(i * BLK, BLK), n * BLK)


def attend_nt(a, b):
    return lax.dot_general(a, b, (((1,), (1,)), ((), ())), preferred_element_type=F32)


def fwd_kernel(n_blk, pairs, seg_s, seg_ref, pad_ref, q_ref, k_ref, v_ref, o_ref, lse_ref, bias_ref, vt_ref):
    row = pl.program_id(0)

    @pl.when(pl.program_id(1) == 0)
    def _():
        build_bias(seg_ref[...], pad_ref[...], bias_ref, n_blk)

    lanes = [slice(i * BLK, (i + 1) * BLK) for i in range(pairs)]
    for kb in range(n_blk):
        for h in lanes:
            vt_ref[h, kb * BLK:(kb + 1) * BLK] = v_ref[kb * BLK:(kb + 1) * BLK, h].T

    def one(n, qb):
        keys, here = block(qb - n + 1, n), block(qb)
        b = twice(bias_ref[qb, (WIN - n) * BLK:, :])
        s = [attend_nt(k_ref[keys, h], stack_heads(q_ref[here, h])) + b for h in lanes]
        for i, h in enumerate(lanes):
            m = jnp.max(s[i], axis=0, keepdims=True)
            p = jnp.exp(s[i] - m)
            total = jnp.sum(p, axis=0, keepdims=True)
            o2 = jnp.dot(vt_ref[h, keys], p.astype(BF16), preferred_element_type=F32) * (1.0 / total)
            o_ref[here, h] = join_heads(o2).astype(BF16).T
            lse_ref[i, qb] = m + jnp.log(total)
    over_queries(seg_s, row, n_blk, one)


def attend(q, k, v, seg, pad):
    rows, length, width = q.shape
    n_blk, pairs = length // BLK, PAIRS_FWD
    groups = width // 128 // pairs
    tok = pl.BlockSpec((None, length, pairs * 128), lambda r, h, s: (r, 0, h))
    ids = pl.BlockSpec((None, 1, length), lambda r, h, s: (r, 0, 0))
    return pl.pallas_call(
        functools.partial(fwd_kernel, n_blk, pairs),
        grid_spec=pltpu.PrefetchScalarGridSpec(
            num_scalar_prefetch=1, grid=(rows, groups),
            in_specs=[ids, ids, tok, tok, tok],
            out_specs=[tok, pl.BlockSpec((None, pairs, n_blk, 1, 2 * BLK), lambda r, h, s: (r, h, 0, 0, 0))],
            scratch_shapes=[pltpu.VMEM((n_blk, WIN * BLK, BLK), F32), pltpu.VMEM((pairs * BLK, length), BF16)]),
        out_shape=[jax.ShapeDtypeStruct((rows, length, width), BF16), jax.ShapeDtypeStruct((rows, width // 128, n_blk, 1, 2 * BLK), F32)],
        compiler_params=pltpu.CompilerParams(dimension_semantics=("arbitrary", "arbitrary"), vmem_limit_bytes=64000 << 10),
        name="attend",
    )(seg, seg, pad, q, k, v)


def bwd_kernel(n_blk, pairs, seg_s, seg_ref, pad_ref, q_ref, k_ref, v_ref, g_ref, lse_ref, result_ref, dq_ref, dk_ref, dv_ref, dskip_ref, result_out,
               bias_ref, kt_ref, dk_acc, dv_acc):
    row = pl.program_id(0)
    result_out[...] = result_ref[...]

    @pl.when(pl.program_id(1) == 0)
    def _():
        build_bias(seg_ref[...], pad_ref[...], bias_ref, n_blk)

    lanes = [slice(i * BLK, (i + 1) * BLK) for i in range(pairs)]
    for kb in range(n_blk):
        for h in lanes:
            kt_ref[h, kb * BLK:(kb + 1) * BLK] = k_ref[kb * BLK:(kb + 1) * BLK, h].T
    dk_acc[...] = jnp.zeros_like(dk_acc)
    dv_acc[...] = jnp.zeros_like(dv_acc)

    def one(n, qb):
        keys, here = block(qb - n + 1, n), block(qb)
        b = twice(bias_ref[qb, (WIN - n) * BLK:, :])
        for i, h in enumerate(lanes):
            q2, g2 = stack_heads(q_ref[here, h]), stack_heads(g_ref[here, h])
            p = jnp.exp(attend_nt(k_ref[keys, h], q2) + b - lse_ref[i, qb])
            dp = attend_nt(v_ref[keys, h], g2)
            inner = jnp.sum(p * dp, axis=0, keepdims=True)
            ds = (p * (dp - inner)).astype(BF16)
            dv_acc[keys, h] += jnp.dot(p.astype(BF16), g2, preferred_element_type=F32)
            dk_acc[keys, h] += jnp.dot(ds, q2, preferred_element_type=F32)
            dq2 = jnp.dot(kt_ref[h, keys], ds, preferred_element_type=F32)
            dq_ref[here, h] = (join_heads(dq2) * 0.125).astype(BF16).T
    over_queries(seg_s, row, n_blk, one)
    dk_ref[...] = dk_acc[...].astype(BF16)
    dv_ref[...] = dv_acc[...].astype(BF16)

    @pl.when(pl.program_id(1) == pl.num_programs(1) - 1)
    def _():
        dskip_ref[...] = dv_ref[:, dv_ref.shape[1] - dskip_ref.shape[1]:].astype(F32)


def attend_back(q, k, v, g, lse, seg, pad, result, half):
    rows, length, width = q.shape
    n_blk, pairs = length // BLK, PAIRS_BWD
    groups = width // 128 // pairs
    tok = pl.BlockSpec((None, length, pairs * 128), lambda r, h, s: (r, 0, h))
    ids = pl.BlockSpec((None, 1, length), lambda r, h, s: (r, 0, 0))
    out = jax.ShapeDtypeStruct((rows, length, width), BF16)
    return pl.pallas_call(
        functools.partial(bwd_kernel, n_blk, pairs),
        grid_spec=pltpu.PrefetchScalarGridSpec(
            num_scalar_prefetch=1, grid=(rows, groups),
            in_specs=[ids, ids, tok, tok, tok, tok, pl.BlockSpec((None, pairs, n_blk, 1, 2 * BLK), lambda r, h, s: (r, h, 0, 0, 0)), tok],
            out_specs=[tok, tok, tok, pl.BlockSpec((None, length, half), lambda r, h, s: (r, 0, 0)), tok],
            scratch_shapes=[pltpu.VMEM((n_blk, WIN * BLK, BLK), F32), pltpu.VMEM((pairs * BLK, length), BF16),
                            pltpu.VMEM((length, pairs * BLK), F32), pltpu.VMEM((length, pairs * BLK), F32)]),
        out_shape=[out, out, out, jax.ShapeDtypeStruct((rows, length, half), F32), out],
        compiler_params=pltpu.CompilerParams(dimension_semantics=("arbitrary", "arbitrary"), vmem_limit_bytes=64000 << 10),
        name="attend_back",
    )(seg, seg, pad, q, k, v, g, lse, result)


MESH = pl.DeviceIdType.MESH
NZ = 4


class Place:
    def __init__(self):
        dp, fs = lax.axis_index("dp"), lax.axis_index("fsdp")
        self.x, self.z, self.y, self.c = dp, fs // 4, (fs // 2) % 2, fs % 2
        self.slot = self.x * 16 + fs
        self.first = self.id(x=jnp.where(self.c == 0, 1 - self.x, self.x), y=jnp.where(self.c == 0, self.y, 1 - self.y))
        self.second = self.id(x=jnp.where(self.c == 0, self.x, 1 - self.x), y=jnp.where(self.c == 0, 1 - self.y, self.y))
        self.partner = self.id(c=1 - self.c)

    def id(self, x=None, y=None, z=None, c=None):
        x = self.x if x is None else x
        y = self.y if y is None else y
        z = self.z if z is None else z
        c = self.c if c is None else c
        return (x, z * 4 + y * 2 + c)

    def z_at(self, k):
        return (self.z + k) % NZ

    def peers(self):
        return [self.partner, self.first, self.second] + [self.id(z=self.z_at(k)) for k in (1, 2, 3)]

    def slot_of(self, df, ds, z):
        dx = jnp.where(self.c == 0, df, ds)
        dy = jnp.where(self.c == 0, ds, df)
        x = jnp.where(dx == 1, 1 - self.x, self.x)
        y = jnp.where(dy == 1, 1 - self.y, self.y)
        return x * 16 + z * 4 + y * 2 + self.c


def enter(place):
    bar = pltpu.get_barrier_semaphore()
    for peer in place.peers():
        pl.semaphore_signal(bar, inc=1, device_id=peer, device_id_type=MESH)
    pl.semaphore_wait(bar, 6)


class Gather:
    SENDS = 31

    def __init__(self, place, shard, out, send, recv, own):
        self.p, self.shard, self.out, self.send, self.recv, self.own = place, shard, out, send, recv, own
        self.size = shard.shape[0]

    def at(self, slot, n=1):
        return self.out.at[pl.ds(pl.multiple_of(slot * self.size, 8), n * self.size), :]

    def push(self, src, slot, to):
        pltpu.make_async_remote_copy(src_ref=src, dst_ref=self.at(slot), send_sem=self.send, recv_sem=self.recv.at[slot],
                                     device_id=to, device_id_type=MESH).start()

    def arrived(self, slot):
        pltpu.make_async_copy(self.at(slot), self.at(slot), self.recv.at[slot]).wait()

    def keep(self, slot):
        return pltpu.make_async_copy(self.shard, self.at(slot), self.own)

    def s1(self):
        p = self.p
        self.keep(p.slot).start()
        for k in (1, 3, 2):
            self.push(self.shard, p.slot, p.id(z=p.z_at(k)))
        for to in (p.first, p.partner, p.second):
            self.push(self.shard, p.slot, to)

    def each(self, n, slot_at, targets):
        def go(i, carry):
            slot = slot_at(i)
            self.arrived(slot)
            for to in targets:
                self.push(self.at(slot), slot, to)
            return carry
        lax.fori_loop(0, n, go, 0)

    def s2(self):
        p = self.p
        self.each(3, lambda i: p.slot_of(0, 0, p.z_at(i + 1)), (p.first, p.second, p.partner))

    def s3(self):
        p = self.p
        self.each(4, lambda i: p.slot_of(1, 0, p.z_at(i)), (p.second, p.partner))

    def s4(self):
        p = self.p
        self.each(8, lambda i: p.slot_of(i // 4, 1, p.z_at(i % 4)), (p.partner,))

    def s5(self):
        self.each(16, lambda i: 2 * i + 1 - self.p.c, ())
        self.keep(self.p.slot).wait()

    def drain(self):
        done = self.at(0, self.SENDS)
        pltpu.make_async_copy(done, done, self.send).wait()


VMEM_BYTES = 64000 << 10
TILE = 512
SMALL_TILE = 256
EPS = 1e-5
GELU_C = 0.7978845608028654
GELU_A = 0.044715


def dot(a, b):
    return jnp.dot(a, b, preferred_element_type=F32)


def dot_nt(a, b):
    return lax.dot_general(a, b, (((1,), (1,)), ((), ())), preferred_element_type=F32)


def dot_tn(a, b):
    return lax.dot_general(a, b, (((0,), (0,)), ((), ())), preferred_element_type=F32)


def normalise(v):
    centred = v - jnp.mean(v, axis=-1, keepdims=True)
    rstd = lax.rsqrt(jnp.mean(centred * centred, axis=-1, keepdims=True) + EPS)
    return centred * rstd, rstd


def norm_back(g, xhat, rstd, gain):
    gh = g * gain
    return rstd * (gh - jnp.mean(gh, axis=-1, keepdims=True) - xhat * jnp.mean(gh * xhat, axis=-1, keepdims=True))


def gelu_both(u, grad):
    sq = u * u
    t = jnp.tanh(u * (GELU_C + (GELU_C * GELU_A) * sq))
    half = 0.5 + 0.5 * t
    act = u * half
    slope = half + act * (1.0 - half) * (2.0 * GELU_C + (6.0 * GELU_C * GELU_A) * sq)
    return act, grad * slope


def tile_at(t):
    return pl.ds(pl.multiple_of(t * TILE, TILE), TILE)


def qkv_kernel(tok_ref, skip_ref, w_ref, gs_ref, q_ref, k_ref, v_ref):
    width, half = tok_ref.shape[1], skip_ref.shape[1]
    xhat, _ = normalise(tok_ref[...].astype(F32))
    normed = (xhat * gs_ref[0:1, :] + gs_ref[2:3, :]).astype(BF16)
    q_ref[...] = (dot(normed, w_ref[:, :width]) * 0.125).astype(BF16)
    k_ref[...] = dot(normed, w_ref[:, width:2 * width]).astype(BF16)
    v_ref[:, :half] = dot(normed, w_ref[:, 2 * width:]).astype(BF16)
    v_ref[:, half:] = skip_ref[...]


def project(tokens, skip, w, gs):
    n, width = tokens.shape
    row = lambda c: pl.BlockSpec((TILE, c), lambda t: (t, 0))
    whole = lambda a: pl.BlockSpec(a.shape, lambda t: (0, 0))
    out = jax.ShapeDtypeStruct((n, width), BF16)
    return pl.pallas_call(
        qkv_kernel, grid=(n // TILE,), in_specs=[row(width), row(skip.shape[1]), whole(w), whole(gs)],
        out_specs=[row(width)] * 3, out_shape=[out] * 3,
        compiler_params=pltpu.CompilerParams(vmem_limit_bytes=VMEM_BYTES), name="project",
    )(tokens, skip, w, gs)


def lane_mod(x, period):
    return jnp.broadcast_to(lax.rem(lax.broadcasted_iota(jnp.int32, (1, x.shape[1]), 1), jnp.int32(period)), x.shape)


def gather_groups(x, groups, size, parts):
    out = []
    total = x.shape[1]
    for j in range(parts):
        y = pltpu.roll(x, total - j * size, 1) if j else x
        span = size
        while span < groups * size:
            m = lane_mod(y, 2 * parts * span)
            y = jnp.where((m >= span) & (m < 2 * span), pltpu.roll(y, total - (parts - 1) * span, 1), y)
            span *= 2
        out.append(y[:, :groups * size])
    return out


def spread_groups(pieces, groups, size):
    parts = len(pieces)
    out = None
    for j, piece in enumerate(pieces):
        y = jnp.concatenate([piece] + [jnp.zeros_like(piece)] * (parts - 1), axis=1)
        span = groups * size
        while span > size:
            span //= 2
            m = lane_mod(y, 2 * parts * span)
            y = jnp.where((m >= parts * span) & (m < (parts + 1) * span), pltpu.roll(y, (parts - 1) * span, 1), y)
        y = pltpu.roll(y, j * size, 1) if j else y
        m = lane_mod(y, parts * size)
        y = jnp.where((m >= j * size) & (m < (j + 1) * size), y, 0.0)
        out = y if out is None else out + y
    return out


N_FF = 4


def start_kernel(tok_h, skip_h, gain_ref, shift_ref, qkv_ref, out_ref, fc_ref, proj_h,
                 q_h, k_h, v_h, gs_ref, fcp_ref, gs_all, qkv_all, out_all, fc_all, proj_all,
                 tok, skip, xhat, w, gsb, q, k, v, normed, rows_ref, insem, osem, send, recv, own):
    n, width = tok.shape
    half = skip.shape[1]
    n_t = n // TILE
    n_dev = qkv_all.shape[0] // qkv_ref.shape[0]
    size = proj_h.shape[0] // N_FF
    place = Place()
    loads = [pltpu.make_async_copy(tok_h, tok, insem.at[0]), pltpu.make_async_copy(skip_h, skip, insem.at[1])]
    for c in loads:
        c.start()
    enter(place)
    cols = [pl.ds(0, width), pl.ds(width, width), pl.ds(2 * width, half)]
    shards = (rows_ref, *[qkv_ref.at[:, c] for c in cols], out_ref, fcp_ref.at[0], proj_h.at[pl.ds(0, size), :])
    outs = (gs_all, *[qkv_all.at[:, c] for c in cols], out_all, fc_all, proj_all)
    jobs = [Gather(place, s, o, send.at[i], recv.at[i], own.at[i]) for i, (s, o) in enumerate(zip(shards, outs))]
    rows, wq, wk, wv, out, fc, proj = jobs
    wq.s1()
    mine = jnp.concatenate([gain_ref[...], shift_ref[...]], axis=0)
    lane = lax.broadcasted_iota(jnp.int32, (mine.shape[1], width), 1) - mine.shape[1] * place.slot
    spot = (lane == lax.broadcasted_iota(jnp.int32, lane.shape, 0)).astype(BF16)
    rows_ref[0:4, :] = dot(mine, spot).astype(BF16)
    rows_ref[4:8, :] = jnp.zeros((4, width), BF16)
    wk.s1(), wv.s1()
    for j, piece in enumerate(gather_groups(fc_ref[...].astype(F32), n_dev, size, N_FF)):
        fcp_ref[j] = piece.astype(BF16)
    rows.s1()
    for c in loads:
        c.wait()

    def centre(t, carry):
        r = tile_at(t)
        xhat[r, :], _ = normalise(tok[r, :].astype(F32))
        return carry
    lax.fori_loop(0, n_t // 2, centre, 0)
    wq.s2(), wk.s2(), wv.s2(), rows.s2(), out.s1()
    wq.s3(), wk.s3(), rows.s3(), wv.s3()
    lax.fori_loop(n_t // 2, n_t, centre, 0)
    fc.s1(), proj.s1()
    wq.s4(), rows.s4(), wk.s4(), out.s2(), wq.s5(), rows.s5()
    wloads = [pltpu.make_async_copy(qkv_all.at[:, c], w.at[:, c], insem.at[4 + i]) for i, c in enumerate(cols)]
    gload = pltpu.make_async_copy(gs_all, gsb, insem.at[3])
    wloads[0].start(), gload.start()
    wv.s4(), fc.s2(), proj.s2()
    gload.wait()
    gs_ref[...] = jnp.sum(gsb[...].astype(F32).reshape(n_dev, 8, width), axis=0)
    wloads[0].wait()

    def copies(r):
        return [pltpu.make_async_copy(s.at[r, :], h.at[r, :], osem.at[i]) for i, (s, h) in enumerate([(q, q_h), (k, k_h), (v, v_h)])]

    def third(i, put):
        def tile(t, carry):
            r = pl.ds(pl.multiple_of(t * SMALL_TILE, SMALL_TILE), SMALL_TILE)
            put(r)
            copies(r)[i].start()
            return carry
        lax.fori_loop(0, n // SMALL_TILE, tile, 0)

    def put_q(r):
        normed[r, :] = (xhat[r, :] * gs_ref[0:1, :] + gs_ref[2:3, :]).astype(BF16)
        q[r, :] = (dot(normed[r, :], w[:, :width]) * 0.125).astype(BF16)

    def put_k(r):
        k[r, :] = dot(normed[r, :], w[:, width:2 * width]).astype(BF16)

    def put_v(r):
        v[r, :half] = dot(normed[r, :], w[:, 2 * width:]).astype(BF16)
        v[r, half:] = skip[r, :]
    third(0, put_q)
    out.s3(), wk.s5()
    wloads[1].start()
    wv.s5()
    wloads[2].start()
    fc.s3()
    wloads[1].wait()
    third(1, put_k)
    proj.s3(), out.s4()
    wloads[2].wait()
    third(2, put_v)
    fc.s4(), out.s5(), proj.s4(), fc.s5(), proj.s5()
    for job in jobs:
        job.drain()
    for c in copies(pl.ds(0, n)):
        c.wait()


def start(tokens, skip, gains, shifts, qkv, out, fc, proj):
    n, width = tokens.shape
    n_dev = width // out.shape[0]
    s, dma = jax.ShapeDtypeStruct, pltpu.SemaphoreType.DMA
    any_, vm = pl.BlockSpec(memory_space=pl.ANY), pl.BlockSpec(memory_space=pltpu.VMEM)
    big = lambda d: pltpu.VMEM((n, width), d)
    act = s((n, width), BF16)
    gathered = [(8 * n_dev, width), (width, qkv.shape[1]), (width, width), (width, width), (width, width)]
    return pl.pallas_call(
        start_kernel, in_specs=[any_, any_] + [vm] * 5 + [any_], out_specs=[any_] * 3 + [vm] * 2 + [any_] * 5,
        out_shape=[act] * 3 + [s((8, width), F32), s((N_FF, fc.shape[0], width), BF16)] + [s(g, BF16) for g in gathered],
        scratch_shapes=[big(BF16), pltpu.VMEM(skip.shape, BF16), big(F32), pltpu.VMEM((width, qkv.shape[1]), BF16), pltpu.VMEM((8 * n_dev, width), BF16),
                        big(BF16), big(BF16), big(BF16), big(BF16), pltpu.VMEM((8, width), BF16), dma((7,)), dma((3,)), dma((7,)), dma((7, n_dev)), dma((7,))],
        compiler_params=pltpu.CompilerParams(vmem_limit_bytes=VMEM_BYTES, collective_id=0, has_side_effects=True), name="start",
    )(tokens, skip, gains, shifts, qkv, out, fc, proj)


MLP_STEPS = {1: (-1, 0, 1, 2), 2: (1, 2, 4, 6), 3: (3, 5, 7, 9)}


def mlp_kernel(remote, tok_h, att_h, cot_h, wout_h, *refs):
    if remote:
        fc0_h, proj0_h, fcp_ref, proj_ref, *refs = refs
    else:
        wfc_h, wproj_h, *refs = refs
    (gs_ref, lout_h, ghid_h, gatt_h, n2_h, gb_h, act_h, gi_h, stat_ref), refs = refs[:9], refs[9:]
    if remote:
        (fc_all, proj_all), refs = refs[:2], refs[2:]
    (tok, att, cot, hidden, oacc, gacc, n2, gb, wout, wfc, wproj, act, gi, insem, wsem, asem, osem), sems = refs[:17], refs[17:]
    n, width = tok.shape
    n_ff = N_FF
    n_t = n // TILE
    gain, shift = gs_ref[1:2, :], gs_ref[3:4, :]

    def load(src_fc, src_proj, slot):
        return (pltpu.make_async_copy(src_fc, wfc.at[slot], wsem.at[0, slot]), pltpu.make_async_copy(src_proj, wproj.at[slot], wsem.at[1, slot]))

    loads = [pltpu.make_async_copy(h, v, insem.at[i]) for i, (h, v) in enumerate([(wout_h, wout), (att_h, att), (tok_h, tok), (cot_h, cot)])]
    for c in loads:
        c.start()
    plan = {}
    if remote:
        send, recv, own = sems
        place = Place()
        enter(place)
        size = proj_ref.shape[0] // n_ff
        sets = []
        for i in range(1, n_ff):
            srcs = (fcp_ref.at[i], proj_ref.at[pl.ds(i * size, size), :])
            sets.append([Gather(place, srcs[k], (fc_all, proj_all)[k].at[i - 1], send.at[i - 1, k], recv.at[i - 1, k], own.at[i - 1, k]) for k in range(2)])

        def run(i, step):
            return lambda: [getattr(job, step)() for job in sets[i - 1]]

        def fetch(i):
            def go():
                for c in load(fc_all.at[i - 1], proj_all.at[i - 1], i % 2):
                    c.start()
            return go
        for i in range(1, n_ff):
            run(i, "s1")()
        early = []
        for i, steps in MLP_STEPS.items():
            for when, name in zip(steps, ("s2", "s3", "s4", "s5")):
                (early if when < 0 else plan.setdefault(when, [])).append(run(i, name))
            plan[steps[3]].append(fetch(i))
        for c in load(fc0_h, proj0_h, 0):
            c.start()
    else:
        early = []
        cols = lambda j: pl.ds(j * width, width)
        for i in range(1, n_ff):
            def fetch(i=i):
                for c in load(wfc_h.at[:, cols(i)], wproj_h.at[cols(i), :], i % 2):
                    c.start()
            plan[(i - 1) * n_t + 3] = [fetch]
        for c in load(wfc_h.at[:, cols(0)], wproj_h.at[cols(0), :], 0):
            c.start()
    for c in loads[:3]:
        c.wait()

    def out_copy(v, h, r, i):
        return pltpu.make_async_copy(v.at[r, :], h.at[r, :], osem.at[i])

    def forward(t, carry):
        r = pl.ds(pl.multiple_of(t * SMALL_TILE, SMALL_TILE), SMALL_TILE)
        h = tok[r, :].astype(F32) + dot(att[r, :], wout[...])
        hidden[r, :] = h
        oacc[r, :] = h
        gacc[r, :] = jnp.zeros_like(h)
        xhat, _ = normalise(h)
        n2[r, :] = (xhat * gain + shift).astype(BF16)
        out_copy(n2, n2_h, r, 3).start()
        return carry
    lax.fori_loop(0, n // SMALL_TILE, forward, 0)
    for step in early:
        step()
    loads[3].wait()

    def saves(i, t, slot):
        return (pltpu.make_async_copy(act.at[slot], act_h.at[i, tile_at(t), :], asem.at[0, slot]),
                pltpu.make_async_copy(gi.at[slot], gi_h.at[i, tile_at(t), :], asem.at[1, slot]))

    def tile(step, carry):
        i, t, slot = step // n_t, step % n_t, step % 2
        ws = i % 2
        r = tile_at(t)

        @pl.when(t == 0)
        def _():
            for c in load(wfc.at[ws], wproj.at[ws], ws):
                c.wait()

        @pl.when(step >= 2)
        def _():
            for c in saves(i, t, slot):
                c.wait()
        a, g = gelu_both(dot(n2[r, :], wfc[ws]), dot_nt(cot[r, :], wproj[ws]))
        a, g = a.astype(BF16), g.astype(BF16)
        act[slot] = a
        gi[slot] = g
        oacc[r, :] += dot(a, wproj[ws])
        gacc[r, :] += dot_nt(g, wfc[ws])
        for c in saves(i, t, slot):
            c.start()
        for when, steps in plan.items():
            @pl.when(step == when)
            def _():
                for s in steps:
                    s()
        return carry
    lax.fori_loop(0, n_ff * n_t, tile, 0)
    stat_ref[...] = jnp.zeros_like(stat_ref)

    def backward(t, carry):
        r = pl.ds(pl.multiple_of(t * SMALL_TILE, SMALL_TILE), SMALL_TILE)
        tok[r, :] = oacc[r, :].astype(BF16)
        xhat, rstd = normalise(hidden[r, :])
        g = gacc[r, :]
        stat_ref[1:2, :] += jnp.sum(g * xhat, axis=0, keepdims=True)
        stat_ref[3:4, :] += jnp.sum(g, axis=0, keepdims=True)
        gh = cot[r, :].astype(F32) + norm_back(g, xhat, rstd, gain)
        hidden[r, :] = gh
        b = gh.astype(BF16)
        gb[r, :] = b
        att[r, :] = dot_nt(b, wout[...]).astype(BF16)
        for i, (v, h) in enumerate([(tok, lout_h), (hidden, ghid_h), (att, gatt_h)]):
            out_copy(v, h, r, i).start()
        out_copy(gb, gb_h, r, 4).start()
        return carry
    lax.fori_loop(0, n // SMALL_TILE, backward, 0)
    if remote:
        for job in sets[0] + sets[1] + sets[2]:
            job.drain()
    for slot in range(2):
        for c in saves(0, 0, slot):
            c.wait()
    for i, (v, h) in enumerate([(tok, lout_h), (hidden, ghid_h), (att, gatt_h), (n2, n2_h), (gb, gb_h)]):
        out_copy(v, h, pl.ds(0, n), i).wait()


def mlp(remote, tokens, att, cot, wout, weights, gs):
    n, width = tokens.shape
    s, dma = jax.ShapeDtypeStruct, pltpu.SemaphoreType.DMA
    any_, vm = pl.BlockSpec(memory_space=pl.ANY), pl.BlockSpec(memory_space=pltpu.VMEM)
    big = lambda d: pltpu.VMEM((n, width), d)
    sq = pltpu.VMEM((2, width, width), BF16)
    part = pltpu.VMEM((2, TILE, width), BF16)
    rows = lambda d: s((n, width), d)
    outs = [rows(BF16), rows(F32), rows(BF16), rows(BF16), rows(BF16), s((4, n, width), BF16), s((4, n, width), BF16), s((8, width), F32)]
    out_specs = [any_] * 7 + [vm]
    scratch = [big(BF16), big(BF16), big(BF16), big(F32), big(F32), big(F32), big(BF16), big(BF16), pltpu.VMEM((width, width), BF16),
               sq, sq, part, part, dma((4,)), dma((2, 2)), dma((2, 2)), dma((5,))]
    params = dict(vmem_limit_bytes=VMEM_BYTES)
    if remote:
        n_dev = width // weights[2].shape[1]
        outs += [s((3, width, width), BF16), s((3, width, width), BF16)]
        out_specs += [any_] * 2
        scratch += [dma((3, 2)), dma((3, 2, n_dev)), dma((3, 2))]
        params.update(collective_id=1, has_side_effects=True)
    return pl.pallas_call(
        functools.partial(mlp_kernel, remote), in_specs=[any_] * 6 + ([vm, any_] if remote else []) + [vm], out_specs=out_specs, out_shape=outs,
        scratch_shapes=scratch, compiler_params=pltpu.CompilerParams(**params), name="mlp",
    )(tokens, att, cot, wout, *weights, gs)[:8]


class Piece:
    def __init__(self, place, parts, total, recv, local, sems):
        self.p, self.parts, self.total, self.sems = place, parts, total, sems
        self.from_core, self.in1, self.in2, self.in3 = recv
        self.out1, self.keep1, self.out2, self.keep2, self.out3 = local

    def hop(self, i, src, dst, to):
        return pltpu.make_async_remote_copy(src_ref=src, dst_ref=dst, send_sem=self.sems.at[0, i], recv_sem=self.sems.at[1, i],
                                            device_id=to, device_id_type=MESH)

    def core(self):
        return self.hop(0, self.parts.at[:, 1 - self.p.c], self.from_core, self.p.partner)

    def h1(self):
        return self.hop(1, self.out1, self.in1, self.p.first2)

    def h2(self):
        return self.hop(2, self.out2, self.in2, self.p.second2)

    def h3(self, k):
        return self.hop(2 + k, self.out3.at[k - 1], self.in3.at[k - 1], self.p.id(z=self.p.z_at(k)))

    def t0(self):
        self.core().start()

    def t1(self):
        p = self.p
        self.core().wait_recv()

        def both(k):
            return self.parts[k, p.c].astype(F32) + self.from_core[k].astype(F32)

        def away(b, carry):
            self.out1[b] = both(p.block(1, b // 4, b % 4)).astype(BF16)
            return carry
        lax.fori_loop(0, 8, away, 0)
        self.h1().start()

        def here(b, carry):
            self.keep1[b] = both(p.block(0, b // 4, b % 4))
            return carry
        lax.fori_loop(0, 8, here, 0)
        self.core().wait_send()

    def t2(self):
        self.h1().wait_recv()

        def away(z, carry):
            self.out2[z] = (self.keep1[4 + z] + self.in1[4 + z].astype(F32)).astype(BF16)
            return carry
        lax.fori_loop(0, 4, away, 0)
        self.h2().start()

        def here(z, carry):
            self.keep2[z] = self.keep1[z] + self.in1[z].astype(F32)
            return carry
        lax.fori_loop(0, 4, here, 0)
        self.h1().wait_send()

    def t3(self):
        p = self.p
        self.h2().wait_recv()
        for k in (2, 1, 3):
            z = p.z_at(k)
            self.out3[k - 1] = (self.keep2[z] + self.in2[z].astype(F32)).astype(BF16)
            self.h3(k).start()
        self.keep2[p.z] = self.keep2[p.z] + self.in2[p.z].astype(F32)
        self.h2().wait_send()

    def t4(self):
        total = self.keep2[self.p.z]
        for k in (1, 3, 2):
            self.h3(k).wait_recv()
            total = total + self.in3[k - 1].astype(F32)
        rows, half = self.total.shape[0], total.shape[1]
        for i in range(self.total.shape[1] // half):
            self.total[:, i * half:(i + 1) * half] = total[i * rows:(i + 1) * rows]
        for k in (1, 2, 3):
            self.h3(k).wait_send()


class Sum:
    def __init__(self, place, stage, came, sems):
        self.p, self.stage, self.came, self.sems = place, stage, came, sems

    def hop(self, i):
        p = self.p
        to = [p.partner, p.first2, p.second2] + [p.id(z=p.z_at(k)) for k in (1, 2, 3)]
        return pltpu.make_async_remote_copy(src_ref=self.stage.at[min(i, 3)], dst_ref=self.came.at[i], send_sem=self.sems.at[0, i],
                                            recv_sem=self.sems.at[1, i], device_id=to[i], device_id_type=MESH)

    def step(self, i):
        self.hop(i).wait_recv()
        self.stage[i + 1] = self.stage[i] + self.came[i]
        for k in (i + 1,) if i < 2 else (3, 4, 5):
            self.hop(k).start()

    def finish(self):
        for i in (3, 4, 5):
            self.hop(i).wait_recv()
        for i in range(6):
            self.hop(i).wait_send()
        return self.stage[3] + self.came[3] + self.came[4] + self.came[5]


class ReducePlace(Place):
    def __init__(self):
        super().__init__()
        self.first2, self.second2 = self.second, self.first

    def block(self, df, ds, z):
        return self.slot_of(ds, df, z) // 2


AXES = ("dp", "fsdp")
U_OUT, U_PROJ, U_Q, U_END = 4, 5, 9, 12
LAST_ROWS = 32
DELAYS = (0, 1, 4, 6, 8)
RING_1, RING_2 = 4, 6
RECV = (16, 8, 4, 3)


def pack(g):
    half = g.shape[-1] // 2
    return jnp.concatenate([g[..., :half], g[..., half:]], axis=-2)


def grads_kernel(remote, tok_h, ghid_h, gq_h, gk_h, gv_h, w_h, act_h, gi_h, n2_h, cot_h, att_h, gb_h, gs_ref, stat_two, gtok_h, *refs):
    outs, (pool, gw, w, ghid, stat, insem, tsem, osem), refs = refs[:5], refs[5:13], refs[13:]
    stat_ref = outs[4]
    n, width = pool.shape[1:]
    fresh = w.shape[1] - 2 * width
    n_t = n // TILE
    gain, shift = gs_ref[0:1, :], gs_ref[2:3, :]

    def load(src, i):
        return pltpu.make_async_copy(src, pool.at[i], insem.at[i])

    def loaded(i):
        load(pool.at[i], i).wait()
    wload = pltpu.make_async_copy(w_h, w, insem.at[6])
    for i, src in enumerate((n2_h, gi_h.at[0], gi_h.at[1], att_h, gb_h, tok_h)):
        load(src, i).start()
    wload.start()
    if remote:
        plan, late, moving = reduce_plan(gw, outs, refs)
    else:
        (plan, late), moving = collect_plan(gw, outs, refs), lambda u: None
    loaded(0)

    def normalised():
        loaded(5)

        def tile(t, carry):
            r = tile_at(t)
            xhat, _ = normalise(pool[5, r, :].astype(F32))
            pool[3, r, :] = (xhat * gain + shift).astype(BF16)
            return carry
        lax.fori_loop(0, n_t, tile, 0)

    after = {0: [load(gi_h.at[2], 1).start], 1: [load(gi_h.at[3], 2).start], 2: [load(act_h.at[0], 1).start],
             3: [load(act_h.at[1], 2).start, load(cot_h, 0).start], U_OUT: [load(gq_h, 4).start, normalised],
             5: [load(act_h.at[2], 1).start], 6: [load(act_h.at[3], 2).start],
             8: [load(gk_h, 0).start, load(gv_h, 2).start]}

    def unit(u, carry):
        slot = u % 2
        ring = 1 + jnp.where(u < U_OUT, u, u - U_PROJ) % 2
        proj = (u >= U_PROJ) & (u < U_Q)
        lhs = jnp.where(u < U_OUT, 0, jnp.where(proj, ring, 3))
        rhs = jnp.where(u < U_OUT, ring, jnp.where((u == U_OUT) | (u == U_Q), 4, jnp.where(proj | (u == U_Q + 1), 0, 2)))

        @pl.when((u < U_OUT) | proj)
        def _():
            loaded(ring)

        for when, bufs in {U_OUT: (3, 4), U_PROJ: (0,), U_Q: (4,), U_Q + 1: (0,), U_Q + 2: (2,)}.items():
            @pl.when(u == when)
            def _():
                for b in bufs:
                    loaded(b)

        def rows(m, carry):
            c = pl.ds(pl.multiple_of(m * 384, 128), 384)
            g = dot_tn(pool[lhs, :, c], pool[rhs])
            gw[slot, pl.ds(m * 8, 8)] = pack(g.reshape(8, 2, 24, width)).astype(BF16)
            return carry
        lax.fori_loop(0, 2, rows, 0)
        moving(u)
        for when in range(U_END):
            steps = after.get(when, []) + plan.get(when, [])
            if steps:
                @pl.when(u == when)
                def _():
                    for s in steps:
                        s()
        return carry
    lax.fori_loop(0, U_END, unit, 0)
    wload.wait()
    stat[...] = jnp.zeros_like(stat)

    def gin(t):
        return pltpu.make_async_copy(ghid_h.at[tile_at(t), :], ghid.at[t % 2], tsem.at[t % 2])

    def gout(t):
        return pltpu.make_async_copy(ghid.at[t % 2], gtok_h.at[tile_at(t), :], osem.at[t % 2])

    gin(0).start()

    def tile(t, carry):
        r, slot = tile_at(t), t % 2
        g = (dot_nt(pool[4, r, :], w[:, :width]) + dot_nt(pool[0, r, :], w[:, width:2 * width])
             + dot_nt(pool[2, r, :fresh], w[:, 2 * width:]))
        gin(t).wait()

        @pl.when(t > 0)
        def _():
            gout(t - 1).wait()

        @pl.when(t + 1 < n_t)
        def _():
            gin(t + 1).start()
        xhat, rstd = normalise(pool[5, r, :].astype(F32))
        stat[0:1, :] += jnp.sum(g * xhat, axis=0, keepdims=True)
        stat[2:3, :] += jnp.sum(g, axis=0, keepdims=True)
        ghid[slot] += norm_back(g, xhat, rstd, gain)
        gout(t).start()
        moving(U_END + t)
        for when in range(n_t):
            steps = plan.get(U_END + when, [])
            if steps:
                @pl.when(t == when)
                def _():
                    for s in steps:
                        s()
        return carry
    lax.fori_loop(0, n_t, tile, 0)
    stat[...] = stat[...] + stat_two[...]
    late(stat)
    gout(n_t - 1).wait()


def collect_plan(gw, outs, refs):
    parts, stat_ref = outs[0], outs[4]
    sem = refs[0]

    def emit(u):
        def go():
            c = pltpu.make_async_copy(gw.at[u % 2], parts.at[u], sem)
            c.start()
            c.wait()
        return go

    def late(stat):
        stat_ref[...] = stat[...]
    return {u: [emit(u)] for u in range(U_END)}, late


def reduce_plan(gw, outs, refs):
    fc_t, proj_t, out_t, qkv_t, stat_ref = outs
    recv, local, (fcp, stage, came, sems, ssem) = refs[:4], refs[4:9], refs[9:]
    small, width = out_t.shape
    last = qkv_t.shape[1] - 2 * width
    place = ReducePlace()
    enter(place)
    dest = [fcp.at[u] for u in range(N_FF)] + [out_t] + [proj_t.at[pl.ds(u * small, small), :] for u in range(N_FF)] + [
        qkv_t.at[:, pl.ds(0, width)], qkv_t.at[:, pl.ds(width, width)], qkv_t.at[:, pl.ds(2 * width, last)]]
    pieces = []
    for u in range(U_END):
        whole = dest[u].shape[1] == width
        pick = lambda ref, *at: ref.at[at] if whole else ref.at[at + (slice(None),) * (len(ref.shape) - len(at) - 2) + (pl.ds(0, LAST_ROWS),)]
        bufs = [pick(b, u) for b in recv], [pick(b, u % (RING_1 if i < 2 else RING_2)) for i, b in enumerate(local)]
        pieces.append(Piece(place, pick(gw, u % 2), dest[u], *bufs, sems.at[u]))
    todo = [(u + d, -k, u) for u in range(U_END) for k, d in enumerate(DELAYS)]
    todo.sort(key=lambda e: (e[0], e[1] if e[1] else -9, e[2]))
    plan, rest = {}, []
    for when, neg, u in todo:
        step = getattr(pieces[u], "t%d" % -neg)
        if when < U_END + 4:
            if neg == -4 or u == U_END - 1:
                plan.setdefault(when, []).append(step)
        else:
            rest.append(step)
    sums = Sum(place, stage, came, ssem)

    def moving(time):
        for k in (0, 3, 2, 1):
            p = time - DELAYS[k]

            @pl.when((p >= 0) & (p < U_END - 1))
            def _():
                local_p = [b.at[p % (RING_1 if i < 2 else RING_2)] for i, b in enumerate(local)]
                getattr(Piece(place, gw.at[p % 2], None, [b.at[p] for b in recv], local_p, sems.at[p]), "t%d" % k)()

    def late(stat):
        stage[0] = stat[...]
        sums.hop(0).start()
        between = [lambda: sums.step(0), lambda: sums.step(1), lambda: sums.step(2)]
        fc_t[...] = spread_groups([fcp[j] for j in range(N_FF)], width // small, small)
        for step in rest:
            step()
            if between:
                between.pop(0)()
        for step in between:
            step()
        stat_ref[...] = sums.finish()
    return plan, late, moving


def grads(remote, tokens, ghid, gq, gk, gv, w, act, gi, n2, cot, att, gb, gs, stat):
    n, width = tokens.shape
    fresh = w.shape[1] - 2 * width
    small = 24
    ff = act.shape[0] * width
    s, dma = jax.ShapeDtypeStruct, pltpu.SemaphoreType.DMA
    any_, vm = pl.BlockSpec(memory_space=pl.ANY), pl.BlockSpec(memory_space=pltpu.VMEM)
    block = (2 * small, width // 2)
    outs = [s((n, width), F32)]
    scratch = [pltpu.VMEM((6, n, width), BF16), pltpu.VMEM((2, 16, 2) + block, BF16), pltpu.VMEM(w.shape, BF16), pltpu.VMEM((2, TILE, width), F32),
               pltpu.VMEM((8, width), F32), dma((7,)), dma((2,)), dma((2,))]
    params = dict(vmem_limit_bytes=VMEM_BYTES)
    if remote:
        outs += [s((small, ff), F32), s((ff // 32, width), F32), s((small, width), F32), s((small, w.shape[1]), F32)]
        specs = [vm] * 4
        scratch += [pltpu.VMEM((U_END, k) + block, BF16) for k in RECV]
        scratch += [pltpu.VMEM((r, k) + block, d) for r, k, d in ((RING_1, 8, BF16), (RING_1, 8, F32), (RING_2, 4, BF16), (RING_2, 4, F32), (RING_2, 3, BF16))]
        scratch += [pltpu.VMEM((N_FF, small, width), F32), pltpu.VMEM((4, 8, width), F32), pltpu.VMEM((6, 8, width), F32), dma((U_END, 2, 6)), dma((2, 6))]
        params.update(collective_id=2, has_side_effects=True)
    else:
        outs += [s((U_END, 16, 2) + block, BF16)] + [s((8, 128), F32)] * 3
        specs = [any_] * 4
        scratch += [dma(())]
    return pl.pallas_call(
        functools.partial(grads_kernel, remote), in_specs=[any_] * 12 + [vm] * 2, out_specs=[any_] + specs + [vm],
        out_shape=outs + [s((8, width), F32)], scratch_shapes=scratch,
        compiler_params=pltpu.CompilerParams(**params), name="grads",
    )(tokens, ghid, gq, gk, gv, w, act, gi, n2, cot, att, gb, gs, stat)


def unpack_parts(parts, width, fresh):
    p = parts.astype(F32).reshape(U_END, width // 24, 2, 24, width // 2).transpose(0, 1, 3, 2, 4).reshape(U_END, width, width)
    return (jnp.concatenate([p[U_Q], p[U_Q + 1], p[U_Q + 2, :, :fresh]], axis=1), p[U_OUT], jnp.concatenate(list(p[:N_FF]), axis=1),
            p[U_PROJ:U_Q].reshape(-1, width))


N_COPY = 8


def finish_kernel(tok, fc, proj, out, qkv, stat, tok_o, fc_o, proj_o, out_o, qkv_o, gain_o, shift_o, buf, isem, osem):
    n = tok.shape[0] // N_COPY
    rows = [pl.ds(i * n, n) for i in range(N_COPY)]
    loads = [pltpu.make_async_copy(tok.at[r, :], buf.at[r, :], isem.at[i]) for i, r in enumerate(rows)]
    stores = [pltpu.make_async_copy(buf.at[r, :], tok_o.at[r, :], osem.at[i]) for i, r in enumerate(rows)]
    for c in loads:
        c.start()
    fc_o[...], proj_o[...], out_o[...], qkv_o[...] = fc[...], proj[...], out[...], qkv[...]
    width, own = stat.shape[1], gain_o.shape[1]
    mine = pltpu.roll(stat[...], lax.rem(width - own * lax.axis_index(AXES), width), 1)
    gain_o[...] = mine[0:2, :own]
    shift_o[...] = mine[2:4, :own]
    for load, store in zip(loads, stores):
        load.wait()
        store.start()
    for c in stores:
        c.wait()


def finish(tok, fc, proj, out, qkv, stat, own):
    small = jax.ShapeDtypeStruct((2, own), F32)
    outs = [jax.ShapeDtypeStruct(a.shape, F32) for a in (tok, fc, proj, out, qkv)] + [small, small]
    any_, vm = pl.BlockSpec(memory_space=pl.ANY), pl.BlockSpec(memory_space=pltpu.VMEM)
    return pl.pallas_call(
        finish_kernel, in_specs=[any_] + [vm] * 5, out_specs=[any_] + [vm] * 6, out_shape=outs,
        scratch_shapes=[pltpu.VMEM(tok.shape, F32), pltpu.SemaphoreType.DMA((N_COPY,)), pltpu.SemaphoreType.DMA((N_COPY,))],
        compiler_params=pltpu.CompilerParams(vmem_limit_bytes=VMEM_BYTES), name="finish",
    )(tok, fc, proj, out, qkv, stat)


def body(direct, tokens, skip_values, w_qkv, w_out, w_fc, w_proj, norm_gains, norm_shifts, segment_ids, pad_mask, cotangent):
    micro, rows, length, width = tokens.shape
    half, ff = skip_values.shape[3], w_fc.shape[1]
    seqs = micro * rows
    n = seqs * length
    own = norm_gains.shape[1]
    flat = lambda a: a.reshape(n, a.shape[-1])
    seq = lambda a: a.reshape(seqs, length, a.shape[-1])
    tok, skip, cot = flat(tokens), flat(skip_values), flat(cotangent)
    seg, pad = segment_ids.reshape(seqs, 1, length), pad_mask.reshape(seqs, 1, length)
    if direct:
        q, k, v, gs, fcp, _, qkv, out, fc0, proj0 = start(tok, skip, norm_gains, norm_shifts, w_qkv, w_out, w_fc, w_proj)
        weights = (fc0, proj0, fcp, w_proj)
    else:
        qkv, out, *weights = [lax.all_gather(w, AXES, axis=0, tiled=True) for w in (w_qkv, w_out, w_fc, w_proj)]
        rows8 = jnp.concatenate([norm_gains, norm_shifts, jnp.zeros((4, own), BF16)], axis=0)
        gs = lax.all_gather(rows8, AXES, axis=1, tiled=True).astype(F32)
        q, k, v = project(tok, skip, qkv, gs)
    att, lse = attend(seq(q), seq(k), seq(v), seg, pad)
    att = flat(att)
    lout, ghid, gatt, n2, gb, act, gi, stat = mlp(direct, tok, att, cot, out, weights, gs)
    gq, gk, gv, gskip, lout = attend_back(seq(q), seq(k), seq(v), seq(gatt), lse, seg, pad, seq(lout), half)
    gtok, gfc, gproj, gout, gqkv, stat = grads(
        direct, tok, ghid, flat(gq), flat(gk), flat(gv), qkv, act, gi, n2, cot, att, gb, gs, stat)
    if direct:
        gtok, total_fc, total_proj, total_out, total_qkv, gains, shifts = finish(gtok, gfc, gproj, gout, gqkv, stat, own)
    else:
        total_qkv, total_out, total_fc, total_proj = [
            lax.psum_scatter(g, AXES, scatter_dimension=0, tiled=True) for g in unpack_parts(gfc, width, width - half)]
        gains = lax.psum_scatter(stat[0:2], AXES, scatter_dimension=1, tiled=True)
        shifts = lax.psum_scatter(stat[2:4], AXES, scatter_dimension=1, tiled=True)
    shape4 = lambda a: a.reshape(micro, rows, length, a.shape[-1])
    return (shape4(lout), shape4(gtok), shape4(gskip), total_qkv, total_out, total_fc, total_proj, gains, shifts)


def solution(mesh):
    tok, mat, row, ids = P(None, AXES, None, None), P(AXES, None), P(None, AXES), P(None, AXES, None)
    direct = dict(mesh.shape) == {"dp": 2, "fsdp": 16}
    return jax.shard_map(
        functools.partial(body, direct), mesh=mesh,
        in_specs=(tok, tok, mat, mat, mat, mat, row, row, ids, ids, tok),
        out_specs=(tok, tok, tok, mat, mat, mat, mat, row, row), check_vma=False)
```
